32 devices in a mesh: dp: 8 (over y, x, core), tensor: 4 (over z).
Axes of the slice: x: 2, y: 2, z: 4, core: 2. Of those that a mesh axis runs over, the one named last changes fastest.
Arguments:
- clip_rows: bfloat16 [12544, 1024], P(('dp', 'tensor')), may hold values from -6 to 6
- out_grad: bfloat16 [12544, 1024], P(('dp', 'tensor')), may hold values from -6 to 6
- clip_valid: int32 [8], P('dp'), may hold values from 0 to 1, as said below
- gain_rows: bfloat16 [2, 1024], P(None, ('dp', 'tensor')), may hold values from 0.099609375 to 1.8984375
- bias_rows: bfloat16 [4, 1024], P(None, ('dp', 'tensor')), may hold values from -1.796875 to 1.796875
- qkv_weight: bfloat16 [3, 1024, 1024], P(None, 'dp', 'tensor'), may hold values from -0.1875 to 0.1875
- qv_bias: bfloat16 [2, 16, 64], P(None, 'tensor', 'dp'), may hold values from -3 to 3
- proj_weight: bfloat16 [1024, 1024], P('tensor', 'dp'), may hold values from -4 to 4
- fc1_weight: bfloat16 [1024, 4096], P('dp', 'tensor'), may hold values from -0.1875 to 0.1875
- fc1_bias: bfloat16 [4, 1024], P('tensor', 'dp'), may hold values from -1.796875 to 1.796875
- fc2_weight: bfloat16 [4096, 1024], P('tensor', 'dp'), may hold values from -0.125 to 0.125
Outputs:
- layer_out: bfloat16 [12544, 1024], P(('dp', 'tensor'))
- input_grad: float32 [12544, 1024], P(('dp', 'tensor'))
- grad_gains: float32 [2, 1024], P(None, ('dp', 'tensor'))
- grad_biases: float32 [4, 1024], P(None, ('dp', 'tensor'))
- grad_qkv: float32 [3, 1024, 1024], P(None, 'dp', 'tensor')
- grad_qv_bias: float32 [2, 16, 64], P(None, 'tensor', 'dp')
- grad_proj: float32 [1024, 1024], P('tensor', 'dp')
- grad_fc1: float32 [1024, 4096], P('dp', 'tensor')
- grad_fc1_bias: float32 [4, 1024], P('tensor', 'dp')
- grad_fc2: float32 [4096, 1024], P('tensor', 'dp')
- grad_fc2_bias: float32 [1024], P(('dp', 'tensor'))
The draws below stay inside these ranges and needn't reach their ends.
Inputs may be any that keep to these rules, and one draw needn't show every extreme that they name: `clip_valid`: exactly 2 of the 8 slots hold a clip; which ones is drawn from the seed.
All inputs are finite; a program needn't handle non-finite values.
Results may differ from the reference program's by a relative error of at most 0.012.
Values may be sent and summed in bfloat16 or wider, within the bound.
No kernel may reach another device: no remote copies, remote signals or barrier semaphores. Data moves between devices by JAX's collectives and lax.ppermute only.
A program may use at most 256 MiB of HBM per device.

```python
import math
import jax
import jax.numpy as jnp
from jax import lax

D = 1024
H = 16
HD = 64
FF = 4096
SEQ = 1568
CLIPS = 8
VALID_CLIPS = 2
TOKENS = 12544
N_TENSOR = 4


def draw_clip_valid(key, part):
    order = jax.random.permutation(jax.random.fold_in(key, 17), CLIPS)
    return (order < VALID_CLIPS).astype(jnp.int32)


def levels(stream_key, dims, pieces, low, top_value):
    def one(position, parts):
        heights = jax.random.uniform(jax.random.fold_in(jax.random.fold_in(stream_key, 6), position), (parts,), jnp.float32, low / len(pieces), top_value / len(pieces))
        return jnp.repeat(jnp.exp(heights), dims[position] // parts).reshape((-1,) + (1,) * (len(dims) - position - 1))

    level = one(*pieces[0])
    for cut in pieces[1:]:
        level = level * one(*cut)
    return level


def gaussian(rng, shape, width, limit, cuts=(), dtype=jnp.bfloat16):
    loudness = levels(rng, shape, cuts, -0.22, 0.18) if cuts else 1.0
    array = jax.random.normal(rng, shape, jnp.float32) * width * loudness
    return jnp.minimum(jnp.maximum(array, -limit), limit).astype(dtype)


def setup_inputs(seed: int = 0) -> dict:
    splits = jax.random.split(jax.random.key(seed), 12)
    return {
        "clip_rows": gaussian(splits[0], (TOKENS, D), 1.0, 6.0, ((0, 32),)),
        "out_grad": gaussian(splits[1], (TOKENS, D), 1.0, 6.0, ((0, 32),)),
        "clip_valid": draw_clip_valid(jax.random.fold_in(splits[11], 71), 0),
        "gain_rows": jnp.clip(1.0 + 0.18 * jax.random.normal(splits[3], (2, D), jnp.float32), 0.099609375, 1.8984375).astype(jnp.bfloat16),
        "bias_rows": gaussian(splits[4], (4, D), 0.3, 1.796875, ((1, 32),)),
        "qkv_weight": gaussian(splits[5], (3, D, D), D ** -0.5, 0.1875, ((1, 8), (2, 4))),
        "qv_bias": gaussian(splits[6], (2, H, HD), 0.5, 3.0, ((1, 4), (2, 8))),
        "proj_weight": gaussian(splits[7], (D, D), (max(1, D * 4 // SEQ)) ** -0.5, 4.0, ((0, 4), (1, 8))),
        "fc1_weight": gaussian(splits[8], (D, FF), D ** -0.5, 0.1875, ((0, 8), (1, 4))),
        "fc1_bias": gaussian(splits[9], (N_TENSOR, FF // N_TENSOR), 0.3, 1.796875, ((0, 4), (1, 8))),
        "fc2_weight": gaussian(splits[10], (FF, D), (FF // 2) ** -0.5, 0.125, ((0, 4), (1, 8))),
    }


@jax.custom_vjp
def low(v):
    return lax.optimization_barrier(v.astype(jnp.bfloat16)).astype(jnp.float32)

@jax.custom_vjp
def low_back(v):
    return v

def low_keep(v):
    return (low(v), None)

def low_pass(kept, grad):
    return (grad,)

def back_keep(v):
    return (v, None)

def back_low(kept, grad):
    return (low(grad),)
low.defvjp(low_keep, low_pass)
low_back.defvjp(back_keep, back_low)
norm_eps = 1e-06
root_half = 0.7071067811865476
highest = lax.Precision.HIGHEST

def both_round(values):
    return low(low_back(values))

def normalize(values, gain_row, shift_row):
    centre = lax.optimization_barrier(jnp.mean(values, axis=1, keepdims=True))
    offsets = values - centre
    inverse = lax.rsqrt(lax.optimization_barrier(jnp.mean(offsets * offsets, axis=1, keepdims=True)) + norm_eps)
    return offsets * inverse * gain_row + shift_row

def gelu_value(inputs):
    return 0.5 * inputs * (1.0 + lax.erf(inputs * root_half))

def layer(clip_in, clip_weight, gain_rows, bias_rows, qkv_weight, qv_bias, proj_weight, fc1_weight, fc1_bias, fc2_weight):
    normed_one = low(normalize(clip_in, gain_rows[0], bias_rows[0]))
    projected = jnp.einsum('sd,jde->jse', normed_one, qkv_weight, precision=highest)
    bias_cols = qv_bias.reshape(2, D)
    queries = both_round(projected[0] + bias_cols[0]).reshape(SEQ, H, HD)
    keys_all = both_round(projected[1]).reshape(SEQ, H, HD)
    values_all = both_round(projected[2] + bias_cols[1]).reshape(SEQ, H, HD)
    scores = low_back(jnp.einsum('qhd,khd->hqk', queries, keys_all, precision=highest) * (1.0 / math.sqrt(HD)))
    attn_probs = low(jax.nn.softmax(scores, axis=2))
    attended = both_round(jnp.einsum('hqk,khd->qhd', attn_probs, values_all, precision=highest).reshape(SEQ, D))
    residual_one = clip_in + low_back(jnp.dot(attended, proj_weight, precision=highest) + bias_rows[2])
    normed_two = low(normalize(residual_one, gain_rows[1], bias_rows[1]))
    pre_act = low_back(jnp.dot(normed_two, fc1_weight, precision=highest) + fc1_bias.reshape(FF))
    hidden = low(gelu_value(pre_act))
    branch = low_back(jnp.dot(hidden, fc2_weight, precision=highest) + bias_rows[3])
    return clip_weight * (residual_one + branch)

def reference(clip_rows, out_grad, clip_valid, gain_rows, bias_rows, qkv_weight, qv_bias, proj_weight, fc1_weight, fc1_bias, fc2_weight):
    params = (gain_rows.astype(jnp.float32), bias_rows.astype(jnp.float32), qkv_weight.astype(jnp.float32), qv_bias.astype(jnp.float32), proj_weight.astype(jnp.float32), fc1_weight.astype(jnp.float32), fc1_bias.astype(jnp.float32), fc2_weight.astype(jnp.float32))
    inputs = clip_rows.astype(jnp.float32).reshape(CLIPS, SEQ, D)
    grads_in = out_grad.astype(jnp.float32).reshape(CLIPS, SEQ, D)
    weights_clip = clip_valid.astype(jnp.float32)

    def one_clip(totals, items):
        clip_in, clip_grad, clip_weight = items

        def apply_layer(values, *layer_params):
            return layer(values, clip_weight, *layer_params)
        result, pullback = jax.vjp(apply_layer, clip_in, *params)
        pulled = pullback(clip_grad)
        totals = jax.tree.map(lambda left, right: left + right, totals, tuple(pulled[1:]))
        return (totals, (result, pulled[0]))
    start_totals = jax.tree.map(jnp.zeros_like, params)
    totals, outcome = lax.scan(one_clip, start_totals, (inputs, grads_in, weights_clip))
    results, input_grads = outcome
    return (results.reshape(TOKENS, D).astype(jnp.bfloat16), input_grads.reshape(TOKENS, D), totals[0], totals[1], totals[2], totals[3], totals[4], totals[5], totals[6], totals[7], totals[1][3])
```

```python
import math

import jax
import jax.numpy as jnp
from jax import lax
from jax.experimental import pallas as pl
from jax.experimental.pallas import tpu as pltpu
from jax.sharding import PartitionSpec as P

HD = 64


norm_eps = 1e-06
root_half = 0.7071067811865476
inv_root_tau = 0.3989422804014327


def normalize(values, gain_row, shift_row):
    centre = jnp.mean(values, axis=1, keepdims=True)
    offsets = values - centre
    inverse = lax.rsqrt(jnp.mean(offsets * offsets, axis=1, keepdims=True) + norm_eps)
    scaled = offsets * inverse
    return (scaled * gain_row + shift_row, scaled, inverse)


def normalize_back(upstream, scaled, inverse, gain_row):
    grad_hat = upstream * gain_row
    return (
        grad_hat
        - jnp.mean(grad_hat, axis=1, keepdims=True)
        - scaled * jnp.mean(grad_hat * scaled, axis=1, keepdims=True)
    ) * inverse


def gelu_value(inputs):
    return 0.5 * inputs * (1.0 + lax.erf(inputs * root_half))


def gelu_slope(inputs):
    return (
        0.5 * (1.0 + lax.erf(inputs * root_half))
        + inputs * jnp.exp(-0.5 * inputs * inputs) * inv_root_tau
    )


def fetch(qkv_weight, proj_weight, fc1_weight, fc2_weight, qv_bias, fc1_bias, gain_rows, bias_rows):
    matrices = (
        lax.all_gather(qkv_weight, "dp", axis=1, tiled=True),
        lax.all_gather(proj_weight, "dp", axis=1, tiled=True),
        lax.all_gather(fc1_weight, "dp", axis=0, tiled=True),
        lax.all_gather(fc2_weight, "dp", axis=1, tiled=True),
        lax.all_gather(qv_bias, "dp", axis=2, tiled=True),
        lax.all_gather(fc1_bias, "dp", axis=1, tiled=True),
    )
    vectors = (
        lax.all_gather(gain_rows, ("dp", "tensor"), axis=1, tiled=True),
        lax.all_gather(bias_rows, ("dp", "tensor"), axis=1, tiled=True),
    )
    return (matrices, (vectors[0].astype(jnp.float32), vectors[1].astype(jnp.float32)))


def spread_rows(local_rows):
    return lax.all_gather(local_rows, "tensor", axis=0, tiled=True)


def reduce_rows(term_fn, row_count):
    return lax.psum_scatter(
        term_fn(jnp.int32(0), lax.axis_size("tensor") * row_count),
        "tensor",
        scatter_dimension=0,
        tiled=True,
    )


def spread_grads(local_rows):
    return lax.all_gather(local_rows, "tensor", axis=0, tiled=True)


def reduce_grads(term_fn, row_count):
    return lax.psum_scatter(
        term_fn(jnp.int32(0), lax.axis_size("tensor") * row_count),
        "tensor",
        scatter_dimension=0,
        tiled=True,
    )


def forward(clip_rows, matrices, vectors):
    w_qkv, w_proj, w_fc1, w_fc2, b_qv, b_fc1 = matrices
    gain_rows, bias_rows = vectors
    row_count = clip_rows.shape[0]
    head_cols = w_qkv.shape[2]
    heads_here = head_cols // HD
    score_scale = 1.0 / math.sqrt(HD)
    inputs = clip_rows.astype(jnp.float32)
    normed_one, scaled_one, inverse_one = normalize(inputs, gain_rows[0], bias_rows[0])
    whole_one = spread_rows(normed_one.astype(jnp.bfloat16))
    seq_len = whole_one.shape[0]
    projected = jnp.einsum("sd,jde->jse", whole_one, w_qkv, preferred_element_type=jnp.float32)
    bias_cols = b_qv.reshape(2, head_cols).astype(jnp.float32)
    queries = (projected[0] + bias_cols[0]).astype(jnp.bfloat16).reshape(seq_len, heads_here, HD)
    keys_all = projected[1].astype(jnp.bfloat16).reshape(seq_len, heads_here, HD)
    values_all = (projected[2] + bias_cols[1]).astype(jnp.bfloat16).reshape(seq_len, heads_here, HD)
    scores = (
        jnp.einsum("qhd,khd->hqk", queries, keys_all, preferred_element_type=jnp.float32)
        * score_scale
    )
    top_score = jnp.max(scores, axis=2, keepdims=True)
    weights_exp = jnp.exp(scores - top_score)
    totals = jnp.sum(weights_exp, axis=2, keepdims=True)
    attn_probs = (weights_exp / totals).astype(jnp.bfloat16)
    log_total = top_score + jnp.log(totals)
    attended = (
        jnp.einsum("hqk,khd->qhd", attn_probs, values_all, preferred_element_type=jnp.float32)
        .reshape(seq_len, head_cols)
        .astype(jnp.bfloat16)
    )

    def proj_term(offset, length):
        return jnp.dot(attended, w_proj, preferred_element_type=jnp.float32)

    residual_one = inputs + (reduce_rows(proj_term, row_count) + bias_rows[2])
    normed_two, scaled_two, inverse_two = normalize(residual_one, gain_rows[1], bias_rows[1])
    whole_two = spread_rows(normed_two.astype(jnp.bfloat16))
    pre_act = jnp.dot(whole_two, w_fc1, preferred_element_type=jnp.float32) + b_fc1.reshape(
        -1
    ).astype(jnp.float32)
    hidden = gelu_value(pre_act).astype(jnp.bfloat16)

    def fc2_term(offset, length):
        return jnp.dot(hidden, w_fc2, preferred_element_type=jnp.float32)

    layer_out = residual_one + (reduce_rows(fc2_term, row_count) + bias_rows[3])
    stored = (
        scaled_one,
        inverse_one,
        whole_one,
        queries,
        keys_all,
        values_all,
        log_total,
        attended,
        scaled_two,
        inverse_two,
        whole_two,
        pre_act,
        hidden,
    )
    return (layer_out, stored)


def backward(upstream, matrices, vectors, stored):
    w_qkv, w_proj, w_fc1, w_fc2, b_qv, b_fc1 = matrices
    gain_rows, bias_rows = vectors
    (
        scaled_one,
        inverse_one,
        whole_one,
        queries,
        keys_all,
        values_all,
        log_total,
        attended,
        scaled_two,
        inverse_two,
        whole_two,
        pre_act,
        hidden,
    ) = stored
    row_count = upstream.shape[0]
    seq_len = queries.shape[0]
    heads_here = queries.shape[1]
    head_cols = heads_here * HD
    score_scale = 1.0 / math.sqrt(HD)
    grad_mlp = upstream.astype(jnp.bfloat16)
    grad_fc2_bias = jnp.sum(grad_mlp.astype(jnp.float32), axis=0)
    whole_mlp = spread_grads(grad_mlp)
    grad_fc2 = jnp.einsum("sf,sd->fd", hidden, whole_mlp, preferred_element_type=jnp.float32)
    grad_hidden = jnp.einsum("sd,fd->sf", whole_mlp, w_fc2, preferred_element_type=jnp.float32)
    grad_pre = (grad_hidden * gelu_slope(pre_act)).astype(jnp.bfloat16)
    grad_fc1_bias = jnp.sum(grad_pre.astype(jnp.float32), axis=0)
    grad_fc1 = jnp.einsum("sd,sf->df", whole_two, grad_pre, preferred_element_type=jnp.float32)

    def fc1_back(offset, length):
        return jnp.einsum("sf,df->sd", grad_pre, w_fc1, preferred_element_type=jnp.float32)

    grad_normed_two = reduce_grads(fc1_back, row_count)
    grad_residual = upstream + normalize_back(
        grad_normed_two, scaled_two, inverse_two, gain_rows[1]
    )
    grad_branch = grad_residual.astype(jnp.bfloat16)
    grad_proj_bias = jnp.sum(grad_branch.astype(jnp.float32), axis=0)
    whole_branch = spread_grads(grad_branch)
    grad_proj = jnp.einsum("se,sd->ed", attended, whole_branch, preferred_element_type=jnp.float32)
    grad_att = (
        jnp.einsum("sd,ed->se", whole_branch, w_proj, preferred_element_type=jnp.float32)
        .astype(jnp.bfloat16)
        .reshape(seq_len, heads_here, HD)
    )
    scores = (
        jnp.einsum("qhd,khd->hqk", queries, keys_all, preferred_element_type=jnp.float32)
        * score_scale
    )
    attn_probs = jnp.exp(scores - log_total)
    grad_probs = jnp.einsum(
        "qhd,khd->hqk", grad_att, values_all, preferred_element_type=jnp.float32
    )
    row_dot = jnp.sum(attn_probs * grad_probs, axis=2, keepdims=True)
    grad_scores = (attn_probs * (grad_probs - row_dot)).astype(jnp.bfloat16)
    grad_query = (
        jnp.einsum("hqk,khd->qhd", grad_scores, keys_all, preferred_element_type=jnp.float32)
        * score_scale
    ).astype(jnp.bfloat16)
    grad_key = (
        jnp.einsum("hqk,qhd->khd", grad_scores, queries, preferred_element_type=jnp.float32)
        * score_scale
    ).astype(jnp.bfloat16)
    grad_value = jnp.einsum(
        "hqk,qhd->khd",
        attn_probs.astype(jnp.bfloat16),
        grad_att,
        preferred_element_type=jnp.float32,
    ).astype(jnp.bfloat16)
    grad_qkv = jnp.stack([grad_query, grad_key, grad_value]).reshape(3, seq_len, head_cols)
    grad_qv = jnp.stack(
        [
            jnp.sum(grad_query.astype(jnp.float32), axis=0),
            jnp.sum(grad_value.astype(jnp.float32), axis=0),
        ]
    )
    grad_qkv_weight = jnp.einsum(
        "sd,jse->jde", whole_one, grad_qkv, preferred_element_type=jnp.float32
    )

    def qkv_back(offset, length):
        return jnp.einsum("jse,jde->sd", grad_qkv, w_qkv, preferred_element_type=jnp.float32)

    grad_normed_one = reduce_grads(qkv_back, row_count)
    grad_input = grad_residual + normalize_back(
        grad_normed_one, scaled_one, inverse_one, gain_rows[0]
    )
    grad_gain = jnp.stack(
        [
            jnp.sum(grad_normed_one * scaled_one, axis=0),
            jnp.sum(grad_normed_two * scaled_two, axis=0),
        ]
    )
    grad_bias = jnp.stack(
        [
            jnp.sum(grad_normed_one, axis=0),
            jnp.sum(grad_normed_two, axis=0),
            grad_proj_bias,
            grad_fc2_bias,
        ]
    )
    weight_part = (
        lax.psum_scatter(grad_qkv_weight, "dp", scatter_dimension=1, tiled=True),
        lax.psum_scatter(grad_proj, "dp", scatter_dimension=1, tiled=True),
        lax.psum_scatter(grad_fc1, "dp", scatter_dimension=0, tiled=True),
        lax.psum_scatter(grad_fc2, "dp", scatter_dimension=1, tiled=True),
        lax.psum_scatter(grad_qv, "dp", scatter_dimension=2, tiled=True),
        lax.psum_scatter(grad_fc1_bias.reshape(1, -1), "dp", scatter_dimension=1, tiled=True),
    )
    vector_part = (
        lax.psum_scatter(grad_gain, ("dp", "tensor"), scatter_dimension=1, tiled=True),
        lax.psum_scatter(grad_bias, ("dp", "tensor"), scatter_dimension=1, tiled=True),
    )
    return (grad_input, weight_part, vector_part)


def on_device(
    clip_rows,
    out_grad,
    clip_valid,
    gain_rows,
    bias_rows,
    qkv_weight,
    qv_bias,
    proj_weight,
    fc1_weight,
    fc1_bias,
    fc2_weight,
):
    clip_weight = clip_valid[0].astype(jnp.float32)
    upstream = out_grad.astype(jnp.float32) * clip_weight
    matrices, vectors = fetch(
        qkv_weight, proj_weight, fc1_weight, fc2_weight, qv_bias, fc1_bias, gain_rows, bias_rows
    )
    layer_out, stored = forward(clip_rows, matrices, vectors)
    matrices, vectors = fetch(
        qkv_weight, proj_weight, fc1_weight, fc2_weight, qv_bias, fc1_bias, gain_rows, bias_rows
    )
    unused_out, stored = forward(clip_rows, matrices, vectors)
    grad_input, weight_part, vector_part = backward(upstream, matrices, vectors, stored)
    return (
        (layer_out * clip_weight).astype(jnp.bfloat16),
        grad_input,
        vector_part[0],
        vector_part[1],
        weight_part[0],
        weight_part[4],
        weight_part[1],
        weight_part[2],
        weight_part[5],
        weight_part[3],
        vector_part[1][3],
    )


VALID_CLIPS = 2
AXES = ("dp", "tensor")
Z_LOW, Z_HIGH, CORE, X, Y = 1, 2, 4, 8, 16
CHIP_MASKS = (0, X, Y, X | Y)
BF16, F32 = jnp.bfloat16, jnp.float32


def swap(value, mask):
    return lax.ppermute(value, AXES, [(i, i ^ mask) for i in range(32)])


def dot(left, right, dims):
    return lax.dot_general(left, right, (dims, ((), ())), preferred_element_type=F32)


NN = ((1,), (0,))
NT = ((1,), (1,))
TN = ((0,), (0,))


def call(body, outs, scalar, *args):
    return pl.pallas_call(
        body,
        out_shape=[jax.ShapeDtypeStruct(s, t) for s, t in outs],
        in_specs=[pl.BlockSpec(memory_space=pltpu.SMEM)]
        + [pl.BlockSpec(memory_space=pltpu.VMEM)] * len(args),
        out_specs=[pl.BlockSpec(memory_space=pltpu.VMEM)] * len(outs),
    )(scalar, *args)


def qkv_kernel(chip, rows, w0, w1, w2, w3, bias, out):
    weights = (w0, w1, w2, w3)
    for j in range(3):
        cols = slice(256 * j, 256 * j + 256)
        total = bias[j : j + 1, :]
        for m in range(4):
            total = total + dot(rows[:, 256 * m : 256 * m + 256], weights[m][:, cols], NN)
        total = total.astype(BF16)
        for h in range(4):
            out[h ^ chip[0], :, 64 * j : 64 * j + 64] = total[:, 64 * h : 64 * h + 64]


def attention_kernel(chip, qkv, out, lse):
    keys = qkv[:, 64:128]
    values = qkv[:, 128:192]
    step = 224

    def body(i, carry):
        start = pl.multiple_of(i * step, 32)
        queries = qkv[pl.ds(start, step), 0:64] * 0.125
        scores = dot(queries, keys, NT)
        top = jnp.max(scores, axis=1, keepdims=True)
        weights = jnp.exp(scores - top)
        total = jnp.sum(weights, axis=1, keepdims=True)
        mixed = dot(weights.astype(BF16), values, NN)
        out[pl.ds(start, step), :] = (mixed / total).astype(BF16)
        spread = jnp.broadcast_to(top + jnp.log(total), (step, 128))
        lse[i, :, :] = jnp.transpose(spread)[0:8, :]
        return carry

    lax.fori_loop(0, qkv.shape[0] // step, body, 0)


def attention_back_kernel(chip, qkv, grads, lse, out, grad_k, grad_v):
    keys = qkv[:, 64:128]
    values = qkv[:, 128:192]
    keys_t = jnp.transpose(keys)
    step = 224
    grad_k[...] = jnp.zeros_like(grad_k)
    grad_v[...] = jnp.zeros_like(grad_v)

    def body(i, carry):
        start = pl.multiple_of(i * step, 32)
        queries = qkv[pl.ds(start, step), 0:64] * 0.125
        grad = grads[pl.ds(start, step), :]
        probs = jnp.exp(dot(keys, queries, NT) - lse[i, 0:1, :])
        grad_probs = dot(values, grad, NT)
        row_dot = jnp.sum(probs * grad_probs, axis=0, keepdims=True)
        grad_scores = (probs * (grad_probs - row_dot)).astype(BF16)
        grad_v[...] += dot(probs.astype(BF16), grad, NN)
        grad_k[...] += dot(grad_scores, queries, NN)
        grad_q = jnp.transpose(dot(keys_t, grad_scores, NN)) * 0.125
        out[pl.ds(start, step), 0:64] = grad_q.astype(BF16)
        return carry

    lax.fori_loop(0, qkv.shape[0] // step, body, 0)
    out[:, 64:128] = grad_k[...].astype(BF16)
    out[:, 128:192] = grad_v[...].astype(BF16)


def proj_kernel(chip, mixed, w0, w1, w2, w3, joined, keep, send):
    weights = (w0, w1, w2, w3)
    half = keep.shape[0]
    for h in range(4):
        joined[:, 64 * h : 64 * h + 64] = mixed[h ^ chip[0], :, :]
    rows = joined[...]
    for m in range(4):
        cols = slice(256 * m, 256 * m + 256)
        total = dot(rows, weights[m][...], NT)
        keep[:, cols] = total[:half]
        send[:, cols] = total[half:].astype(BF16)


def grad_att_kernel(chip, grads, w0, w1, w2, w3, out):
    weights = (w0, w1, w2, w3)
    total = dot(grads[:, 0:256], w0[...], NN)
    for m in range(1, 4):
        total = total + dot(grads[:, 256 * m : 256 * m + 256], weights[m][...], NN)
    total = total.astype(BF16)
    for h in range(4):
        out[h ^ chip[0], :, :] = total[:, 64 * h : 64 * h + 64]


def qkv_back_kernel(chip, grads, w0, w1, w2, w3, joined, keep, send, sums):
    weights = (w0, w1, w2, w3)
    half = keep.shape[0]
    for h in range(4):
        for j in range(3):
            joined[:, 256 * j + 64 * h : 256 * j + 64 * h + 64] = grads[
                h ^ chip[0], :, 64 * j : 64 * j + 64
            ]
    rows = joined[...]
    for m in range(4):
        cols = slice(256 * m, 256 * m + 256)
        total = dot(rows, weights[m][...], NT)
        keep[:, cols] = total[:half]
        send[:, cols] = total[half:].astype(BF16)
    sums[...] = jnp.sum(rows.astype(F32), axis=0, keepdims=True)


def back_rows(total, upstream, scaled, inverse, gain):
    return upstream + normalize_back(total, scaled, inverse, gain)


def sum_grad(parts, x_first):
    first, second, near, far = (X, Y, 1, 2) if x_first else (Y, X, 2, 1)
    got = swap(jnp.stack([parts[near], parts[3]]).astype(BF16), first).astype(F32)
    whole = parts[0] + got[0]
    other = parts[far] + got[1]
    return whole + swap(other.astype(BF16), second).astype(F32)


def settle_grad(part, core):
    pairs = [(i, i ^ Z_HIGH) for i in range(32) if i & CORE]
    moved = lax.ppermute(part.astype(BF16), AXES, pairs).astype(F32)
    part = jnp.where(core == 0, part, moved)
    low, high = part[:128], part[128:]
    send = jnp.where(core == 0, high, low)
    keep = jnp.where(core == 0, low, high)
    return keep + swap(send.astype(BF16), CORE).astype(F32)


def on_device_spread(
    clip_rows,
    out_grad,
    clip_valid,
    gain_rows,
    bias_rows,
    qkv_weight,
    qv_bias,
    proj_weight,
    fc1_weight,
    fc1_bias,
    fc2_weight,
):
    d, t = lax.axis_index("dp"), lax.axis_index("tensor")
    z_high = t >> 1
    core = d & 1
    chip = d >> 1
    x_bit, y_bit = chip & 1, chip >> 1
    chip_ref = chip.reshape(1).astype(jnp.int32)
    quarter = jnp.where(core == 0, t, t ^ 2)
    share = clip_rows.shape[0] // 8

    def turn(value, axis):
        size = value.shape
        value = value.reshape(*size[:axis], 2, 2, size[axis] // 4, *size[axis + 1 :])
        value = jnp.where(x_bit == 1, jnp.flip(value, axis + 1), value)
        value = jnp.where(y_bit == 1, jnp.flip(value, axis), value)
        return value.reshape(size)

    def home(shard):
        far = swap(shard, Z_HIGH)
        keep = jnp.where(core == 0, shard, far)
        got = swap(jnp.where(core == 0, far, shard), CORE)
        return jnp.concatenate(
            [jnp.where(core == 0, keep, got), jnp.where(core == 0, got, keep)], axis=0
        )

    def around(block, by_y):
        w1, w2 = swap(block, X), swap(block, Y)
        w3 = swap(w1, Y) if by_y else swap(w2, X)
        return block, w1, w2, w3

    flag = jnp.broadcast_to(clip_valid.astype(BF16).reshape(1, 1, 1), (8, 1, clip_rows.shape[1]))
    sent = jnp.concatenate([clip_rows.reshape(8, share, -1), flag], axis=1)
    got = lax.all_to_all(sent, "dp", 0, 0)
    valid = got[:, share, 0] > 0.5
    numbers = jnp.arange(8)
    first = jnp.min(jnp.where(valid, numbers, 8))
    second = jnp.max(jnp.where(valid, numbers, -1))
    mine = jnp.where(z_high == 0, first, second)
    other = jnp.where(z_high == 0, second, first)

    def settle(blocks):
        here = lax.dynamic_index_in_dim(blocks, mine, 0, keepdims=False)[:share]
        there = lax.dynamic_index_in_dim(blocks, other, 0, keepdims=False)[:share]
        pair = jnp.concatenate([here, swap(there, Z_HIGH)])
        pair = turn(pair, 1)
        return jnp.concatenate([pair, swap(pair, Z_LOW)])

    rows = settle(got)
    small = jnp.concatenate(
        [v.reshape(-1) for v in (gain_rows, bias_rows, qv_bias, fc1_bias)]
    )
    small = lax.all_gather(small, AXES, axis=0)
    vectors = turn(small[:, :192].astype(F32), 0).reshape(32, 6, 32)
    vectors = jnp.transpose(vectors, (1, 0, 2)).reshape(6, -1)
    gains, biases = vectors[:2], vectors[2:]
    mine_small = lax.dynamic_index_in_dim(small.reshape(8, 4, -1), quarter, 1, keepdims=False)
    mine_small = mine_small.astype(F32)
    qv = jnp.transpose(mine_small[:, 192:256].reshape(8, 2, 4, 8), (1, 2, 0, 3)).reshape(2, 256)
    b_fc1 = mine_small[:, 256:].reshape(-1)
    qkv_bias = jnp.stack([qv[0], jnp.zeros_like(qv[0]), qv[1]])

    w_qkv = around(home(jnp.transpose(qkv_weight, (1, 0, 2)).reshape(128, -1)), True)
    w_proj = around(home(jnp.transpose(proj_weight)), False)
    w_fc1 = around(home(fc1_weight), False)
    w_fc2 = around(home(jnp.transpose(fc2_weight)), True)

    own = rows.shape[0] // 2
    inputs = rows.astype(F32)
    normed_one, scaled_one, inverse_one = normalize(inputs, gains[0:1], biases[0:1])
    normed_one = normed_one.astype(BF16)
    whole_one = jnp.concatenate([normed_one, swap(normed_one, CORE)])
    tokens = whole_one.shape[0]
    (qkv,) = call(qkv_kernel, [((4, tokens, 192), BF16)], chip_ref, whole_one, *w_qkv, qkv_bias)

    def trade(blocks):
        return jnp.stack([blocks[0]] + [swap(blocks[m], CHIP_MASKS[m]) for m in range(1, 4)])

    qkv = trade(qkv).reshape(4 * tokens, 192)
    steps = qkv.shape[0] // 224
    mixed, lse = call(
        attention_kernel,
        [((4 * tokens, 64), BF16), ((steps, 8, 224), F32)],
        chip_ref,
        qkv,
    )
    mixed = trade(mixed.reshape(4, tokens, 64))
    half = tokens // 2
    attended, keep, send = call(
        proj_kernel,
        [((tokens, 256), BF16), ((half, 1024), F32), ((half, 1024), BF16)],
        chip_ref,
        mixed,
        *w_proj,
    )

    def all_z(keep, send):
        part = keep + swap(send, CORE).astype(F32)
        turned = jnp.concatenate([part[own:], part[:own]]).astype(BF16)
        return part + swap(turned, Z_LOW).astype(F32)

    def one_z(keep, send):
        part = keep + swap(send, CORE).astype(F32)
        return part[:own] + swap(part[own:].astype(BF16), Z_LOW).astype(F32)

    residual_one = inputs + (all_z(keep, send) + biases[2:3])
    normed_two, scaled_two, inverse_two = normalize(residual_one, gains[1:2], biases[1:2])
    normed_two = normed_two.astype(BF16)
    whole_two = jnp.concatenate([normed_two, swap(normed_two, CORE)])

    grad_rows = settle(lax.all_to_all(out_grad.reshape(8, share, -1), "dp", 0, 0))
    upstream = grad_rows.astype(F32)
    whole_mlp = jnp.concatenate([grad_rows, swap(grad_rows, CORE)])

    m_fc1 = jnp.concatenate(w_fc1)
    m_fc2 = jnp.concatenate(w_fc2)
    pre_act = dot(whole_two, m_fc1, NN) + b_fc1
    hidden = gelu_value(pre_act).astype(BF16)
    grad_hidden = dot(whole_mlp, m_fc2, NN)
    grad_pre = (grad_hidden * gelu_slope(pre_act)).astype(BF16)
    grad_fc1_bias = jnp.sum(grad_pre.astype(F32), axis=0)
    back = dot(grad_pre, m_fc1, NT)
    grad_normed_two = all_z(back[:half], back[half:].astype(BF16))
    grad_residual = back_rows(grad_normed_two, upstream, scaled_two, inverse_two, gains[1:2])
    grad_branch = grad_residual.astype(BF16)
    whole_branch = jnp.concatenate([grad_branch, swap(grad_branch, CORE)])

    (grad_att,) = call(
        grad_att_kernel, [((4, tokens, 64), BF16)], chip_ref, whole_branch, *w_proj
    )
    grad_att = trade(grad_att).reshape(4 * tokens, 64)
    (grad_qkv,) = pl.pallas_call(
        attention_back_kernel,
        out_shape=[jax.ShapeDtypeStruct(qkv.shape, BF16)],
        in_specs=[pl.BlockSpec(memory_space=pltpu.SMEM)]
        + [pl.BlockSpec(memory_space=pltpu.VMEM)] * 3,
        out_specs=[pl.BlockSpec(memory_space=pltpu.VMEM)],
        scratch_shapes=[pltpu.VMEM((4 * tokens, 64), F32)] * 2,
    )(chip_ref, qkv, grad_att, lse)
    grad_qkv = trade(grad_qkv.reshape(4, tokens, 192))
    joined, keep, send, qkv_sums = call(
        qkv_back_kernel,
        [((tokens, 768), BF16), ((half, 1024), F32), ((half, 1024), BF16), ((1, 768), F32)],
        chip_ref,
        grad_qkv,
        *w_qkv,
    )
    grad_normed_one = one_z(keep, send)
    grad_input = back_rows(
        grad_normed_one, grad_residual[:own], scaled_one[:own], inverse_one[:own], gains[0:1]
    )

    def give_back(value):
        value = turn(value.astype(BF16), 1)
        away = swap(value[share:], Z_HIGH)
        goal = numbers.reshape(8, 1, 1)
        blank = jnp.zeros((), BF16)
        sent = jnp.where(
            goal == mine, value[:share], jnp.where(goal == other, away, blank)
        )
        return lax.all_to_all(sent, "dp", 0, 0).reshape(clip_rows.shape)

    grad_input = give_back(grad_input).astype(F32)
    out = dot(hidden, m_fc2, NT)
    out = one_z(out[:half], out[half:].astype(BF16))
    layer_out = give_back(residual_one[:own] + (out + biases[3:4]))

    def blocks(value):
        return value.reshape(4, 256, -1)

    grad_fc2 = settle_grad(sum_grad(blocks(dot(whole_mlp, hidden, TN)), True), core)
    grad_fc1 = settle_grad(sum_grad(blocks(dot(whole_two, grad_pre, TN)), False), core)
    grad_proj = settle_grad(sum_grad(blocks(dot(whole_branch, attended, TN)), True), core)
    grad_w = settle_grad(sum_grad(blocks(dot(whole_one, joined, TN)), False), core)

    sums = jnp.stack(
        [
            jnp.sum(grad_normed_one * scaled_one[:own], axis=0),
            jnp.sum(grad_normed_two[:own] * scaled_two[:own], axis=0),
            jnp.sum(grad_normed_one, axis=0),
            jnp.sum(grad_normed_two[:own], axis=0),
            jnp.sum(grad_branch[:own].astype(F32), axis=0),
            jnp.sum(upstream[:own], axis=0),
        ]
    )
    sums = jnp.transpose(sums.reshape(6, 32, 32), (1, 0, 2)).reshape(32, 192)
    sums = turn(sums, 0)
    here = jnp.arange(4).reshape(1, 4, 1) == quarter
    by_part = jnp.concatenate(
        [
            jnp.transpose(
                jnp.stack([qkv_sums[0, :256], qkv_sums[0, 512:]]).reshape(2, 4, 8, 8), (2, 0, 1, 3)
            ).reshape(8, 64),
            grad_fc1_bias.reshape(8, 128),
        ],
        axis=1,
    )
    by_part = jnp.where(here, by_part[:, None, :], 0.0).reshape(32, 192)
    vector = jnp.concatenate([sums, by_part], axis=1)
    for mask, bit in ((Y, y_bit), (X, x_bit), (CORE, core), (Z_HIGH, z_high), (Z_LOW, t & 1)):
        low, high = vector[: vector.shape[0] // 2], vector[vector.shape[0] // 2 :]
        send = jnp.where(bit == 1, low, high)
        vector = jnp.where(bit == 1, high, low) + swap(send, mask)
    vector = vector[0]
    grad_biases = vector[64:192].reshape(4, 32)
    return (
        layer_out,
        grad_input,
        vector[:64].reshape(2, 32),
        grad_biases,
        jnp.transpose(grad_w.reshape(128, 3, 256), (1, 0, 2)),
        vector[192:256].reshape(2, 4, 8),
        jnp.transpose(grad_proj),
        grad_fc1,
        vector[256:].reshape(1, 128),
        jnp.transpose(grad_fc2),
        grad_biases[3],
    )


def solution(mesh):
    spread = (mesh.shape["dp"], mesh.shape["tensor"]) == (8, 4)
    in_specs = (
        P(("dp", "tensor"), None),
        P(("dp", "tensor"), None),
        P("dp"),
        P(None, ("dp", "tensor")),
        P(None, ("dp", "tensor")),
        P(None, "dp", "tensor"),
        P(None, "tensor", "dp"),
        P("tensor", "dp"),
        P("dp", "tensor"),
        P("tensor", "dp"),
        P("tensor", "dp"),
    )
    out_specs = (
        P(("dp", "tensor"), None),
        P(("dp", "tensor"), None),
        P(None, ("dp", "tensor")),
        P(None, ("dp", "tensor")),
        P(None, "dp", "tensor"),
        P(None, "tensor", "dp"),
        P("tensor", "dp"),
        P("dp", "tensor"),
        P("tensor", "dp"),
        P("tensor", "dp"),
        P(("dp", "tensor")),
    )
    return jax.shard_map(
        on_device_spread if spread else on_device, mesh=mesh, in_specs=in_specs, out_specs=out_specs, check_vma=False
    )
```

```python
import math

import jax
import jax.numpy as jnp
from jax import lax
from jax.experimental import pallas as pl
from jax.experimental.pallas import tpu as pltpu
from jax.sharding import PartitionSpec as P

HD = 64


norm_eps = 1e-06
root_half = 0.7071067811865476
inv_root_tau = 0.3989422804014327


def normalize(values, gain_row, shift_row):
    centre = jnp.mean(values, axis=1, keepdims=True)
    offsets = values - centre
    inverse = lax.rsqrt(jnp.mean(offsets * offsets, axis=1, keepdims=True) + norm_eps)
    scaled = offsets * inverse
    return (scaled * gain_row + shift_row, scaled, inverse)


def normalize_back(upstream, scaled, inverse, gain_row):
    grad_hat = upstream * gain_row
    return (
        grad_hat
        - jnp.mean(grad_hat, axis=1, keepdims=True)
        - scaled * jnp.mean(grad_hat * scaled, axis=1, keepdims=True)
    ) * inverse


def gelu_value(inputs):
    return 0.5 * inputs * (1.0 + lax.erf(inputs * root_half))


def gelu_slope(inputs):
    return (
        0.5 * (1.0 + lax.erf(inputs * root_half))
        + inputs * jnp.exp(-0.5 * inputs * inputs) * inv_root_tau
    )


def fetch(qkv_weight, proj_weight, fc1_weight, fc2_weight, qv_bias, fc1_bias, gain_rows, bias_rows):
    matrices = (
        lax.all_gather(qkv_weight, "dp", axis=1, tiled=True),
        lax.all_gather(proj_weight, "dp", axis=1, tiled=True),
        lax.all_gather(fc1_weight, "dp", axis=0, tiled=True),
        lax.all_gather(fc2_weight, "dp", axis=1, tiled=True),
        lax.all_gather(qv_bias, "dp", axis=2, tiled=True),
        lax.all_gather(fc1_bias, "dp", axis=1, tiled=True),
    )
    vectors = (
        lax.all_gather(gain_rows, ("dp", "tensor"), axis=1, tiled=True),
        lax.all_gather(bias_rows, ("dp", "tensor"), axis=1, tiled=True),
    )
    return (matrices, (vectors[0].astype(jnp.float32), vectors[1].astype(jnp.float32)))


def spread_rows(local_rows):
    return lax.all_gather(local_rows, "tensor", axis=0, tiled=True)


def reduce_rows(term_fn, row_count):
    return lax.psum_scatter(
        term_fn(jnp.int32(0), lax.axis_size("tensor") * row_count),
        "tensor",
        scatter_dimension=0,
        tiled=True,
    )


def spread_grads(local_rows):
    return lax.all_gather(local_rows, "tensor", axis=0, tiled=True)


def reduce_grads(term_fn, row_count):
    return lax.psum_scatter(
        term_fn(jnp.int32(0), lax.axis_size("tensor") * row_count),
        "tensor",
        scatter_dimension=0,
        tiled=True,
    )


def forward(clip_rows, matrices, vectors):
    w_qkv, w_proj, w_fc1, w_fc2, b_qv, b_fc1 = matrices
    gain_rows, bias_rows = vectors
    row_count = clip_rows.shape[0]
    head_cols = w_qkv.shape[2]
    heads_here = head_cols // HD
    score_scale = 1.0 / math.sqrt(HD)
    inputs = clip_rows.astype(jnp.float32)
    normed_one, scaled_one, inverse_one = normalize(inputs, gain_rows[0], bias_rows[0])
    whole_one = spread_rows(normed_one.astype(jnp.bfloat16))
    seq_len = whole_one.shape[0]
    projected = jnp.einsum("sd,jde->jse", whole_one, w_qkv, preferred_element_type=jnp.float32)
    bias_cols = b_qv.reshape(2, head_cols).astype(jnp.float32)
    queries = (projected[0] + bias_cols[0]).astype(jnp.bfloat16).reshape(seq_len, heads_here, HD)
    keys_all = projected[1].astype(jnp.bfloat16).reshape(seq_len, heads_here, HD)
    values_all = (projected[2] + bias_cols[1]).astype(jnp.bfloat16).reshape(seq_len, heads_here, HD)
    scores = (
        jnp.einsum("qhd,khd->hqk", queries, keys_all, preferred_element_type=jnp.float32)
        * score_scale
    )
    top_score = jnp.max(scores, axis=2, keepdims=True)
    weights_exp = jnp.exp(scores - top_score)
    totals = jnp.sum(weights_exp, axis=2, keepdims=True)
    attn_probs = (weights_exp / totals).astype(jnp.bfloat16)
    log_total = top_score + jnp.log(totals)
    attended = (
        jnp.einsum("hqk,khd->qhd", attn_probs, values_all, preferred_element_type=jnp.float32)
        .reshape(seq_len, head_cols)
        .astype(jnp.bfloat16)
    )

    def proj_term(offset, length):
        return jnp.dot(attended, w_proj, preferred_element_type=jnp.float32)

    residual_one = inputs + (reduce_rows(proj_term, row_count) + bias_rows[2])
    normed_two, scaled_two, inverse_two = normalize(residual_one, gain_rows[1], bias_rows[1])
    whole_two = spread_rows(normed_two.astype(jnp.bfloat16))
    pre_act = jnp.dot(whole_two, w_fc1, preferred_element_type=jnp.float32) + b_fc1.reshape(
        -1
    ).astype(jnp.float32)
    hidden = gelu_value(pre_act).astype(jnp.bfloat16)

    def fc2_term(offset, length):
        return jnp.dot(hidden, w_fc2, preferred_element_type=jnp.float32)

    layer_out = residual_one + (reduce_rows(fc2_term, row_count) + bias_rows[3])
    stored = (
        scaled_one,
        inverse_one,
        whole_one,
        queries,
        keys_all,
        values_all,
        log_total,
        attended,
        scaled_two,
        inverse_two,
        whole_two,
        pre_act,
        hidden,
    )
    return (layer_out, stored)


def backward(upstream, matrices, vectors, stored):
    w_qkv, w_proj, w_fc1, w_fc2, b_qv, b_fc1 = matrices
    gain_rows, bias_rows = vectors
    (
        scaled_one,
        inverse_one,
        whole_one,
        queries,
        keys_all,
        values_all,
        log_total,
        attended,
        scaled_two,
        inverse_two,
        whole_two,
        pre_act,
        hidden,
    ) = stored
    row_count = upstream.shape[0]
    seq_len = queries.shape[0]
    heads_here = queries.shape[1]
    head_cols = heads_here * HD
    score_scale = 1.0 / math.sqrt(HD)
    grad_mlp = upstream.astype(jnp.bfloat16)
    grad_fc2_bias = jnp.sum(grad_mlp.astype(jnp.float32), axis=0)
    whole_mlp = spread_grads(grad_mlp)
    grad_fc2 = jnp.einsum("sf,sd->fd", hidden, whole_mlp, preferred_element_type=jnp.float32)
    grad_hidden = jnp.einsum("sd,fd->sf", whole_mlp, w_fc2, preferred_element_type=jnp.float32)
    grad_pre = (grad_hidden * gelu_slope(pre_act)).astype(jnp.bfloat16)
    grad_fc1_bias = jnp.sum(grad_pre.astype(jnp.float32), axis=0)
    grad_fc1 = jnp.einsum("sd,sf->df", whole_two, grad_pre, preferred_element_type=jnp.float32)

    def fc1_back(offset, length):
        return jnp.einsum("sf,df->sd", grad_pre, w_fc1, preferred_element_type=jnp.float32)

    grad_normed_two = reduce_grads(fc1_back, row_count)
    grad_residual = upstream + normalize_back(
        grad_normed_two, scaled_two, inverse_two, gain_rows[1]
    )
    grad_branch = grad_residual.astype(jnp.bfloat16)
    grad_proj_bias = jnp.sum(grad_branch.astype(jnp.float32), axis=0)
    whole_branch = spread_grads(grad_branch)
    grad_proj = jnp.einsum("se,sd->ed", attended, whole_branch, preferred_element_type=jnp.float32)
    grad_att = (
        jnp.einsum("sd,ed->se", whole_branch, w_proj, preferred_element_type=jnp.float32)
        .astype(jnp.bfloat16)
        .reshape(seq_len, heads_here, HD)
    )
    scores = (
        jnp.einsum("qhd,khd->hqk", queries, keys_all, preferred_element_type=jnp.float32)
        * score_scale
    )
    attn_probs = jnp.exp(scores - log_total)
    grad_probs = jnp.einsum(
        "qhd,khd->hqk", grad_att, values_all, preferred_element_type=jnp.float32
    )
    row_dot = jnp.sum(attn_probs * grad_probs, axis=2, keepdims=True)
    grad_scores = (attn_probs * (grad_probs - row_dot)).astype(jnp.bfloat16)
    grad_query = (
        jnp.einsum("hqk,khd->qhd", grad_scores, keys_all, preferred_element_type=jnp.float32)
        * score_scale
    ).astype(jnp.bfloat16)
    grad_key = (
        jnp.einsum("hqk,qhd->khd", grad_scores, queries, preferred_element_type=jnp.float32)
        * score_scale
    ).astype(jnp.bfloat16)
    grad_value = jnp.einsum(
        "hqk,qhd->khd",
        attn_probs.astype(jnp.bfloat16),
        grad_att,
        preferred_element_type=jnp.float32,
    ).astype(jnp.bfloat16)
    grad_qkv = jnp.stack([grad_query, grad_key, grad_value]).reshape(3, seq_len, head_cols)
    grad_qv = jnp.stack(
        [
            jnp.sum(grad_query.astype(jnp.float32), axis=0),
            jnp.sum(grad_value.astype(jnp.float32), axis=0),
        ]
    )
    grad_qkv_weight = jnp.einsum(
        "sd,jse->jde", whole_one, grad_qkv, preferred_element_type=jnp.float32
    )

    def qkv_back(offset, length):
        return jnp.einsum("jse,jde->sd", grad_qkv, w_qkv, preferred_element_type=jnp.float32)

    grad_normed_one = reduce_grads(qkv_back, row_count)
    grad_input = grad_residual + normalize_back(
        grad_normed_one, scaled_one, inverse_one, gain_rows[0]
    )
    grad_gain = jnp.stack(
        [
            jnp.sum(grad_normed_one * scaled_one, axis=0),
            jnp.sum(grad_normed_two * scaled_two, axis=0),
        ]
    )
    grad_bias = jnp.stack(
        [
            jnp.sum(grad_normed_one, axis=0),
            jnp.sum(grad_normed_two, axis=0),
            grad_proj_bias,
            grad_fc2_bias,
        ]
    )
    weight_part = (
        lax.psum_scatter(grad_qkv_weight, "dp", scatter_dimension=1, tiled=True),
        lax.psum_scatter(grad_proj, "dp", scatter_dimension=1, tiled=True),
        lax.psum_scatter(grad_fc1, "dp", scatter_dimension=0, tiled=True),
        lax.psum_scatter(grad_fc2, "dp", scatter_dimension=1, tiled=True),
        lax.psum_scatter(grad_qv, "dp", scatter_dimension=2, tiled=True),
        lax.psum_scatter(grad_fc1_bias.reshape(1, -1), "dp", scatter_dimension=1, tiled=True),
    )
    vector_part = (
        lax.psum_scatter(grad_gain, ("dp", "tensor"), scatter_dimension=1, tiled=True),
        lax.psum_scatter(grad_bias, ("dp", "tensor"), scatter_dimension=1, tiled=True),
    )
    return (grad_input, weight_part, vector_part)


def on_device(
    clip_rows,
    out_grad,
    clip_valid,
    gain_rows,
    bias_rows,
    qkv_weight,
    qv_bias,
    proj_weight,
    fc1_weight,
    fc1_bias,
    fc2_weight,
):
    clip_weight = clip_valid[0].astype(jnp.float32)
    upstream = out_grad.astype(jnp.float32) * clip_weight
    matrices, vectors = fetch(
        qkv_weight, proj_weight, fc1_weight, fc2_weight, qv_bias, fc1_bias, gain_rows, bias_rows
    )
    layer_out, stored = forward(clip_rows, matrices, vectors)
    matrices, vectors = fetch(
        qkv_weight, proj_weight, fc1_weight, fc2_weight, qv_bias, fc1_bias, gain_rows, bias_rows
    )
    unused_out, stored = forward(clip_rows, matrices, vectors)
    grad_input, weight_part, vector_part = backward(upstream, matrices, vectors, stored)
    return (
        (layer_out * clip_weight).astype(jnp.bfloat16),
        grad_input,
        vector_part[0],
        vector_part[1],
        weight_part[0],
        weight_part[4],
        weight_part[1],
        weight_part[2],
        weight_part[5],
        weight_part[3],
        vector_part[1][3],
    )


AXES = ("dp", "tensor")
Z_LOW, Z_HIGH, CORE, X, Y = 1, 2, 4, 8, 16
CHIP_MASKS = (0, X, Y, X | Y)
BF16, F32 = jnp.bfloat16, jnp.float32
NN, NT, TN = ((1,), (0,)), ((1,), (1,)), ((0,), (0,))
SHARE = 49
PAD = 56
CHIP_ID, CORE_ID, D_ID, T_ID = range(4)


def swap(value, mask):
    return lax.ppermute(value, AXES, [(i, i ^ mask) for i in range(32)])


def dot(left, right, dims):
    return lax.dot_general(left, right, (dims, ((), ())), preferred_element_type=F32)


def call(body, outs, scalars, *args, scratch=(), flops=0):
    moved = sum(math.prod(a.shape) * a.dtype.itemsize for a in args)
    moved += sum(math.prod(s) * jnp.dtype(t).itemsize for s, t in outs)
    held = sum(math.prod(s[:-1]) * max(s[-1], 128) * jnp.dtype(t).itemsize for s, t in scratch)
    return pl.pallas_call(
        body,
        out_shape=[jax.ShapeDtypeStruct(s, t) for s, t in outs],
        in_specs=[pl.BlockSpec(memory_space=pltpu.SMEM)]
        + [pl.BlockSpec(memory_space=pltpu.VMEM)] * len(args),
        out_specs=[pl.BlockSpec(memory_space=pltpu.VMEM)] * len(outs),
        scratch_shapes=[pltpu.VMEM(s, t) for s, t in scratch],
        compiler_params=pltpu.CompilerParams(vmem_limit_bytes=moved + held + (4 << 20)),
        cost_estimate=pl.CostEstimate(flops=flops, bytes_accessed=moved, transcendentals=0),
    )(scalars, *args)


def chip_lanes(ids, m):
    return pl.ds(pl.multiple_of((ids[CHIP_ID] ^ m) * 256, 256), 256)


def lanes(m):
    return slice(256 * m, 256 * m + 256)


def row_ids(shape):
    return lax.broadcasted_iota(jnp.int32, shape, 0)


def pick(condition, left, right):
    return jnp.where(jnp.full(left.shape, condition, jnp.int32) != 0, left, right)


def is_zero(number):
    return jnp.where(number == 0, 1, 0)


def z_low(ids):
    return ids[T_ID] & 1


def z_high(ids):
    return ids[T_ID] >> 1


def pack_kernel(ids, rows, gains, biases, qv, b_fc1, out, wide):
    lane32 = lax.broadcasted_iota(jnp.int32, (32, 128), 1)
    spot = (lane32 == row_ids((32, 128)) + 32 * ids[T_ID]).astype(F32).astype(BF16)
    lane8 = lax.broadcasted_iota(jnp.int32, (8, 128), 1)
    spot8 = (lane8 == row_ids((8, 128)) + 8 * ids[D_ID]).astype(F32).astype(BF16)
    g = dot(gains[...], spot, NN)
    b = dot(biases[...], spot, NN)
    qv_rows = dot(qv[...], spot8, NN)
    row_a = jnp.concatenate(
        [g[k : k + 1] for k in range(2)]
        + [b[k : k + 1] for k in range(4)]
        + [b_fc1[...].astype(F32), jnp.zeros((1, 128), F32)],
        axis=1,
    )
    row_b = jnp.concatenate([qv_rows[k : k + 1] for k in range(8)], axis=1)
    flag = jnp.full((PAD, 1024), ids[4], jnp.int32).astype(F32)
    row = row_ids((PAD, 1024))
    tail = jnp.where(row == SHARE, row_a, jnp.where(row == SHARE + 1, row_b, flag))
    wide[0 : rows.shape[0], :] = rows[...].astype(F32)
    for j in range(8):
        block = wide[SHARE * j : SHARE * j + PAD, :]
        out[j, :, :] = jnp.where(row < SHARE, block, tail).astype(BF16)


def pack_grad_kernel(ids, rows, out, wide):
    wide[0 : rows.shape[0], :] = rows[...].astype(F32)
    for j in range(8):
        out[j, :, :] = wide[SHARE * j : SHARE * j + PAD, :].astype(BF16)


def pick_kernel(ids, got, here, there, slots):
    row8 = row_ids((8, 1024))
    row = row_ids((PAD, 1024))
    seen = jnp.zeros((1, 1024), F32)
    mine = jnp.zeros((PAD, 1024), F32)
    other = jnp.zeros((PAD, 1024), F32)
    params = jnp.zeros((8, 1024), F32)
    qv = jnp.zeros((1, 1024), F32)
    high = jnp.full((1, 1024), z_high(ids), jnp.int32).astype(F32)
    for c in range(8):
        block = got[c, :, :].astype(F32)
        flag = block[SHARE + 2 : SHARE + 3]
        is_mine = jnp.where(seen == high, flag, 0.0)
        is_other = flag - is_mine
        seen = seen + flag
        mine = jnp.where(is_mine > 0.5, block, mine)
        other = jnp.where(is_other > 0.5, block, other)
        params = jnp.where(row8 == c, block[SHARE : SHARE + 1], params)
        qv = qv + block[SHARE + 1 : SHARE + 2]
        slots[c : c + 1, :] = is_mine[:, 0:128]
        slots[8 + c : 9 + c, :] = is_other[:, 0:128]
    for value, out in ((mine, here), (other, there)):
        out[0:PAD, :] = jnp.where(row == PAD - 1, qv, value).astype(BF16)
        out[PAD : PAD + 8, :] = params.astype(BF16)


def pick_grad_kernel(ids, slots, got, here, there):
    mine = jnp.zeros((PAD, 1024), F32)
    other = jnp.zeros((PAD, 1024), F32)
    for c in range(8):
        block = got[c, :, :].astype(F32)
        mine = jnp.where(slots[c : c + 1, 0:1] > 0.5, block, mine)
        other = jnp.where(slots[8 + c : 9 + c, 0:1] > 0.5, block, other)
    here[...] = mine.astype(BF16)
    there[...] = other.astype(BF16)


def lay_rows(ids, here, r1, r2, r3, wide):
    low = is_zero(z_low(ids))
    for m in range(4):
        cols = chip_lanes(ids, m)
        blocks = [ref[0:PAD, cols].astype(F32) for ref in (here, r1, r2, r3)]
        order = (
            pick(low, blocks[0], blocks[1]),
            pick(low, blocks[2], blocks[3]),
            pick(low, blocks[1], blocks[0]),
            pick(low, blocks[3], blocks[2]),
        )
        for i, block in enumerate(order):
            wide[SHARE * i : SHARE * i + SHARE, lanes(m)] = block[0:SHARE]


def norm_parts(values):
    centre = jnp.mean(values, axis=1, keepdims=True)
    offsets = values - centre
    inverse = lax.rsqrt(jnp.mean(offsets * offsets, axis=1, keepdims=True) + norm_eps)
    return offsets * inverse, inverse


def norm_one_kernel(ids, here, r1, r2, r3, rows, normed, vec, qv_bias, b_fc1, wide, small):
    lay_rows(ids, here, r1, r2, r3, wide)
    own = here[PAD - 8 : PAD + 8, :].astype(F32)
    far = r2[PAD - 8 : PAD + 8, :].astype(F32)
    tails = [own[8:], far[8:]] + [r[PAD : PAD + 8, :].astype(F32) for r in (r1, r3)]
    params = tails[0] + tails[1] + tails[2] + tails[3]
    small[...] = jnp.zeros_like(small)
    for d in range(8):
        for k in range(6):
            small[k : k + 1, 128 * d : 128 * d + 128] = params[
                d : d + 1, 128 * k : 128 * k + 128
            ]
    for m in range(4):
        vec[:, lanes(m)] = small[:, chip_lanes(ids, m)]
    home = pick(is_zero(ids[CORE_ID]), own, far)
    for k in range(8):
        qv_bias[k : k + 1, :] = home[7:8, 128 * k : 128 * k + 128]
        b_fc1[0:1, 128 * k : 128 * k + 128] = home[8 + k : 9 + k, 768:896]
    values = wide[...]
    scaled, _ = norm_parts(values)
    rows[...] = values.astype(BF16)
    normed[...] = (scaled * vec[0:1, :] + vec[2:3, :]).astype(BF16)


def lay_grad_kernel(ids, here, r1, r2, r3, out, wide):
    lay_rows(ids, here, r1, r2, r3, wide)
    out[...] = wide[...].astype(BF16)


def join_rows(wide, own, got):
    half = own.shape[0]
    wide[0:half, :] = own[...].astype(F32)
    wide[half : 2 * half, :] = got[...].astype(F32)


def qkv_kernel(ids, own, got, qv_bias, w0, w1, w2, w3, whole, o0, o1, o2, o3, wide, heads):
    weights = (w0, w1, w2, w3)
    join_rows(wide, own, got)
    whole[...] = wide[...].astype(BF16)
    for j in range(3):
        total = dot(whole[:, lanes(0)], w0[:, lanes(j)], NN)
        for m in range(1, 4):
            total = total + dot(whole[:, lanes(m)], weights[m][:, lanes(j)], NN)
        for h in range(4):
            part = total[:, 64 * h : 64 * h + 64]
            if j != 1:
                k = (j // 2) * 4 + h
                part = part + qv_bias[k : k + 1, 0:64]
            heads[h, :, 64 * j : 64 * j + 64] = part.astype(BF16)
    for m, out in enumerate((o0, o1, o2, o3)):
        out[...] = heads[ids[CHIP_ID] ^ m, :, :]


STEP = 224


def attention_kernel(ids, a0, a1, a2, a3, o0, o1, o2, o3, lse, stage, q, k, v):
    tokens = a0.shape[0]
    for m, part in enumerate((a0, a1, a2, a3)):
        stage[tokens * m : tokens * m + tokens, :] = part[...].astype(F32)
    q[...] = (stage[:, 0:64] * 0.125).astype(BF16)
    k[...] = stage[:, 64:128].astype(BF16)
    v[...] = stage[:, 128:192].astype(BF16)

    def body(i, carry):
        rows = pl.ds(pl.multiple_of(i * STEP, 32), STEP)
        scores = dot(q[rows, :], k[...], NT)
        top = jnp.max(scores, axis=1, keepdims=True)
        weights = jnp.exp(scores - top)
        total = jnp.sum(weights, axis=1, keepdims=True)
        mixed = dot(weights.astype(BF16), v[...], NN)
        stage[rows, 0:64] = mixed / total
        spread = jnp.broadcast_to(top + jnp.log(total), (STEP, 128))
        lse[i, :, :] = jnp.transpose(spread)[0:8, :]
        return carry

    lax.fori_loop(0, stage.shape[0] // STEP, body, 0)
    for m, out in enumerate((o0, o1, o2, o3)):
        out[...] = stage[tokens * m : tokens * m + tokens, 0:64].astype(BF16)


def attention_back_kernel(
    ids, a0, a1, a2, a3, g0, g1, g2, g3, lse, o0, o1, o2, o3, stage, q, k, v, g, grad_k, grad_v
):
    tokens = a0.shape[0]
    for m, part in enumerate((a0, a1, a2, a3)):
        stage[tokens * m : tokens * m + tokens, :] = part[...].astype(F32)
    q[...] = (stage[:, 0:64] * 0.125).astype(BF16)
    k[...] = stage[:, 64:128].astype(BF16)
    v[...] = stage[:, 128:192].astype(BF16)
    for m, part in enumerate((g0, g1, g2, g3)):
        stage[tokens * m : tokens * m + tokens, 0:64] = part[...].astype(F32)
    g[...] = stage[:, 0:64].astype(BF16)
    keys_t = jnp.transpose(k[...])
    grad_k[...] = jnp.zeros_like(grad_k)
    grad_v[...] = jnp.zeros_like(grad_v)

    def body(i, carry):
        rows = pl.ds(pl.multiple_of(i * STEP, 32), STEP)
        queries, grad = q[rows, :], g[rows, :]
        probs = jnp.exp(dot(k[...], queries, NT) - lse[i, 0:1, :])
        grad_probs = dot(v[...], grad, NT)
        row_dot = jnp.sum(probs * grad_probs, axis=0, keepdims=True)
        grad_scores = (probs * (grad_probs - row_dot)).astype(BF16)
        grad_v[...] += dot(probs.astype(BF16), grad, NN)
        grad_k[...] += dot(grad_scores, queries, NN)
        stage[rows, 0:64] = jnp.transpose(dot(keys_t, grad_scores, NN)) * 0.125
        return carry

    lax.fori_loop(0, stage.shape[0] // STEP, body, 0)
    for m, out in enumerate((o0, o1, o2, o3)):
        rows = slice(tokens * m, tokens * m + tokens)
        out[:, 0:64] = stage[rows, 0:64].astype(BF16)
        out[:, 64:128] = grad_k[rows, :].astype(BF16)
        out[:, 128:192] = grad_v[rows, :].astype(BF16)


def split_rows(total, keep, send, cols):
    half = keep.shape[0]
    keep[:, cols] = total[:half]
    send[:, cols] = total[half:].astype(BF16)


def proj_kernel(ids, a0, a1, a2, a3, w0, w1, w2, w3, joined, keep, send, heads):
    for m, part in enumerate((a0, a1, a2, a3)):
        heads[m, :, :] = part[...]
    for h in range(4):
        joined[:, 64 * h : 64 * h + 64] = heads[h ^ ids[CHIP_ID], :, :]
    for m, weight in enumerate((w0, w1, w2, w3)):
        split_rows(dot(joined[...], weight[:, 0:256], NT), keep, send, lanes(m))


def pair_kernel(ids, keep, got, part, send):
    total = keep[...] + got[...].astype(F32)
    part[...] = total
    send[...] = total.astype(BF16)


def half_kernel(ids, keep, got, part, send):
    own = part.shape[0]
    total = keep[...] + got[...].astype(F32)
    low = is_zero(z_low(ids))
    part[...] = pick(low, total[:own], total[own:])
    send[...] = pick(low, total[own:], total[:own]).astype(BF16)


def norm_two_kernel(ids, rows, part, got, vec, residual, normed):
    total = rows[...].astype(F32) + (part[...] + got[...].astype(F32) + vec[4:5, :])
    residual[...] = total
    scaled, _ = norm_parts(total)
    normed[...] = (scaled * vec[1:2, :] + vec[3:4, :]).astype(BF16)


def grad_hidden_kernel(ids, own, got, w0, w1, w2, w3, whole, out, wide):
    join_rows(wide, own, got)
    whole[...] = wide[...].astype(BF16)
    for c in range(4):
        total = dot(whole[:, lanes(0)], w0[:, lanes(c)], NN)
        for m, weight in enumerate((w1, w2, w3)):
            total = total + dot(whole[:, lanes(m + 1)], weight[:, lanes(c)], NN)
        out[:, lanes(c)] = total


def fc_kernel(
    ids, own, got, grad_hidden, b_fc1, w0, w1, w2, w3, whole, hidden, grad_pre, sums, keep, send, wide
):
    weights = (w0, w1, w2, w3)
    join_rows(wide, own, got)
    whole[...] = wide[...].astype(BF16)
    wide[...] = jnp.zeros_like(wide)

    def body(c, carry):
        cols = pl.ds(pl.multiple_of(c * 256, 256), 256)
        fc1 = pl.ds(pl.multiple_of(c * 256 + 256, 256), 256)
        pre = b_fc1[:, cols] + dot(whole[:, lanes(0)], w0[:, fc1], NN)
        for m in range(1, 4):
            pre = pre + dot(whole[:, lanes(m)], weights[m][:, fc1], NN)
        half_erf = 0.5 * (1.0 + lax.erf(pre * root_half))
        hidden[:, cols] = (pre * half_erf).astype(BF16)
        slope = half_erf + pre * jnp.exp(-0.5 * pre * pre) * inv_root_tau
        grad = (grad_hidden[:, cols] * slope).astype(BF16)
        grad_pre[:, cols] = grad
        sums[:, cols] = jnp.sum(grad.astype(F32), axis=0, keepdims=True)
        for m in range(4):
            wide[:, lanes(m)] += dot(grad, weights[m][:, fc1], NT)
        return carry

    lax.fori_loop(0, 4, body, 0)
    for m in range(4):
        split_rows(wide[:, lanes(m)], keep, send, lanes(m))


def norm_back(total, scaled, inverse, gain):
    hat = total * gain
    return (
        hat
        - jnp.mean(hat, axis=1, keepdims=True)
        - scaled * jnp.mean(hat * scaled, axis=1, keepdims=True)
    ) * inverse


def norm_two_back_kernel(ids, residual, part, got, grads, vec, grad_residual, grad_branch, sums):
    scaled, inverse = norm_parts(residual[...])
    total = part[...] + got[...].astype(F32)
    upstream = grads[...].astype(F32)
    result = upstream + norm_back(total, scaled, inverse, vec[1:2, :])
    branch = result.astype(BF16)
    grad_residual[...] = result
    grad_branch[...] = branch
    own = total.shape[0] // 2
    row = row_ids(total.shape)
    low = jnp.full(total.shape, z_low(ids), jnp.int32)
    mine = jnp.where(row < own, 1 - low, low) != 0

    def column_sum(value):
        return jnp.sum(jnp.where(mine, value, 0.0), axis=0, keepdims=True)

    sums[0:1, :] = column_sum(total * scaled)
    sums[1:2, :] = column_sum(total)
    sums[2:3, :] = column_sum(branch.astype(F32))
    sums[3:4, :] = column_sum(upstream)
    sums[4:8, :] = jnp.zeros((4, sums.shape[1]), F32)


def grad_att_kernel(ids, own, got, w0, w1, w2, w3, whole, o0, o1, o2, o3, wide, heads):
    join_rows(wide, own, got)
    whole[...] = wide[...].astype(BF16)
    total = dot(whole[:, lanes(0)], w0[:, 0:256], NN)
    for m, weight in enumerate((w1, w2, w3)):
        total = total + dot(whole[:, lanes(m + 1)], weight[:, 0:256], NN)
    for h in range(4):
        heads[h, :, :] = total[:, 64 * h : 64 * h + 64].astype(BF16)
    for m, out in enumerate((o0, o1, o2, o3)):
        out[...] = heads[ids[CHIP_ID] ^ m, :, :]


def qkv_back_kernel(ids, g0, g1, g2, g3, w0, w1, w2, w3, joined, keep, send, sums, heads):
    for m, part in enumerate((g0, g1, g2, g3)):
        heads[m, :, :] = part[...]
    for h in range(4):
        part = heads[h ^ ids[CHIP_ID], :, :]
        for j in range(3):
            piece = part[:, 64 * j : 64 * j + 64]
            joined[:, 256 * j + 64 * h : 256 * j + 64 * h + 64] = piece
            if j != 1:
                k = (j // 2) * 4 + h
                total = jnp.sum(piece.astype(F32), axis=0, keepdims=True)
                sums[0:1, 128 * k : 128 * k + 128] = jnp.concatenate(
                    [total, jnp.zeros((1, 64), F32)], axis=1
                )
    for m, weight in enumerate((w0, w1, w2, w3)):
        split_rows(dot(joined[...], weight[...], NT), keep, send, lanes(m))


def to_owners(ids, value, wide, here, there):
    wide[0 : 2 * SHARE, :] = value
    wide[2 * SHARE :, :] = jnp.zeros((wide.shape[0] - 2 * SHARE, wide.shape[1]), F32)
    for m in range(4):
        cols = chip_lanes(ids, m)
        here[0:PAD, cols] = wide[0:PAD, lanes(m)].astype(BF16)
        there[0:PAD, cols] = wide[SHARE : SHARE + PAD, lanes(m)].astype(BF16)


def own_half(ids, ref):
    own = ref.shape[0] // 2
    value = ref[...].astype(F32)
    return pick(is_zero(z_low(ids)), value[:own], value[own:])


def norm_one_back_kernel(
    ids, rows, part, got, grad_residual, vec, sums_two, sums_fc1, sums_qv, here, there, small_out, wide
):
    scaled, inverse = norm_parts(own_half(ids, rows))
    total = part[...] + got[...].astype(F32)
    result = own_half(ids, grad_residual) + norm_back(total, scaled, inverse, vec[0:1, :])
    to_owners(ids, result, wide, here, there)
    small = jnp.concatenate(
        [
            jnp.sum(total * scaled, axis=0, keepdims=True),
            sums_two[0:1, :],
            jnp.sum(total, axis=0, keepdims=True),
            sums_two[1:4, :],
            sums_qv[...],
            sums_fc1[...],
        ],
        axis=0,
    )
    small_out[...] = small.astype(BF16)
    here[PAD : PAD + 8, :] = small.astype(BF16)
    there[PAD : PAD + 8, :] = small.astype(BF16)


def layer_out_kernel(ids, residual, part, got, vec, here, there, wide):
    result = own_half(ids, residual) + (part[...] + got[...].astype(F32) + vec[5:6, :])
    to_owners(ids, result, wide, here, there)


def fc2_kernel(ids, hidden, w0, w1, w2, w3, keep, send):
    for m, weight in enumerate((w0, w1, w2, w3)):
        split_rows(dot(hidden[...], weight[...], NT), keep, send, lanes(m))


def give_kernel(ids, slots, here, away, out):
    left = here[0:PAD, :].astype(F32)
    right = away[0:PAD, :].astype(F32)
    for c in range(8):
        value = jnp.where(slots[8 + c : 9 + c, 0:1] > 0.5, right, 0.0)
        out[c, :, :] = jnp.where(slots[c : c + 1, 0:1] > 0.5, left, value).astype(BF16)


def give_grad_kernel(ids, slots, here, s1, away, s3, out, rel, flat, tail):
    left = here[0:PAD, :].astype(F32)
    right = away[0:PAD, :].astype(F32)
    own = here[PAD : PAD + 8, :].astype(F32)
    far = away[PAD : PAD + 8, :].astype(F32)
    rel[...] = own + far + s1[...].astype(F32) + s3[...].astype(F32)
    home = pick(is_zero(ids[CORE_ID]), own, far)
    for m in range(4):
        flat[:, chip_lanes(ids, m)] = rel[:, lanes(m)]
    tail[...] = jnp.zeros_like(tail)
    for k in range(8):
        row, lane = (SHARE + k, 128) if k < 7 else (SHARE, 256)
        tail[row : row + 1, lane : lane + 128] = home[6:7, 128 * k : 128 * k + 128]
    row = row_ids((PAD, 1024))
    for c in range(8):
        cols = slice(128 * c, 128 * c + 128)
        tail[SHARE : SHARE + 6, 0:128] = flat[0:6, cols]
        tail[SHARE + 6 : PAD, 0:128] = home[7:8, cols]
        value = jnp.where(slots[8 + c : 9 + c, 0:1] > 0.5, right, 0.0)
        value = jnp.where(slots[c : c + 1, 0:1] > 0.5, left, value)
        out[c, :, :] = jnp.where(row < SHARE, value, tail[...]).astype(BF16)


def take_kernel(ids, got, out, wide):
    for c in range(8):
        wide[SHARE * c : SHARE * c + SHARE, :] = got[c, :, :].astype(F32)[0:SHARE]
    out[...] = wide[...].astype(out.dtype)


def take_grad_kernel(ids, got, out, gains, biases, last, qv, b_fc1):
    total = jnp.zeros((8, 384), F32)
    for c in range(8):
        out[SHARE * c : SHARE * c + SHARE, :] = got[c, :, :].astype(F32)[0:SHARE]
        total = total + got[c, PAD - 8 : PAD, 0:384].astype(F32)
    rows = pltpu.roll(total[:, 0:128], (128 - 32 * ids[T_ID]) & 127, 1)
    gains[...] = rows[1:3, 0:32]
    biases[...] = rows[3:7, 0:32]
    last[...] = rows[6:7, 0:32]
    b_fc1[...] = total[7:8, 0:128]
    parts = jnp.concatenate([total[1:8, 128:256], total[1:2, 256:384]], axis=0)
    qv[...] = pltpu.roll(parts, (128 - 8 * ids[D_ID]) & 127, 1)[:, 0:8]


def shards_kernel(ids, qkv, proj, fc1, fc2, first, second, third):
    for j in range(3):
        first[:, lanes(j)] = qkv[j, :, :]
    second[:, 0:256] = jnp.transpose(proj[...])
    second[:, 256:1280] = fc1[...]
    third[...] = jnp.transpose(fc2[...])


def offer_kernel(ids, own, far, send):
    @pl.when(ids[CORE_ID] == 0)
    def _():
        send[...] = far[...]

    @pl.when(ids[CORE_ID] != 0)
    def _():
        send[...] = own[...]


def merge_kernel(ids, own, far, got, out):
    half = own.shape[0]

    @pl.when(ids[CORE_ID] == 0)
    def _():
        out[0:half, :] = own[...]
        out[half:, :] = got[...]

    @pl.when(ids[CORE_ID] != 0)
    def _():
        out[0:half, :] = got[...]
        out[half:, :] = far[...]


def grads_of(near, far, first_col=0):
    def grads_kernel(ids, left, right, send, here, there):
        for slot, m in ((0, near), (1, 3)):
            send[slot, :, :] = dot(left[:, lanes(m)], right[...], TN).astype(BF16)
        here[...] = dot(left[:, lanes(0)], right[...], TN)
        there[...] = dot(left[:, lanes(far)], right[...], TN)

    return grads_kernel


def sum_grad(ids, left, right, x_first):
    first, second, near, far = (X, Y, 1, 2) if x_first else (Y, X, 2, 1)
    n = right.shape[1]
    send, here, there = call(
        grads_of(near, far),
        [((2, 256, n), BF16), ((256, n), F32), ((256, n), F32)],
        ids,
        left,
        right,
        flops=2 * left.shape[0] * 1024 * n,
    )
    got = swap(send, first)
    other = (there + got[1].astype(F32)).astype(BF16)
    whole = here + got[0].astype(F32)
    return whole + swap(other, second).astype(F32)


def settle_grad(part, core):
    pairs = [(i, i ^ Z_HIGH) for i in range(32) if i & CORE]
    moved = lax.ppermute(part.astype(BF16), AXES, pairs).astype(F32)
    part = jnp.where(core == 0, part, moved)
    low, high = part[:128], part[128:]
    send = jnp.where(core == 0, high, low)
    keep = jnp.where(core == 0, low, high)
    return keep + swap(send.astype(BF16), CORE).astype(F32)


def on_device_spread(
    clip_rows,
    out_grad,
    clip_valid,
    gain_rows,
    bias_rows,
    qkv_weight,
    qv_bias,
    proj_weight,
    fc1_weight,
    fc1_bias,
    fc2_weight,
):
    d, t = lax.axis_index("dp"), lax.axis_index("tensor")
    core = d & 1
    ids = jnp.stack([d >> 1, core, d, t, clip_valid[0]]).astype(jnp.int32)
    count = clip_rows.shape[0]
    half, own = count // 2, count // 4
    block = (8, PAD, 1024)
    behind = (PAD + 8, 1024)

    (sent,) = call(
        pack_kernel,
        [(block, BF16)],
        ids,
        clip_rows,
        gain_rows,
        bias_rows,
        qv_bias.reshape(8, 8),
        fc1_bias,
        scratch=[((400, 1024), F32)],
    )
    shards = call(
        shards_kernel,
        [((128, 768), BF16), ((128, 1280), BF16), ((128, 1024), BF16)],
        ids,
        qkv_weight,
        proj_weight,
        fc1_weight,
        fc2_weight,
    )

    def gather(shard, by_y):
        far = swap(shard, Z_HIGH)
        (send,) = call(offer_kernel, [(shard.shape, BF16)], ids, shard, far)
        (w0,) = call(
            merge_kernel, [((256, shard.shape[1]), BF16)], ids, shard, far, swap(send, CORE)
        )
        w1, w2 = swap(w0, X), swap(w0, Y)
        return w0, w1, w2, (swap(w1, Y) if by_y else swap(w2, X))

    got = lax.all_to_all(sent, "dp", 0, 0)
    w_qkv = gather(shards[0], True)
    here, there, slots = call(
        pick_kernel, [(behind, BF16), (behind, BF16), ((16, 128), F32)], ids, got
    )
    r1, r2, r3 = swap(here, Z_LOW), swap(there, Z_HIGH), swap(there, Z_LOW | Z_HIGH)
    rows, normed, vec, qkv_bias, b_fc1 = call(
        norm_one_kernel,
        [
            ((half, 1024), BF16),
            ((half, 1024), BF16),
            ((8, 1024), F32),
            ((8, 128), F32),
            ((1, 1024), F32),
        ],
        ids,
        here,
        r1,
        r2,
        r3,
        scratch=[((half, 1024), F32), ((8, 1024), F32)],
    )
    late = lax.optimization_barrier((shards[1], shards[2], out_grad, here))
    w_mid = gather(late[0], False)
    w_fc2 = gather(late[1], True)

    wide = ((count, 1024), F32)
    whole_one, *qkv = call(
        qkv_kernel,
        [((count, 1024), BF16)] + [((count, 192), BF16)] * 4,
        ids,
        normed,
        swap(normed, CORE),
        qkv_bias,
        *w_qkv,
        scratch=[wide, ((4, count, 192), BF16)],
        flops=2 * count * 1024 * 768,
    )

    def trade(parts):
        return [parts[0]] + [swap(parts[m], CHIP_MASKS[m]) for m in range(1, 4)]

    qkv = trade(qkv)
    tokens = 4 * count
    *mixed, lse = call(
        attention_kernel,
        [((count, 64), BF16)] * 4 + [((tokens // STEP, 8, STEP), F32)],
        ids,
        *qkv,
        scratch=[((tokens, 192), F32)] + [((tokens, 64), BF16)] * 3,
        flops=4 * tokens * tokens * 64,
    )
    attended, keep, send = call(
        proj_kernel,
        [((count, 256), BF16), ((half, 1024), F32), ((half, 1024), BF16)],
        ids,
        *trade(mixed),
        *w_mid,
        scratch=[((4, count, 64), BF16)],
        flops=2 * count * 1024 * 256,
    )

    def all_z(keep, send):
        part, send = call(
            pair_kernel,
            [((half, 1024), F32), ((half, 1024), BF16)],
            ids,
            keep,
            swap(send, CORE),
        )
        return part, swap(send, Z_LOW)

    def one_z(keep, send):
        part, send = call(
            half_kernel, [((own, 1024), F32), ((own, 1024), BF16)], ids, keep, swap(send, CORE)
        )
        return part, swap(send, Z_LOW)

    residual, normed_two = call(
        norm_two_kernel,
        [((half, 1024), F32), ((half, 1024), BF16)],
        ids,
        rows,
        *all_z(keep, send),
        vec,
    )

    (sent,) = call(
        pack_grad_kernel, [(block, BF16)], ids, late[2], scratch=[((400, 1024), F32)]
    )
    got = lax.all_to_all(sent, "dp", 0, 0)
    here, there = call(pick_grad_kernel, [((PAD, 1024), BF16)] * 2, ids, slots, got)
    r1, r2, r3 = swap(here, Z_LOW), swap(there, Z_HIGH), swap(there, Z_LOW | Z_HIGH)
    (grads,) = call(
        lay_grad_kernel,
        [((half, 1024), BF16)],
        ids,
        here,
        r1,
        r2,
        r3,
        scratch=[((half, 1024), F32)],
    )
    whole_mlp, grad_hidden = call(
        grad_hidden_kernel,
        [((count, 1024), BF16), ((count, 1024), F32)],
        ids,
        grads,
        swap(grads, CORE),
        *w_fc2,
        scratch=[wide],
        flops=2 * count * 1024 * 1024,
    )

    whole_two, hidden, grad_pre, sums_fc1, keep, send = call(
        fc_kernel,
        [((count, 1024), BF16)] * 3
        + [((1, 1024), F32), ((half, 1024), F32), ((half, 1024), BF16)],
        ids,
        normed_two,
        swap(normed_two, CORE),
        grad_hidden,
        b_fc1,
        *w_mid,
        scratch=[wide],
        flops=4 * count * 1024 * 1024,
    )
    grad_residual, grad_branch, sums_two = call(
        norm_two_back_kernel,
        [((half, 1024), F32), ((half, 1024), BF16), ((8, 1024), F32)],
        ids,
        residual,
        *all_z(keep, send),
        grads,
        vec,
    )

    whole_branch, *grad_att = call(
        grad_att_kernel,
        [((count, 1024), BF16)] + [((count, 64), BF16)] * 4,
        ids,
        grad_branch,
        swap(grad_branch, CORE),
        *w_mid,
        scratch=[wide, ((4, count, 64), BF16)],
        flops=2 * count * 1024 * 256,
    )
    grad_qkv = call(
        attention_back_kernel,
        [((count, 192), BF16)] * 4,
        ids,
        *qkv,
        *trade(grad_att),
        lse,
        scratch=[((tokens, 192), F32)] + [((tokens, 64), BF16)] * 4 + [((tokens, 64), F32)] * 2,
        flops=10 * tokens * tokens * 64,
    )
    joined, keep, send, sums_qv = call(
        qkv_back_kernel,
        [((count, 768), BF16), ((half, 1024), F32), ((half, 1024), BF16), ((1, 1024), F32)],
        ids,
        *trade(grad_qkv),
        *w_qkv,
        scratch=[((4, count, 192), BF16)],
        flops=2 * count * 1024 * 768,
    )
    here, there, small = call(
        norm_one_back_kernel,
        [(behind, BF16), (behind, BF16), ((8, 1024), BF16)],
        ids,
        rows,
        *one_z(keep, send),
        grad_residual,
        vec,
        sums_two,
        sums_fc1,
        sums_qv,
        scratch=[((2 * PAD, 1024), F32)],
    )
    (sent,) = call(
        give_grad_kernel,
        [(block, BF16)],
        ids,
        slots,
        here,
        swap(small, Z_LOW),
        swap(there, Z_HIGH),
        swap(small, Z_LOW | Z_HIGH),
        scratch=[((8, 1024), F32), ((8, 1024), F32), ((PAD, 1024), F32)],
    )
    input_grad, grad_gains, grad_biases, grad_last, grad_qv, grad_b_fc1 = call(
        take_grad_kernel,
        [
            ((count, 1024), F32),
            ((2, 32), F32),
            ((4, 32), F32),
            ((1, 32), F32),
            ((8, 8), F32),
            ((1, 128), F32),
        ],
        ids,
        lax.all_to_all(sent, "dp", 0, 0),
    )

    keep, send = call(
        fc2_kernel,
        [((half, 1024), F32), ((half, 1024), BF16)],
        ids,
        hidden,
        *w_fc2,
        flops=2 * count * 1024 * 1024,
    )
    here, there = call(
        layer_out_kernel,
        [((PAD, 1024), BF16)] * 2,
        ids,
        residual,
        *one_z(keep, send),
        vec,
        scratch=[((2 * PAD, 1024), F32)],
    )
    (sent,) = call(
        give_kernel, [(block, BF16)], ids, slots, here, swap(there, Z_HIGH)
    )
    (layer_out,) = call(
        take_kernel,
        [((count, 1024), BF16)],
        ids,
        lax.all_to_all(sent, "dp", 0, 0),
        scratch=[((count, 1024), F32)],
    )

    grad_fc2 = settle_grad(sum_grad(ids, whole_mlp, hidden, True), core)
    grad_fc1 = settle_grad(sum_grad(ids, whole_two, grad_pre, False), core)
    grad_proj = settle_grad(sum_grad(ids, whole_branch, attended, True), core)
    grad_w = settle_grad(sum_grad(ids, whole_one, joined, False), core)
    return (
        layer_out,
        input_grad,
        grad_gains,
        grad_biases,
        jnp.transpose(grad_w.reshape(128, 3, 256), (1, 0, 2)),
        grad_qv.reshape(2, 4, 8),
        jnp.transpose(grad_proj),
        grad_fc1,
        grad_b_fc1,
        jnp.transpose(grad_fc2),
        grad_last[0],
    )


def solution(mesh):
    spread = (mesh.shape["dp"], mesh.shape["tensor"]) == (8, 4)
    in_specs = (
        P(("dp", "tensor"), None),
        P(("dp", "tensor"), None),
        P("dp"),
        P(None, ("dp", "tensor")),
        P(None, ("dp", "tensor")),
        P(None, "dp", "tensor"),
        P(None, "tensor", "dp"),
        P("tensor", "dp"),
        P("dp", "tensor"),
        P("tensor", "dp"),
        P("tensor", "dp"),
    )
    out_specs = (
        P(("dp", "tensor"), None),
        P(("dp", "tensor"), None),
        P(None, ("dp", "tensor")),
        P(None, ("dp", "tensor")),
        P(None, "dp", "tensor"),
        P(None, "tensor", "dp"),
        P("tensor", "dp"),
        P("dp", "tensor"),
        P("tensor", "dp"),
        P("tensor", "dp"),
        P(("dp", "tensor")),
    )
    return jax.shard_map(
        on_device_spread if spread else on_device, mesh=mesh, in_specs=in_specs, out_specs=out_specs, check_vma=False
    )
```

```python
import math

import jax
import jax.numpy as jnp
from jax import lax
from jax.experimental import pallas as pl
from jax.experimental.pallas import tpu as pltpu
from jax.sharding import PartitionSpec as P

HD = 64


norm_eps = 1e-06
root_half = 0.7071067811865476
inv_root_tau = 0.3989422804014327


def normalize(values, gain_row, shift_row):
    centre = jnp.mean(values, axis=1, keepdims=True)
    offsets = values - centre
    inverse = lax.rsqrt(jnp.mean(offsets * offsets, axis=1, keepdims=True) + norm_eps)
    scaled = offsets * inverse
    return (scaled * gain_row + shift_row, scaled, inverse)


def normalize_back(upstream, scaled, inverse, gain_row):
    grad_hat = upstream * gain_row
    return (
        grad_hat
        - jnp.mean(grad_hat, axis=1, keepdims=True)
        - scaled * jnp.mean(grad_hat * scaled, axis=1, keepdims=True)
    ) * inverse


def gelu_value(inputs):
    return 0.5 * inputs * (1.0 + lax.erf(inputs * root_half))


def gelu_slope(inputs):
    return (
        0.5 * (1.0 + lax.erf(inputs * root_half))
        + inputs * jnp.exp(-0.5 * inputs * inputs) * inv_root_tau
    )


def fetch(qkv_weight, proj_weight, fc1_weight, fc2_weight, qv_bias, fc1_bias, gain_rows, bias_rows):
    matrices = (
        lax.all_gather(qkv_weight, "dp", axis=1, tiled=True),
        lax.all_gather(proj_weight, "dp", axis=1, tiled=True),
        lax.all_gather(fc1_weight, "dp", axis=0, tiled=True),
        lax.all_gather(fc2_weight, "dp", axis=1, tiled=True),
        lax.all_gather(qv_bias, "dp", axis=2, tiled=True),
        lax.all_gather(fc1_bias, "dp", axis=1, tiled=True),
    )
    vectors = (
        lax.all_gather(gain_rows, ("dp", "tensor"), axis=1, tiled=True),
        lax.all_gather(bias_rows, ("dp", "tensor"), axis=1, tiled=True),
    )
    return (matrices, (vectors[0].astype(jnp.float32), vectors[1].astype(jnp.float32)))


def spread_rows(local_rows):
    return lax.all_gather(local_rows, "tensor", axis=0, tiled=True)


def reduce_rows(term_fn, row_count):
    return lax.psum_scatter(
        term_fn(jnp.int32(0), lax.axis_size("tensor") * row_count),
        "tensor",
        scatter_dimension=0,
        tiled=True,
    )


def spread_grads(local_rows):
    return lax.all_gather(local_rows, "tensor", axis=0, tiled=True)


def reduce_grads(term_fn, row_count):
    return lax.psum_scatter(
        term_fn(jnp.int32(0), lax.axis_size("tensor") * row_count),
        "tensor",
        scatter_dimension=0,
        tiled=True,
    )


def forward(clip_rows, matrices, vectors):
    w_qkv, w_proj, w_fc1, w_fc2, b_qv, b_fc1 = matrices
    gain_rows, bias_rows = vectors
    row_count = clip_rows.shape[0]
    head_cols = w_qkv.shape[2]
    heads_here = head_cols // HD
    score_scale = 1.0 / math.sqrt(HD)
    inputs = clip_rows.astype(jnp.float32)
    normed_one, scaled_one, inverse_one = normalize(inputs, gain_rows[0], bias_rows[0])
    whole_one = spread_rows(normed_one.astype(jnp.bfloat16))
    seq_len = whole_one.shape[0]
    projected = jnp.einsum("sd,jde->jse", whole_one, w_qkv, preferred_element_type=jnp.float32)
    bias_cols = b_qv.reshape(2, head_cols).astype(jnp.float32)
    queries = (projected[0] + bias_cols[0]).astype(jnp.bfloat16).reshape(seq_len, heads_here, HD)
    keys_all = projected[1].astype(jnp.bfloat16).reshape(seq_len, heads_here, HD)
    values_all = (projected[2] + bias_cols[1]).astype(jnp.bfloat16).reshape(seq_len, heads_here, HD)
    scores = (
        jnp.einsum("qhd,khd->hqk", queries, keys_all, preferred_element_type=jnp.float32)
        * score_scale
    )
    top_score = jnp.max(scores, axis=2, keepdims=True)
    weights_exp = jnp.exp(scores - top_score)
    totals = jnp.sum(weights_exp, axis=2, keepdims=True)
    attn_probs = (weights_exp / totals).astype(jnp.bfloat16)
    log_total = top_score + jnp.log(totals)
    attended = (
        jnp.einsum("hqk,khd->qhd", attn_probs, values_all, preferred_element_type=jnp.float32)
        .reshape(seq_len, head_cols)
        .astype(jnp.bfloat16)
    )

    def proj_term(offset, length):
        return jnp.dot(attended, w_proj, preferred_element_type=jnp.float32)

    residual_one = inputs + (reduce_rows(proj_term, row_count) + bias_rows[2])
    normed_two, scaled_two, inverse_two = normalize(residual_one, gain_rows[1], bias_rows[1])
    whole_two = spread_rows(normed_two.astype(jnp.bfloat16))
    pre_act = jnp.dot(whole_two, w_fc1, preferred_element_type=jnp.float32) + b_fc1.reshape(
        -1
    ).astype(jnp.float32)
    hidden = gelu_value(pre_act).astype(jnp.bfloat16)

    def fc2_term(offset, length):
        return jnp.dot(hidden, w_fc2, preferred_element_type=jnp.float32)

    layer_out = residual_one + (reduce_rows(fc2_term, row_count) + bias_rows[3])
    stored = (
        scaled_one,
        inverse_one,
        whole_one,
        queries,
        keys_all,
        values_all,
        log_total,
        attended,
        scaled_two,
        inverse_two,
        whole_two,
        pre_act,
        hidden,
    )
    return (layer_out, stored)


def backward(upstream, matrices, vectors, stored):
    w_qkv, w_proj, w_fc1, w_fc2, b_qv, b_fc1 = matrices
    gain_rows, bias_rows = vectors
    (
        scaled_one,
        inverse_one,
        whole_one,
        queries,
        keys_all,
        values_all,
        log_total,
        attended,
        scaled_two,
        inverse_two,
        whole_two,
        pre_act,
        hidden,
    ) = stored
    row_count = upstream.shape[0]
    seq_len = queries.shape[0]
    heads_here = queries.shape[1]
    head_cols = heads_here * HD
    score_scale = 1.0 / math.sqrt(HD)
    grad_mlp = upstream.astype(jnp.bfloat16)
    grad_fc2_bias = jnp.sum(grad_mlp.astype(jnp.float32), axis=0)
    whole_mlp = spread_grads(grad_mlp)
    grad_fc2 = jnp.einsum("sf,sd->fd", hidden, whole_mlp, preferred_element_type=jnp.float32)
    grad_hidden = jnp.einsum("sd,fd->sf", whole_mlp, w_fc2, preferred_element_type=jnp.float32)
    grad_pre = (grad_hidden * gelu_slope(pre_act)).astype(jnp.bfloat16)
    grad_fc1_bias = jnp.sum(grad_pre.astype(jnp.float32), axis=0)
    grad_fc1 = jnp.einsum("sd,sf->df", whole_two, grad_pre, preferred_element_type=jnp.float32)

    def fc1_back(offset, length):
        return jnp.einsum("sf,df->sd", grad_pre, w_fc1, preferred_element_type=jnp.float32)

    grad_normed_two = reduce_grads(fc1_back, row_count)
    grad_residual = upstream + normalize_back(
        grad_normed_two, scaled_two, inverse_two, gain_rows[1]
    )
    grad_branch = grad_residual.astype(jnp.bfloat16)
    grad_proj_bias = jnp.sum(grad_branch.astype(jnp.float32), axis=0)
    whole_branch = spread_grads(grad_branch)
    grad_proj = jnp.einsum("se,sd->ed", attended, whole_branch, preferred_element_type=jnp.float32)
    grad_att = (
        jnp.einsum("sd,ed->se", whole_branch, w_proj, preferred_element_type=jnp.float32)
        .astype(jnp.bfloat16)
        .reshape(seq_len, heads_here, HD)
    )
    scores = (
        jnp.einsum("qhd,khd->hqk", queries, keys_all, preferred_element_type=jnp.float32)
        * score_scale
    )
    attn_probs = jnp.exp(scores - log_total)
    grad_probs = jnp.einsum(
        "qhd,khd->hqk", grad_att, values_all, preferred_element_type=jnp.float32
    )
    row_dot = jnp.sum(attn_probs * grad_probs, axis=2, keepdims=True)
    grad_scores = (attn_probs * (grad_probs - row_dot)).astype(jnp.bfloat16)
    grad_query = (
        jnp.einsum("hqk,khd->qhd", grad_scores, keys_all, preferred_element_type=jnp.float32)
        * score_scale
    ).astype(jnp.bfloat16)
    grad_key = (
        jnp.einsum("hqk,qhd->khd", grad_scores, queries, preferred_element_type=jnp.float32)
        * score_scale
    ).astype(jnp.bfloat16)
    grad_value = jnp.einsum(
        "hqk,qhd->khd",
        attn_probs.astype(jnp.bfloat16),
        grad_att,
        preferred_element_type=jnp.float32,
    ).astype(jnp.bfloat16)
    grad_qkv = jnp.stack([grad_query, grad_key, grad_value]).reshape(3, seq_len, head_cols)
    grad_qv = jnp.stack(
        [
            jnp.sum(grad_query.astype(jnp.float32), axis=0),
            jnp.sum(grad_value.astype(jnp.float32), axis=0),
        ]
    )
    grad_qkv_weight = jnp.einsum(
        "sd,jse->jde", whole_one, grad_qkv, preferred_element_type=jnp.float32
    )

    def qkv_back(offset, length):
        return jnp.einsum("jse,jde->sd", grad_qkv, w_qkv, preferred_element_type=jnp.float32)

    grad_normed_one = reduce_grads(qkv_back, row_count)
    grad_input = grad_residual + normalize_back(
        grad_normed_one, scaled_one, inverse_one, gain_rows[0]
    )
    grad_gain = jnp.stack(
        [
            jnp.sum(grad_normed_one * scaled_one, axis=0),
            jnp.sum(grad_normed_two * scaled_two, axis=0),
        ]
    )
    grad_bias = jnp.stack(
        [
            jnp.sum(grad_normed_one, axis=0),
            jnp.sum(grad_normed_two, axis=0),
            grad_proj_bias,
            grad_fc2_bias,
        ]
    )
    weight_part = (
        lax.psum_scatter(grad_qkv_weight, "dp", scatter_dimension=1, tiled=True),
        lax.psum_scatter(grad_proj, "dp", scatter_dimension=1, tiled=True),
        lax.psum_scatter(grad_fc1, "dp", scatter_dimension=0, tiled=True),
        lax.psum_scatter(grad_fc2, "dp", scatter_dimension=1, tiled=True),
        lax.psum_scatter(grad_qv, "dp", scatter_dimension=2, tiled=True),
        lax.psum_scatter(grad_fc1_bias.reshape(1, -1), "dp", scatter_dimension=1, tiled=True),
    )
    vector_part = (
        lax.psum_scatter(grad_gain, ("dp", "tensor"), scatter_dimension=1, tiled=True),
        lax.psum_scatter(grad_bias, ("dp", "tensor"), scatter_dimension=1, tiled=True),
    )
    return (grad_input, weight_part, vector_part)


def on_device(
    clip_rows,
    out_grad,
    clip_valid,
    gain_rows,
    bias_rows,
    qkv_weight,
    qv_bias,
    proj_weight,
    fc1_weight,
    fc1_bias,
    fc2_weight,
):
    clip_weight = clip_valid[0].astype(jnp.float32)
    upstream = out_grad.astype(jnp.float32) * clip_weight
    matrices, vectors = fetch(
        qkv_weight, proj_weight, fc1_weight, fc2_weight, qv_bias, fc1_bias, gain_rows, bias_rows
    )
    layer_out, stored = forward(clip_rows, matrices, vectors)
    matrices, vectors = fetch(
        qkv_weight, proj_weight, fc1_weight, fc2_weight, qv_bias, fc1_bias, gain_rows, bias_rows
    )
    unused_out, stored = forward(clip_rows, matrices, vectors)
    grad_input, weight_part, vector_part = backward(upstream, matrices, vectors, stored)
    return (
        (layer_out * clip_weight).astype(jnp.bfloat16),
        grad_input,
        vector_part[0],
        vector_part[1],
        weight_part[0],
        weight_part[4],
        weight_part[1],
        weight_part[2],
        weight_part[5],
        weight_part[3],
        vector_part[1][3],
    )


AXES = ("dp", "tensor")
Z_LOW, Z_HIGH, CORE, X, Y = 1, 2, 4, 8, 16
CHIP_MASKS = (0, X, Y, X | Y)
BF16, F32 = jnp.bfloat16, jnp.float32
NN, NT, TN = ((1,), (0,)), ((1,), (1,)), ((0,), (0,))
SHARE = 49
PAD = 56
CHIP_ID, CORE_ID, D_ID, T_ID = range(4)


def swap(value, mask):
    return lax.ppermute(value, AXES, [(i, i ^ mask) for i in range(32)])


def dot(left, right, dims):
    return lax.dot_general(left, right, (dims, ((), ())), preferred_element_type=F32)


def call(body, outs, scalars, *args, scratch=(), flops=0):
    moved = sum(math.prod(a.shape) * a.dtype.itemsize for a in args)
    moved += sum(math.prod(s) * jnp.dtype(t).itemsize for s, t in outs)
    held = sum(math.prod(s[:-1]) * max(s[-1], 128) * jnp.dtype(t).itemsize for s, t in scratch)
    return pl.pallas_call(
        body,
        out_shape=[jax.ShapeDtypeStruct(s, t) for s, t in outs],
        in_specs=[pl.BlockSpec(memory_space=pltpu.SMEM)]
        + [pl.BlockSpec(memory_space=pltpu.VMEM)] * len(args),
        out_specs=[pl.BlockSpec(memory_space=pltpu.VMEM)] * len(outs),
        scratch_shapes=[pltpu.VMEM(s, t) for s, t in scratch],
        compiler_params=pltpu.CompilerParams(vmem_limit_bytes=moved + held + (4 << 20)),
        cost_estimate=pl.CostEstimate(flops=flops, bytes_accessed=moved, transcendentals=0),
    )(scalars, *args)


def chip_lanes(ids, m):
    return pl.ds(pl.multiple_of((ids[CHIP_ID] ^ m) * 256, 256), 256)


def lanes(m):
    return slice(256 * m, 256 * m + 256)


def row_ids(shape):
    return lax.broadcasted_iota(jnp.int32, shape, 0)


def pick(condition, left, right):
    return jnp.where(jnp.full(left.shape, condition, jnp.int32) != 0, left, right)


def is_zero(number):
    return jnp.where(number == 0, 1, 0)


def z_low(ids):
    return ids[T_ID] & 1


def z_high(ids):
    return ids[T_ID] >> 1


def far_chips(ids, core_flip):
    return [(ids[CHIP_ID] ^ m) * 2 + (ids[CORE_ID] ^ core_flip) for m in range(4)]


def pack_kernel(ids, rows, grads, params, keep, send, wide, stage):
    lane32 = lax.broadcasted_iota(jnp.int32, (32, 128), 1)
    spot = (lane32 == row_ids((32, 128)) + 32 * ids[T_ID]).astype(F32).astype(BF16)
    lane8 = lax.broadcasted_iota(jnp.int32, (8, 128), 1)
    spot8 = (lane8 == row_ids((8, 128)) + 8 * ids[D_ID]).astype(F32).astype(BF16)
    placed = dot(params[0:8, 0:32], spot, NN)
    qv_rows = dot(params[8:16, 0:8], spot8, NN)
    row_a = jnp.concatenate(
        [placed[k : k + 1] for k in range(6)]
        + [params[...].astype(F32)[16:17], jnp.zeros((1, 128), F32)],
        axis=1,
    )
    row_b = jnp.concatenate([qv_rows[k : k + 1] for k in range(8)], axis=1)
    flag = jnp.full((PAD, 1024), ids[4], jnp.int32).astype(F32)
    row = row_ids((PAD, 1024))
    tail = jnp.where(row == SHARE, row_a, jnp.where(row == SHARE + 1, row_b, flag))
    wide[0 : rows.shape[0], :] = rows[...].astype(F32)
    for j in range(8):
        block = wide[SHARE * j : SHARE * j + PAD, :]
        stage[j, 0:PAD, :] = jnp.where(row < SHARE, block, tail).astype(BF16)
    wide[0 : rows.shape[0], :] = grads[...].astype(F32)
    for j in range(8):
        stage[j, PAD : 2 * PAD, :] = wide[SHARE * j : SHARE * j + PAD, :].astype(BF16)
    for m, (d0, d1) in enumerate(zip(far_chips(ids, 0), far_chips(ids, 1))):
        keep[m, :, :] = stage[d0, :, :]
        send[m, :, :] = stage[d1, :, :]


def pair_up_kernel(ids, keep, got, o1, o2, o3):
    for m, out in enumerate((o1, o2, o3)):
        out[0, :, :] = keep[m + 1, :, :]
        out[1, :, :] = got[m + 1, :, :]


def arrived(ids, keep, got, d1, d2, d3):
    parts = []
    for m, (a0, a1) in enumerate(zip(far_chips(ids, 0), far_chips(ids, 1))):
        first, second = ((keep, 0), (got, 0)) if m == 0 else (((d1, d2, d3)[m - 1], k) for k in range(2))
        parts += [(a0, *first), (a1, *second)]
    return parts


def pick_kernel(ids, keep, got, d1, d2, d3, here, there, here_grad, there_grad, slots):
    row8 = row_ids((8, 1024))
    row = row_ids((PAD, 1024))
    mine = jnp.zeros((PAD, 1024), F32)
    other, mine_grad, other_grad = mine, mine, mine
    params = jnp.zeros((8, 1024), F32)
    qv = jnp.zeros((1, 1024), F32)
    high = jnp.full((1, 1024), z_high(ids), jnp.int32).astype(F32)
    parts = arrived(ids, keep, got, d1, d2, d3)
    flags = [
        ref[k, PAD - 8 : PAD, :].astype(F32)[SHARE + 10 - PAD : SHARE + 11 - PAD]
        for _, ref, k in parts
    ]
    for i, (a, ref, k) in enumerate(parts):
        seen = jnp.zeros((1, 1024), F32)
        for (c, _, _), flag in zip(parts, flags):
            earlier = jnp.full((1, 1024), jnp.where(c < a, 1, 0), jnp.int32).astype(F32)
            seen = seen + flag * earlier
        block = ref[k, 0:PAD, :].astype(F32)
        grad = ref[k, PAD : 2 * PAD, :].astype(F32)
        is_mine = jnp.where(seen == high, flags[i], 0.0)
        is_other = flags[i] - is_mine
        mine = jnp.where(is_mine > 0.5, block, mine)
        other = jnp.where(is_other > 0.5, block, other)
        mine_grad = jnp.where(is_mine > 0.5, grad, mine_grad)
        other_grad = jnp.where(is_other > 0.5, grad, other_grad)
        params = jnp.where(row8 == a, block[SHARE : SHARE + 1], params)
        qv = qv + block[SHARE + 1 : SHARE + 2]
        slots[a, :, :] = jnp.broadcast_to(is_mine[:, 0:128], (8, 128))
        slots[8 + a, :, :] = jnp.broadcast_to(is_other[:, 0:128], (8, 128))
    for value, out in ((mine, here), (other, there)):
        out[0:PAD, :] = jnp.where(row == PAD - 1, qv, value).astype(BF16)
        out[PAD : PAD + 8, :] = params.astype(BF16)
    here_grad[...] = mine_grad.astype(BF16)
    there_grad[...] = other_grad.astype(BF16)


def lay_rows(ids, here, r1, r2, r3, wide):
    low = is_zero(z_low(ids))
    for m in range(4):
        cols = chip_lanes(ids, m)
        blocks = [ref[0:PAD, cols].astype(F32) for ref in (here, r1, r2, r3)]
        order = (
            pick(low, blocks[0], blocks[1]),
            pick(low, blocks[2], blocks[3]),
            pick(low, blocks[1], blocks[0]),
            pick(low, blocks[3], blocks[2]),
        )
        for i, block in enumerate(order):
            wide[SHARE * i : SHARE * i + SHARE, lanes(m)] = block[0:SHARE]


def norm_parts(values):
    centre = jnp.mean(values, axis=1, keepdims=True)
    offsets = values - centre
    inverse = lax.rsqrt(jnp.mean(offsets * offsets, axis=1, keepdims=True) + norm_eps)
    return offsets * inverse, inverse


def norm_one_kernel(ids, here, r1, r2, r3, rows, normed, vec, qv_bias, b_fc1, wide, small):
    lay_rows(ids, here, r1, r2, r3, wide)
    own = here[PAD - 8 : PAD + 8, :].astype(F32)
    far = r2[PAD - 8 : PAD + 8, :].astype(F32)
    tails = [own[8:], far[8:]] + [r[PAD : PAD + 8, :].astype(F32) for r in (r1, r3)]
    params = tails[0] + tails[1] + tails[2] + tails[3]
    small[...] = jnp.zeros_like(small)
    for d in range(8):
        for k in range(6):
            small[k : k + 1, 128 * d : 128 * d + 128] = params[
                d : d + 1, 128 * k : 128 * k + 128
            ]
    for m in range(4):
        vec[:, lanes(m)] = small[:, chip_lanes(ids, m)]
    home = pick(is_zero(ids[CORE_ID]), own, far)
    for k in range(8):
        qv_bias[k : k + 1, :] = home[7:8, 128 * k : 128 * k + 128]
        b_fc1[0:1, 128 * k : 128 * k + 128] = home[8 + k : 9 + k, 768:896]
    values = wide[...]
    scaled, _ = norm_parts(values)
    rows[...] = values.astype(BF16)
    normed[...] = (scaled * vec[0:1, :] + vec[2:3, :]).astype(BF16)


def lay_grad_kernel(ids, here, r1, r2, r3, out, wide):
    lay_rows(ids, here, r1, r2, r3, wide)
    out[...] = wide[...].astype(BF16)


def join_rows(wide, own, got):
    half = own.shape[0]
    wide[0:half, :] = own[...].astype(F32)
    wide[half : 2 * half, :] = got[...].astype(F32)


PROJ = 3


def qkv_kernel(ids, own, got, qv_bias, w0, w1, w2, w3, whole, o0, o1, o2, o3, wide, heads):
    weights = (w0, w1, w2, w3)
    join_rows(wide, own, got)
    whole[...] = wide[...].astype(BF16)
    for j in range(3):
        total = dot(whole[:, lanes(0)], w0[:, lanes(j)], NN)
        for m in range(1, 4):
            total = total + dot(whole[:, lanes(m)], weights[m][:, lanes(j)], NN)
        for h in range(4):
            part = total[:, 64 * h : 64 * h + 64]
            if j != 1:
                k = (j // 2) * 4 + h
                part = part + qv_bias[k : k + 1, 0:64]
            heads[h, :, 64 * j : 64 * j + 64] = part.astype(BF16)
    for m, out in enumerate((o0, o1, o2, o3)):
        out[...] = heads[ids[CHIP_ID] ^ m, :, :]


STEP = 224


def attention_kernel(ids, a0, a1, a2, a3, o0, o1, o2, o3, lse, stage, q, k, v):
    tokens = a0.shape[0]
    for m, part in enumerate((a0, a1, a2, a3)):
        stage[tokens * m : tokens * m + tokens, :] = part[...].astype(F32)
    q[...] = (stage[:, 0:64] * 0.125).astype(BF16)
    k[...] = stage[:, 64:128].astype(BF16)
    v[...] = stage[:, 128:192].astype(BF16)

    def body(i, carry):
        rows = pl.ds(pl.multiple_of(i * STEP, 32), STEP)
        scores = dot(q[rows, :], k[...], NT)
        top = jnp.max(scores, axis=1, keepdims=True)
        weights = jnp.exp(scores - top)
        total = jnp.sum(weights, axis=1, keepdims=True)
        mixed = dot(weights.astype(BF16), v[...], NN)
        stage[rows, 0:64] = mixed / total
        spread = jnp.broadcast_to(top + jnp.log(total), (STEP, 128))
        lse[i, :, :] = jnp.transpose(spread)[0:8, :]
        return carry

    lax.fori_loop(0, stage.shape[0] // STEP, body, 0)
    for m, out in enumerate((o0, o1, o2, o3)):
        out[...] = stage[tokens * m : tokens * m + tokens, 0:64].astype(BF16)


def attention_back_kernel(
    ids, a0, a1, a2, a3, g0, g1, g2, g3, lse, o0, o1, o2, o3, stage, q, k, v, g, grad_k, grad_v
):
    tokens = a0.shape[0]
    for m, part in enumerate((a0, a1, a2, a3)):
        stage[tokens * m : tokens * m + tokens, :] = part[...].astype(F32)
    q[...] = (stage[:, 0:64] * 0.125).astype(BF16)
    k[...] = stage[:, 64:128].astype(BF16)
    v[...] = stage[:, 128:192].astype(BF16)
    for m, part in enumerate((g0, g1, g2, g3)):
        stage[tokens * m : tokens * m + tokens, 0:64] = part[...].astype(F32)
    g[...] = stage[:, 0:64].astype(BF16)
    keys_t = jnp.transpose(k[...])
    grad_k[...] = jnp.zeros_like(grad_k)
    grad_v[...] = jnp.zeros_like(grad_v)

    def body(i, carry):
        rows = pl.ds(pl.multiple_of(i * STEP, 32), STEP)
        queries, grad = q[rows, :], g[rows, :]
        probs = jnp.exp(dot(k[...], queries, NT) - lse[i, 0:1, :])
        grad_probs = dot(v[...], grad, NT)
        row_dot = jnp.sum(probs * grad_probs, axis=0, keepdims=True)
        grad_scores = (probs * (grad_probs - row_dot)).astype(BF16)
        grad_v[...] += dot(probs.astype(BF16), grad, NN)
        grad_k[...] += dot(grad_scores, queries, NN)
        stage[rows, 0:64] = jnp.transpose(dot(keys_t, grad_scores, NN)) * 0.125
        return carry

    lax.fori_loop(0, stage.shape[0] // STEP, body, 0)
    for m, out in enumerate((o0, o1, o2, o3)):
        rows = slice(tokens * m, tokens * m + tokens)
        out[:, 0:64] = stage[rows, 0:64].astype(BF16)
        out[:, 64:128] = grad_k[rows, :].astype(BF16)
        out[:, 128:192] = grad_v[rows, :].astype(BF16)


def split_rows(total, keep, send, cols):
    half = keep.shape[0]
    keep[:, cols] = total[:half]
    send[:, cols] = total[half:].astype(BF16)


def proj_kernel(ids, a0, a1, a2, a3, w0, w1, w2, w3, joined, keep, send, heads):
    for m, part in enumerate((a0, a1, a2, a3)):
        heads[m, :, :] = part[...]
    for h in range(4):
        joined[:, 64 * h : 64 * h + 64] = heads[h ^ ids[CHIP_ID], :, :]
    for m in range(4):
        weight = (w0, w1, w2, w3)[m]
        split_rows(dot(joined[...], weight[:, lanes(PROJ)], NT), keep, send, lanes(m))


def pair_kernel(ids, keep, got, part, send):
    total = keep[...] + got[...].astype(F32)
    part[...] = total
    send[...] = total.astype(BF16)


def half_kernel(ids, keep, got, part, send):
    own = part.shape[0]
    total = keep[...] + got[...].astype(F32)
    low = is_zero(z_low(ids))
    part[...] = pick(low, total[:own], total[own:])
    send[...] = pick(low, total[own:], total[:own]).astype(BF16)


def norm_two_kernel(ids, rows, part, got, vec, residual, normed):
    total = rows[...].astype(F32) + (part[...] + got[...].astype(F32) + vec[4:5, :])
    residual[...] = total
    scaled, _ = norm_parts(total)
    normed[...] = (scaled * vec[1:2, :] + vec[3:4, :]).astype(BF16)


def grad_hidden_kernel(ids, own, got, w0, w1, w2, w3, whole, out, wide):
    join_rows(wide, own, got)
    whole[...] = wide[...].astype(BF16)
    for c in range(4):
        total = dot(whole[:, lanes(0)], w0[:, lanes(c)], NN)
        for m, weight in enumerate((w1, w2, w3)):
            total = total + dot(whole[:, lanes(m + 1)], weight[:, lanes(c)], NN)
        out[:, lanes(c)] = total


def fc_kernel(
    ids, own, got, grad_hidden, b_fc1, w0, w1, w2, w3, whole, hidden, grad_pre, sums, keep, send, wide
):
    weights = (w0, w1, w2, w3)
    join_rows(wide, own, got)
    whole[...] = wide[...].astype(BF16)
    wide[...] = jnp.zeros_like(wide)

    def body(c, carry):
        cols = pl.ds(pl.multiple_of(c * 256, 256), 256)
        pre = b_fc1[:, cols] + dot(whole[:, lanes(0)], w0[:, cols], NN)
        for m in range(1, 4):
            pre = pre + dot(whole[:, lanes(m)], weights[m][:, cols], NN)
        half_erf = 0.5 * (1.0 + lax.erf(pre * root_half))
        hidden[:, cols] = (pre * half_erf).astype(BF16)
        slope = half_erf + pre * jnp.exp(-0.5 * pre * pre) * inv_root_tau
        grad = (grad_hidden[:, cols] * slope).astype(BF16)
        grad_pre[:, cols] = grad
        sums[:, cols] = jnp.sum(grad.astype(F32), axis=0, keepdims=True)
        for m in range(4):
            wide[:, lanes(m)] += dot(grad, weights[m][:, cols], NT)
        return carry

    lax.fori_loop(0, 4, body, 0)
    for m in range(4):
        split_rows(wide[:, lanes(m)], keep, send, lanes(m))


def norm_back(total, scaled, inverse, gain):
    hat = total * gain
    return (
        hat
        - jnp.mean(hat, axis=1, keepdims=True)
        - scaled * jnp.mean(hat * scaled, axis=1, keepdims=True)
    ) * inverse


def norm_two_back_kernel(ids, residual, part, got, grads, vec, grad_residual, grad_branch, sums):
    scaled, inverse = norm_parts(residual[...])
    total = part[...] + got[...].astype(F32)
    upstream = grads[...].astype(F32)
    result = upstream + norm_back(total, scaled, inverse, vec[1:2, :])
    branch = result.astype(BF16)
    grad_residual[...] = result
    grad_branch[...] = branch
    own = total.shape[0] // 2
    row = row_ids(total.shape)
    low = jnp.full(total.shape, z_low(ids), jnp.int32)
    mine = jnp.where(row < own, 1 - low, low) != 0

    def column_sum(value):
        return jnp.sum(jnp.where(mine, value, 0.0), axis=0, keepdims=True)

    sums[0:1, :] = column_sum(total * scaled)
    sums[1:2, :] = column_sum(total)
    sums[2:3, :] = column_sum(branch.astype(F32))
    sums[3:4, :] = column_sum(upstream)
    sums[4:8, :] = jnp.zeros((4, sums.shape[1]), F32)


def grad_att_kernel(ids, own, got, w0, w1, w2, w3, whole, o0, o1, o2, o3, wide, heads):
    join_rows(wide, own, got)
    whole[...] = wide[...].astype(BF16)
    weights = (w0, w1, w2, w3)
    total = dot(whole[:, lanes(0)], w0[:, lanes(PROJ)], NN)
    for m in range(1, 4):
        total = total + dot(whole[:, lanes(m)], weights[m][:, lanes(PROJ)], NN)
    for h in range(4):
        heads[h, :, :] = total[:, 64 * h : 64 * h + 64].astype(BF16)
    for m, out in enumerate((o0, o1, o2, o3)):
        out[...] = heads[ids[CHIP_ID] ^ m, :, :]


def qkv_back_kernel(ids, g0, g1, g2, g3, w0, w1, w2, w3, joined, keep, send, sums, heads):
    for m, part in enumerate((g0, g1, g2, g3)):
        heads[m, :, :] = part[...]
    for h in range(4):
        part = heads[h ^ ids[CHIP_ID], :, :]
        for j in range(3):
            piece = part[:, 64 * j : 64 * j + 64]
            joined[:, 256 * j + 64 * h : 256 * j + 64 * h + 64] = piece
            if j != 1:
                k = (j // 2) * 4 + h
                total = jnp.sum(piece.astype(F32), axis=0, keepdims=True)
                sums[0:1, 128 * k : 128 * k + 128] = jnp.concatenate(
                    [total, jnp.zeros((1, 64), F32)], axis=1
                )
    for m in range(4):
        weight = (w0, w1, w2, w3)[m]
        total = dot(joined[...], weight[:, 0:768], NT)
        split_rows(total, keep, send, lanes(m))


def to_owners(ids, value, wide, here, there):
    wide[0 : 2 * SHARE, :] = value
    wide[2 * SHARE :, :] = jnp.zeros((wide.shape[0] - 2 * SHARE, wide.shape[1]), F32)
    for m in range(4):
        cols = chip_lanes(ids, m)
        here[0:PAD, cols] = wide[0:PAD, lanes(m)].astype(BF16)
        there[0:PAD, cols] = wide[SHARE : SHARE + PAD, lanes(m)].astype(BF16)


def own_half(ids, ref):
    own = ref.shape[0] // 2
    value = ref[...].astype(F32)
    return pick(is_zero(z_low(ids)), value[:own], value[own:])


def norm_one_back_kernel(
    ids, rows, part, got, grad_residual, vec, sums_two, sums_fc1, sums_qv, here, there, small_out, wide
):
    scaled, inverse = norm_parts(own_half(ids, rows))
    total = part[...] + got[...].astype(F32)
    result = own_half(ids, grad_residual) + norm_back(total, scaled, inverse, vec[0:1, :])
    to_owners(ids, result, wide, here, there)
    small = jnp.concatenate(
        [
            jnp.sum(total * scaled, axis=0, keepdims=True),
            sums_two[0:1, :],
            jnp.sum(total, axis=0, keepdims=True),
            sums_two[1:4, :],
            sums_qv[...],
            sums_fc1[...],
        ],
        axis=0,
    )
    small_out[...] = small.astype(BF16)
    here[PAD : PAD + 8, :] = small.astype(BF16)
    there[PAD : PAD + 8, :] = small.astype(BF16)


def layer_out_kernel(ids, residual, part, got, vec, here, there, wide):
    result = own_half(ids, residual) + (part[...] + got[...].astype(F32) + vec[5:6, :])
    to_owners(ids, result, wide, here, there)


def fc2_kernel(ids, hidden, w0, w1, w2, w3, keep, send):
    for m, weight in enumerate((w0, w1, w2, w3)):
        split_rows(dot(hidden[...], weight[...], NT), keep, send, lanes(m))


def for_slot(slots, d, left, right):
    value = jnp.where(slots[8 + d, 0:1, 0:1] > 0.5, right, 0.0)
    return jnp.where(slots[d, 0:1, 0:1] > 0.5, left, value)


def give_kernel(ids, slots, here, away, keep, send):
    left = here[0:PAD, :].astype(F32)
    right = away[0:PAD, :].astype(F32)
    for out, flip in ((keep, 0), (send, 1)):
        for m, d in enumerate(far_chips(ids, flip)):
            out[m, :, :] = for_slot(slots, d, left, right).astype(BF16)


def give_grad_kernel(ids, slots, here, s1, away, s3, keep, send, rel, flat, tail):
    left = here[0:PAD, :].astype(F32)
    right = away[0:PAD, :].astype(F32)
    own = here[PAD : PAD + 8, :].astype(F32)
    far = away[PAD : PAD + 8, :].astype(F32)
    rel[...] = own + far + s1[...].astype(F32) + s3[...].astype(F32)
    home = pick(is_zero(ids[CORE_ID]), own, far)
    for m in range(4):
        flat[:, chip_lanes(ids, m)] = rel[:, lanes(m)]
    rel[0:1, :] = home[7:8]
    tail[...] = jnp.zeros_like(tail)
    for k in range(8):
        row, lane = (SHARE + k, 128) if k < 7 else (SHARE, 256)
        tail[row : row + 1, lane : lane + 128] = home[6:7, 128 * k : 128 * k + 128]
    row = row_ids((PAD, 1024))
    for out, flip in ((keep, 0), (send, 1)):
        for m, d in enumerate(far_chips(ids, flip)):
            cols = pl.ds(pl.multiple_of(d * 128, 128), 128)
            tail[SHARE : SHARE + 6, 0:128] = flat[0:6, cols]
            tail[SHARE + 6 : PAD, 0:128] = rel[0:1, cols]
            value = for_slot(slots, d, left, right)
            out[m, :, :] = jnp.where(row < SHARE, value, tail[...]).astype(BF16)


def settle_rows(parts, stage, out):
    for a, ref, k in parts:
        stage[a, :, :] = ref[k, :, :].astype(F32)
    for j in range(8):
        out[SHARE * j : SHARE * j + SHARE, :] = stage[j, 0:SHARE, :]


def take_kernel(ids, keep, got, d1, d2, d3, out, stage, wide):
    settle_rows(arrived(ids, keep, got, d1, d2, d3), stage, wide)
    out[...] = wide[...].astype(out.dtype)


def take_grad_kernel(
    ids, keep, got, d1, d2, d3, out, gains, biases, last, qv, b_fc1, stage
):
    parts = arrived(ids, keep, got, d1, d2, d3)
    settle_rows(parts, stage, out)
    total = jnp.zeros((8, 384), F32)
    for _, ref, k in parts:
        total = total + ref[k, PAD - 8 : PAD, 0:384].astype(F32)
    rows = pltpu.roll(total[:, 0:128], (128 - 32 * ids[T_ID]) & 127, 1)
    gains[...] = rows[1:3, 0:32]
    biases[...] = rows[3:7, 0:32]
    last[...] = rows[6:7, 0:32]
    b_fc1[...] = total[7:8, 0:128]
    parts = jnp.concatenate([total[1:8, 128:256], total[1:2, 256:384]], axis=0)
    qv[...] = pltpu.roll(parts, (128 - 8 * ids[D_ID]) & 127, 1)[:, 0:8]


def shards_kernel(ids, qkv, proj, fc2, first, second):
    for j in range(3):
        first[:, lanes(j)] = qkv[j, :, :]
    first[:, lanes(PROJ)] = jnp.transpose(proj[...])
    second[...] = jnp.transpose(fc2[...])


def offer_kernel(ids, own, far, send):
    @pl.when(ids[CORE_ID] == 0)
    def _():
        send[...] = far[...]

    @pl.when(ids[CORE_ID] != 0)
    def _():
        send[...] = own[...]


def merge_kernel(ids, own, far, got, out):
    half = own.shape[0]

    @pl.when(ids[CORE_ID] == 0)
    def _():
        out[0:half, :] = own[...]
        out[half:, :] = got[...]

    @pl.when(ids[CORE_ID] != 0)
    def _():
        out[0:half, :] = got[...]
        out[half:, :] = far[...]


X_FIRST, Y_FIRST = (1, 2), (2, 1)


def blocks_of(order, left, right, cols, send, here, there, out_cols):
    near, far = order
    for slot, m in ((0, near), (1, 3)):
        send[slot, :, out_cols] = dot(left[:, lanes(m)], right[:, cols], TN).astype(BF16)
    here[:, out_cols] = dot(left[:, lanes(0)], right[:, cols], TN)
    there[:, out_cols] = dot(left[:, lanes(far)], right[:, cols], TN)


def grads_fc1_kernel(ids, left, right, send, here, there):
    for c in range(2):
        cols = slice(512 * c, 512 * c + 512)
        blocks_of(X_FIRST, left, right, cols, send, here, there, cols)


def grads_fc2_kernel(ids, left, right, send, here, there):
    for c in range(2):
        cols = slice(512 * c, 512 * c + 512)
        blocks_of(Y_FIRST, left, right, cols, send, here, there, cols)


def grads_att_kernel(
    ids, rows, joined, branch, mixed, send_x, here_x, there_x, send_y, here_y, there_y
):
    blocks_of(X_FIRST, rows, joined, slice(0, 512), send_x, here_x, there_x, slice(0, 512))
    blocks_of(Y_FIRST, rows, joined, slice(512, 768), send_y, here_y, there_y, slice(0, 256))
    blocks_of(Y_FIRST, branch, mixed, slice(0, 256), send_y, here_y, there_y, slice(256, 512))


def fold_kernel(ids, here, there, got, other, whole):
    other[...] = (there[...] + got[1, :, :].astype(F32)).astype(BF16)
    whole[...] = here[...] + got[0, :, :].astype(F32)


def gather_kernel(ids, whole_x, got_x, whole_y, got_y, part, send):
    for k, (whole, got) in enumerate(((whole_x, got_x), (whole_y, got_y))):
        total = whole[...] + got[...].astype(F32)
        part[k, :, :] = total
        send[k, :, :] = total.astype(BF16)


def divide_kernel(ids, part, moved, keep, send):
    @pl.when(ids[CORE_ID] == 0)
    def _():
        keep[...] = part[:, 0:128, :]
        send[...] = part[:, 128:256, :].astype(BF16)

    @pl.when(ids[CORE_ID] != 0)
    def _():
        keep[...] = moved[:, 128:256, :].astype(F32)
        send[...] = moved[:, 0:128, :]


def finish_mlp_kernel(ids, keep, got, fc1, fc2):
    fc1[...] = keep[0, :, :] + got[0, :, :].astype(F32)
    fc2[...] = jnp.transpose(keep[1, :, :] + got[1, :, :].astype(F32))


def finish_att_kernel(ids, keep, got, qkv, proj):
    first = keep[0, :, :] + got[0, :, :].astype(F32)
    second = keep[1, :, :] + got[1, :, :].astype(F32)
    qkv[0, :, :] = first[:, 0:256]
    qkv[1, :, :] = first[:, 256:512]
    qkv[2, :, :] = second[:, 0:256]
    proj[...] = jnp.transpose(second[:, 256:512])


def tie(*values):
    return lax.optimization_barrier(values)


def sum_second(ids, first, second):
    n = first[1].shape[1]
    outs = [((256, n), BF16), ((256, n), F32)]
    other_x, whole_x = call(fold_kernel, outs, ids, *first)
    other_y, whole_y = call(fold_kernel, outs, ids, *second)
    return whole_x, swap(other_x, Y), whole_y, swap(other_y, X)


def sum_third(ids, parts):
    n = parts[0].shape[1]
    part, send = call(
        gather_kernel, [((2, 256, n), F32), ((2, 256, n), BF16)], ids, *parts
    )
    pairs = [(i, i ^ Z_HIGH) for i in range(32) if i & CORE]
    return part, lax.ppermute(send, AXES, pairs)


def sum_last(ids, body, outs, part, moved):
    n = part.shape[2]
    keep, send = call(
        divide_kernel, [((2, 128, n), F32), ((2, 128, n), BF16)], ids, part, moved
    )
    return call(body, outs, ids, keep, swap(send, CORE))


def on_device_spread(
    clip_rows,
    out_grad,
    clip_valid,
    gain_rows,
    bias_rows,
    qkv_weight,
    qv_bias,
    proj_weight,
    fc1_weight,
    fc1_bias,
    fc2_weight,
):
    d, t = lax.axis_index("dp"), lax.axis_index("tensor")
    core = d & 1
    ids = jnp.stack([d >> 1, core, d, t, clip_valid[0]]).astype(jnp.int32)
    count = clip_rows.shape[0]
    half, own = count // 2, count // 4
    behind = (PAD + 8, 1024)
    plain = (PAD, 1024)
    wide = ((count, 1024), F32)

    def to_devices(keep, send):
        got = swap(send, CORE)
        shape = (2, *keep.shape[1:])
        outs = call(pair_up_kernel, [(shape, BF16)] * 3, ids, keep, got)
        return keep, got, *(swap(outs[m], CHIP_MASKS[m + 1]) for m in range(3))

    def offer(shard, far):
        (send,) = call(offer_kernel, [(shard.shape, BF16)], ids, shard, far)
        return send

    def merge(shard, far, send):
        (out,) = call(
            merge_kernel, [((256, shard.shape[1]), BF16)], ids, shard, far, swap(send, CORE)
        )
        return out

    def trade(parts):
        return [parts[0]] + [swap(parts[m], CHIP_MASKS[m]) for m in range(1, 4)]

    params = jnp.concatenate(
        [
            jnp.pad(v, ((0, n - v.shape[0]), (0, 128 - v.shape[1])))
            for v, n in (
                (jnp.concatenate([gain_rows, bias_rows]), 8),
                (qv_bias.reshape(8, 8), 8),
                (fc1_bias, 8),
            )
        ]
    )
    shard_a, shard_g = call(
        shards_kernel,
        [((128, 1024), BF16), ((128, 1024), BF16)],
        ids,
        qkv_weight,
        proj_weight,
        fc2_weight,
    )
    far_a = swap(shard_a, Z_HIGH)
    keep, send = call(
        pack_kernel,
        [((4, 2 * PAD, 1024), BF16)] * 2,
        ids,
        clip_rows,
        out_grad,
        params,
        scratch=[((400, 1024), F32), ((8, 2 * PAD, 1024), BF16)],
    )
    *parts, far_a = tie(*to_devices(keep, send), far_a)
    here, there, here_grad, there_grad, slots = call(
        pick_kernel,
        [(behind, BF16), (behind, BF16), (plain, BF16), (plain, BF16), ((16, 8, 128), F32)],
        ids,
        *parts,
    )
    r1, r2, r3 = swap(here, Z_LOW), swap(there, Z_HIGH), swap(there, Z_LOW | Z_HIGH)
    far_a, shard_a, _ = tie(far_a, shard_a, here)
    w0 = merge(shard_a, far_a, offer(shard_a, far_a))
    w_att = (w0, swap(w0, X), swap(w0, Y), swap(w0, X | Y))
    r1, r2, r3, shard_f = tie(r1, r2, r3, fc1_weight)
    far_f = swap(shard_f, Z_HIGH)
    rows, normed, vec, qkv_bias, b_fc1 = call(
        norm_one_kernel,
        [
            ((half, 1024), BF16),
            ((half, 1024), BF16),
            ((8, 1024), F32),
            ((8, 128), F32),
            ((1, 1024), F32),
        ],
        ids,
        here,
        r1,
        r2,
        r3,
        scratch=[((half, 1024), F32), ((8, 1024), F32)],
    )

    whole_one, *qkv = call(
        qkv_kernel,
        [((count, 1024), BF16)] + [((count, 192), BF16)] * 4,
        ids,
        normed,
        swap(normed, CORE),
        qkv_bias,
        *w_att,
        scratch=[wide, ((4, count, 192), BF16)],
        flops=2 * count * 1024 * 768,
    )
    shard_g, *qkv = tie(shard_g, *qkv)
    far_g = swap(shard_g, Z_HIGH)
    *qkv, f0 = tie(*trade(qkv), merge(shard_f, far_f, offer(shard_f, far_f)))
    f1, f2 = swap(f0, X), swap(f0, Y)
    tokens = 4 * count
    *mixed, lse = call(
        attention_kernel,
        [((count, 64), BF16)] * 4 + [((tokens // STEP, 8, STEP), F32)],
        ids,
        *qkv,
        scratch=[((tokens, 192), F32)] + [((tokens, 64), BF16)] * 3,
        flops=4 * tokens * tokens * 64,
    )
    here_grad, there_grad, *mixed = tie(here_grad, there_grad, *mixed)
    s1, s2, s3 = (
        swap(here_grad, Z_LOW),
        swap(there_grad, Z_HIGH),
        swap(there_grad, Z_LOW | Z_HIGH),
    )
    *mixed, f1, f2, g0 = tie(*trade(mixed), f1, f2, merge(shard_g, far_g, offer(shard_g, far_g)))
    w_fc1 = (f0, f1, f2, swap(f2, X))
    g1, g2 = swap(g0, X), swap(g0, Y)
    attended, keep, send = call(
        proj_kernel,
        [((count, 256), BF16), ((half, 1024), F32), ((half, 1024), BF16)],
        ids,
        *mixed,
        *w_att,
        scratch=[((4, count, 64), BF16)],
        flops=2 * count * 1024 * 256,
    )

    def pair(keep, send):
        return call(
            pair_kernel, [((half, 1024), F32), ((half, 1024), BF16)], ids, keep, swap(send, CORE)
        )

    def halve(keep, send):
        return call(
            half_kernel, [((own, 1024), F32), ((own, 1024), BF16)], ids, keep, swap(send, CORE)
        )

    part, send = pair(keep, send)
    (grads,) = call(
        lay_grad_kernel,
        [((half, 1024), BF16)],
        ids,
        here_grad,
        s1,
        s2,
        s3,
        scratch=[((half, 1024), F32)],
    )
    residual, normed_two = call(
        norm_two_kernel,
        [((half, 1024), F32), ((half, 1024), BF16)],
        ids,
        rows,
        part,
        swap(send, Z_LOW),
        vec,
    )
    w_fc2 = (g0, g1, g2, swap(g1, Y))
    whole_mlp, grad_hidden = call(
        grad_hidden_kernel,
        [((count, 1024), BF16), ((count, 1024), F32)],
        ids,
        grads,
        swap(grads, CORE),
        *w_fc2,
        scratch=[wide],
        flops=2 * count * 1024 * 1024,
    )

    whole_two, hidden, grad_pre, sums_fc1, keep, send = call(
        fc_kernel,
        [((count, 1024), BF16)] * 3
        + [((1, 1024), F32), ((half, 1024), F32), ((half, 1024), BF16)],
        ids,
        normed_two,
        swap(normed_two, CORE),
        grad_hidden,
        b_fc1,
        *w_fc1,
        scratch=[wide],
        flops=4 * count * 1024 * 1024,
    )
    part, send = pair(keep, send)
    late = tie(send, whole_mlp, hidden, whole_two, grad_pre)
    grad_outs = [((2, 256, 1024), BF16), ((256, 1024), F32), ((256, 1024), F32)]
    cost = 2 * count * 1024 * 1024
    send_f, *rest_f = call(grads_fc1_kernel, grad_outs, ids, late[3], late[4], flops=cost)
    send_g, *rest_g = call(grads_fc2_kernel, grad_outs, ids, late[1], late[2], flops=cost)
    sums_f = (*rest_f, swap(send_f, X))
    sums_g = (*rest_g, swap(send_g, Y))
    keep_out, send_out = call(
        fc2_kernel,
        [((half, 1024), F32), ((half, 1024), BF16)],
        ids,
        late[2],
        *w_fc2,
        flops=cost,
    )
    away, keep_out, send_out = tie(swap(send, Z_LOW), keep_out, send_out)
    grad_residual, grad_branch, sums_two = call(
        norm_two_back_kernel,
        [((half, 1024), F32), ((half, 1024), BF16), ((8, 1024), F32)],
        ids,
        residual,
        part,
        away,
        grads,
        vec,
    )

    whole_branch, *grad_att = call(
        grad_att_kernel,
        [((count, 1024), BF16)] + [((count, 64), BF16)] * 4,
        ids,
        grad_branch,
        swap(grad_branch, CORE),
        *w_att,
        scratch=[wide, ((4, count, 64), BF16)],
        flops=2 * count * 1024 * 256,
    )
    *grad_att, keep_out, send_out = tie(*grad_att, keep_out, send_out)
    part_out, send_out = halve(keep_out, send_out)
    here_out, there_out = call(
        layer_out_kernel,
        [(plain, BF16)] * 2,
        ids,
        residual,
        part_out,
        swap(send_out, Z_LOW),
        vec,
        scratch=[((2 * PAD, 1024), F32)],
    )
    grad_qkv = call(
        attention_back_kernel,
        [((count, 192), BF16)] * 4,
        ids,
        *qkv,
        *trade(grad_att),
        lse,
        scratch=[((tokens, 192), F32)] + [((tokens, 64), BF16)] * 4 + [((tokens, 64), F32)] * 2,
        flops=10 * tokens * tokens * 64,
    )
    joined, keep, send, sums_qv = call(
        qkv_back_kernel,
        [((count, 768), BF16), ((half, 1024), F32), ((half, 1024), BF16), ((1, 1024), F32)],
        ids,
        *trade(grad_qkv),
        *w_att,
        scratch=[((4, count, 192), BF16)],
        flops=2 * count * 1024 * 768,
    )
    part, send = halve(keep, send)
    late = tie(send, whole_one, joined, whole_branch, attended)
    grad_outs = [((2, 256, 512), BF16), ((256, 512), F32), ((256, 512), F32)]
    send_x, here_x, there_x, send_y, here_y, there_y = call(
        grads_att_kernel, grad_outs * 2, ids, *late[1:], flops=cost
    )
    here, there, small = call(
        norm_one_back_kernel,
        [(behind, BF16), (behind, BF16), ((8, 1024), BF16)],
        ids,
        rows,
        part,
        swap(send, Z_LOW),
        grad_residual,
        vec,
        sums_two,
        sums_fc1,
        sums_qv,
        scratch=[((2 * PAD, 1024), F32)],
    )
    keep, send = call(
        give_grad_kernel,
        [((4, PAD, 1024), BF16)] * 2,
        ids,
        slots,
        here,
        swap(small, Z_LOW),
        swap(there, Z_HIGH),
        swap(small, Z_LOW | Z_HIGH),
        scratch=[((8, 1024), F32), ((8, 1024), F32), (plain, F32)],
    )
    input_grad, grad_gains, grad_biases, grad_last, grad_qv, grad_b_fc1 = call(
        take_grad_kernel,
        [
            ((count, 1024), F32),
            ((2, 32), F32),
            ((4, 32), F32),
            ((1, 32), F32),
            ((8, 8), F32),
            ((1, 128), F32),
        ],
        ids,
        *to_devices(keep, send),
        scratch=[((8, PAD, 1024), F32)],
    )

    keep, send = call(
        give_kernel,
        [((4, PAD, 1024), BF16)] * 2,
        ids,
        slots,
        here_out,
        swap(there_out, Z_HIGH),
    )
    (layer_out,) = call(
        take_kernel,
        [((count, 1024), BF16)],
        ids,
        *to_devices(keep, send),
        scratch=[((8, PAD, 1024), F32), wide],
    )

    grad_fc1, grad_fc2 = sum_last(
        ids,
        finish_mlp_kernel,
        [((128, 1024), F32), ((1024, 128), F32)],
        *sum_third(ids, sum_second(ids, sums_f, sums_g)),
    )
    grad_w, grad_proj = sum_last(
        ids,
        finish_att_kernel,
        [((3, 128, 256), F32), ((256, 128), F32)],
        *sum_third(
            ids,
            sum_second(
                ids, (here_x, there_x, swap(send_x, X)), (here_y, there_y, swap(send_y, Y))
            ),
        ),
    )
    return (
        layer_out,
        input_grad,
        grad_gains,
        grad_biases,
        grad_w,
        grad_qv.reshape(2, 4, 8),
        grad_proj,
        grad_fc1,
        grad_b_fc1,
        grad_fc2,
        grad_last[0],
    )


def solution(mesh):
    spread = (mesh.shape["dp"], mesh.shape["tensor"]) == (8, 4)
    in_specs = (
        P(("dp", "tensor"), None),
        P(("dp", "tensor"), None),
        P("dp"),
        P(None, ("dp", "tensor")),
        P(None, ("dp", "tensor")),
        P(None, "dp", "tensor"),
        P(None, "tensor", "dp"),
        P("tensor", "dp"),
        P("dp", "tensor"),
        P("tensor", "dp"),
        P("tensor", "dp"),
    )
    out_specs = (
        P(("dp", "tensor"), None),
        P(("dp", "tensor"), None),
        P(None, ("dp", "tensor")),
        P(None, ("dp", "tensor")),
        P(None, "dp", "tensor"),
        P(None, "tensor", "dp"),
        P("tensor", "dp"),
        P("dp", "tensor"),
        P("tensor", "dp"),
        P("tensor", "dp"),
        P(("dp", "tensor")),
    )
    return jax.shard_map(
        on_device_spread if spread else on_device, mesh=mesh, in_specs=in_specs, out_specs=out_specs, check_vma=False
    )
```

```python
import math

import jax
import jax.numpy as jnp
from jax import lax
from jax.experimental import pallas as pl
from jax.experimental.pallas import tpu as pltpu
from jax.sharding import PartitionSpec as P

HD = 64


norm_eps = 1e-06
root_half = 0.7071067811865476
inv_root_tau = 0.3989422804014327


def normalize(values, gain_row, shift_row):
    centre = jnp.mean(values, axis=1, keepdims=True)
    offsets = values - centre
    inverse = lax.rsqrt(jnp.mean(offsets * offsets, axis=1, keepdims=True) + norm_eps)
    scaled = offsets * inverse
    return (scaled * gain_row + shift_row, scaled, inverse)


def normalize_back(upstream, scaled, inverse, gain_row):
    grad_hat = upstream * gain_row
    return (
        grad_hat
        - jnp.mean(grad_hat, axis=1, keepdims=True)
        - scaled * jnp.mean(grad_hat * scaled, axis=1, keepdims=True)
    ) * inverse


def gelu_value(inputs):
    return 0.5 * inputs * (1.0 + lax.erf(inputs * root_half))


def gelu_slope(inputs):
    return (
        0.5 * (1.0 + lax.erf(inputs * root_half))
        + inputs * jnp.exp(-0.5 * inputs * inputs) * inv_root_tau
    )


def fetch(qkv_weight, proj_weight, fc1_weight, fc2_weight, qv_bias, fc1_bias, gain_rows, bias_rows):
    matrices = (
        lax.all_gather(qkv_weight, "dp", axis=1, tiled=True),
        lax.all_gather(proj_weight, "dp", axis=1, tiled=True),
        lax.all_gather(fc1_weight, "dp", axis=0, tiled=True),
        lax.all_gather(fc2_weight, "dp", axis=1, tiled=True),
        lax.all_gather(qv_bias, "dp", axis=2, tiled=True),
        lax.all_gather(fc1_bias, "dp", axis=1, tiled=True),
    )
    vectors = (
        lax.all_gather(gain_rows, ("dp", "tensor"), axis=1, tiled=True),
        lax.all_gather(bias_rows, ("dp", "tensor"), axis=1, tiled=True),
    )
    return (matrices, (vectors[0].astype(jnp.float32), vectors[1].astype(jnp.float32)))


def spread_rows(local_rows):
    return lax.all_gather(local_rows, "tensor", axis=0, tiled=True)


def reduce_rows(term_fn, row_count):
    return lax.psum_scatter(
        term_fn(jnp.int32(0), lax.axis_size("tensor") * row_count),
        "tensor",
        scatter_dimension=0,
        tiled=True,
    )


def spread_grads(local_rows):
    return lax.all_gather(local_rows, "tensor", axis=0, tiled=True)


def reduce_grads(term_fn, row_count):
    return lax.psum_scatter(
        term_fn(jnp.int32(0), lax.axis_size("tensor") * row_count),
        "tensor",
        scatter_dimension=0,
        tiled=True,
    )


def forward(clip_rows, matrices, vectors):
    w_qkv, w_proj, w_fc1, w_fc2, b_qv, b_fc1 = matrices
    gain_rows, bias_rows = vectors
    row_count = clip_rows.shape[0]
    head_cols = w_qkv.shape[2]
    heads_here = head_cols // HD
    score_scale = 1.0 / math.sqrt(HD)
    inputs = clip_rows.astype(jnp.float32)
    normed_one, scaled_one, inverse_one = normalize(inputs, gain_rows[0], bias_rows[0])
    whole_one = spread_rows(normed_one.astype(jnp.bfloat16))
    seq_len = whole_one.shape[0]
    projected = jnp.einsum("sd,jde->jse", whole_one, w_qkv, preferred_element_type=jnp.float32)
    bias_cols = b_qv.reshape(2, head_cols).astype(jnp.float32)
    queries = (projected[0] + bias_cols[0]).astype(jnp.bfloat16).reshape(seq_len, heads_here, HD)
    keys_all = projected[1].astype(jnp.bfloat16).reshape(seq_len, heads_here, HD)
    values_all = (projected[2] + bias_cols[1]).astype(jnp.bfloat16).reshape(seq_len, heads_here, HD)
    scores = (
        jnp.einsum("qhd,khd->hqk", queries, keys_all, preferred_element_type=jnp.float32)
        * score_scale
    )
    top_score = jnp.max(scores, axis=2, keepdims=True)
    weights_exp = jnp.exp(scores - top_score)
    totals = jnp.sum(weights_exp, axis=2, keepdims=True)
    attn_probs = (weights_exp / totals).astype(jnp.bfloat16)
    log_total = top_score + jnp.log(totals)
    attended = (
        jnp.einsum("hqk,khd->qhd", attn_probs, values_all, preferred_element_type=jnp.float32)
        .reshape(seq_len, head_cols)
        .astype(jnp.bfloat16)
    )

    def proj_term(offset, length):
        return jnp.dot(attended, w_proj, preferred_element_type=jnp.float32)

    residual_one = inputs + (reduce_rows(proj_term, row_count) + bias_rows[2])
    normed_two, scaled_two, inverse_two = normalize(residual_one, gain_rows[1], bias_rows[1])
    whole_two = spread_rows(normed_two.astype(jnp.bfloat16))
    pre_act = jnp.dot(whole_two, w_fc1, preferred_element_type=jnp.float32) + b_fc1.reshape(
        -1
    ).astype(jnp.float32)
    hidden = gelu_value(pre_act).astype(jnp.bfloat16)

    def fc2_term(offset, length):
        return jnp.dot(hidden, w_fc2, preferred_element_type=jnp.float32)

    layer_out = residual_one + (reduce_rows(fc2_term, row_count) + bias_rows[3])
    stored = (
        scaled_one,
        inverse_one,
        whole_one,
        queries,
        keys_all,
        values_all,
        log_total,
        attended,
        scaled_two,
        inverse_two,
        whole_two,
        pre_act,
        hidden,
    )
    return (layer_out, stored)


def backward(upstream, matrices, vectors, stored):
    w_qkv, w_proj, w_fc1, w_fc2, b_qv, b_fc1 = matrices
    gain_rows, bias_rows = vectors
    (
        scaled_one,
        inverse_one,
        whole_one,
        queries,
        keys_all,
        values_all,
        log_total,
        attended,
        scaled_two,
        inverse_two,
        whole_two,
        pre_act,
        hidden,
    ) = stored
    row_count = upstream.shape[0]
    seq_len = queries.shape[0]
    heads_here = queries.shape[1]
    head_cols = heads_here * HD
    score_scale = 1.0 / math.sqrt(HD)
    grad_mlp = upstream.astype(jnp.bfloat16)
    grad_fc2_bias = jnp.sum(grad_mlp.astype(jnp.float32), axis=0)
    whole_mlp = spread_grads(grad_mlp)
    grad_fc2 = jnp.einsum("sf,sd->fd", hidden, whole_mlp, preferred_element_type=jnp.float32)
    grad_hidden = jnp.einsum("sd,fd->sf", whole_mlp, w_fc2, preferred_element_type=jnp.float32)
    grad_pre = (grad_hidden * gelu_slope(pre_act)).astype(jnp.bfloat16)
    grad_fc1_bias = jnp.sum(grad_pre.astype(jnp.float32), axis=0)
    grad_fc1 = jnp.einsum("sd,sf->df", whole_two, grad_pre, preferred_element_type=jnp.float32)

    def fc1_back(offset, length):
        return jnp.einsum("sf,df->sd", grad_pre, w_fc1, preferred_element_type=jnp.float32)

    grad_normed_two = reduce_grads(fc1_back, row_count)
    grad_residual = upstream + normalize_back(
        grad_normed_two, scaled_two, inverse_two, gain_rows[1]
    )
    grad_branch = grad_residual.astype(jnp.bfloat16)
    grad_proj_bias = jnp.sum(grad_branch.astype(jnp.float32), axis=0)
    whole_branch = spread_grads(grad_branch)
    grad_proj = jnp.einsum("se,sd->ed", attended, whole_branch, preferred_element_type=jnp.float32)
    grad_att = (
        jnp.einsum("sd,ed->se", whole_branch, w_proj, preferred_element_type=jnp.float32)
        .astype(jnp.bfloat16)
        .reshape(seq_len, heads_here, HD)
    )
    scores = (
        jnp.einsum("qhd,khd->hqk", queries, keys_all, preferred_element_type=jnp.float32)
        * score_scale
    )
    attn_probs = jnp.exp(scores - log_total)
    grad_probs = jnp.einsum(
        "qhd,khd->hqk", grad_att, values_all, preferred_element_type=jnp.float32
    )
    row_dot = jnp.sum(attn_probs * grad_probs, axis=2, keepdims=True)
    grad_scores = (attn_probs * (grad_probs - row_dot)).astype(jnp.bfloat16)
    grad_query = (
        jnp.einsum("hqk,khd->qhd", grad_scores, keys_all, preferred_element_type=jnp.float32)
        * score_scale
    ).astype(jnp.bfloat16)
    grad_key = (
        jnp.einsum("hqk,qhd->khd", grad_scores, queries, preferred_element_type=jnp.float32)
        * score_scale
    ).astype(jnp.bfloat16)
    grad_value = jnp.einsum(
        "hqk,qhd->khd",
        attn_probs.astype(jnp.bfloat16),
        grad_att,
        preferred_element_type=jnp.float32,
    ).astype(jnp.bfloat16)
    grad_qkv = jnp.stack([grad_query, grad_key, grad_value]).reshape(3, seq_len, head_cols)
    grad_qv = jnp.stack(
        [
            jnp.sum(grad_query.astype(jnp.float32), axis=0),
            jnp.sum(grad_value.astype(jnp.float32), axis=0),
        ]
    )
    grad_qkv_weight = jnp.einsum(
        "sd,jse->jde", whole_one, grad_qkv, preferred_element_type=jnp.float32
    )

    def qkv_back(offset, length):
        return jnp.einsum("jse,jde->sd", grad_qkv, w_qkv, preferred_element_type=jnp.float32)

    grad_normed_one = reduce_grads(qkv_back, row_count)
    grad_input = grad_residual + normalize_back(
        grad_normed_one, scaled_one, inverse_one, gain_rows[0]
    )
    grad_gain = jnp.stack(
        [
            jnp.sum(grad_normed_one * scaled_one, axis=0),
            jnp.sum(grad_normed_two * scaled_two, axis=0),
        ]
    )
    grad_bias = jnp.stack(
        [
            jnp.sum(grad_normed_one, axis=0),
            jnp.sum(grad_normed_two, axis=0),
            grad_proj_bias,
            grad_fc2_bias,
        ]
    )
    weight_part = (
        lax.psum_scatter(grad_qkv_weight, "dp", scatter_dimension=1, tiled=True),
        lax.psum_scatter(grad_proj, "dp", scatter_dimension=1, tiled=True),
        lax.psum_scatter(grad_fc1, "dp", scatter_dimension=0, tiled=True),
        lax.psum_scatter(grad_fc2, "dp", scatter_dimension=1, tiled=True),
        lax.psum_scatter(grad_qv, "dp", scatter_dimension=2, tiled=True),
        lax.psum_scatter(grad_fc1_bias.reshape(1, -1), "dp", scatter_dimension=1, tiled=True),
    )
    vector_part = (
        lax.psum_scatter(grad_gain, ("dp", "tensor"), scatter_dimension=1, tiled=True),
        lax.psum_scatter(grad_bias, ("dp", "tensor"), scatter_dimension=1, tiled=True),
    )
    return (grad_input, weight_part, vector_part)


def on_device(
    clip_rows,
    out_grad,
    clip_valid,
    gain_rows,
    bias_rows,
    qkv_weight,
    qv_bias,
    proj_weight,
    fc1_weight,
    fc1_bias,
    fc2_weight,
):
    clip_weight = clip_valid[0].astype(jnp.float32)
    upstream = out_grad.astype(jnp.float32) * clip_weight
    matrices, vectors = fetch(
        qkv_weight, proj_weight, fc1_weight, fc2_weight, qv_bias, fc1_bias, gain_rows, bias_rows
    )
    layer_out, stored = forward(clip_rows, matrices, vectors)
    matrices, vectors = fetch(
        qkv_weight, proj_weight, fc1_weight, fc2_weight, qv_bias, fc1_bias, gain_rows, bias_rows
    )
    unused_out, stored = forward(clip_rows, matrices, vectors)
    grad_input, weight_part, vector_part = backward(upstream, matrices, vectors, stored)
    return (
        (layer_out * clip_weight).astype(jnp.bfloat16),
        grad_input,
        vector_part[0],
        vector_part[1],
        weight_part[0],
        weight_part[4],
        weight_part[1],
        weight_part[2],
        weight_part[5],
        weight_part[3],
        vector_part[1][3],
    )


AXES = ("dp", "tensor")
Z_LOW, Z_HIGH, CORE, X, Y = 1, 2, 4, 8, 16
CHIP_MASKS = (0, X, Y, X | Y)
BF16, F32 = jnp.bfloat16, jnp.float32
NN, NT, TN = ((1,), (0,)), ((1,), (1,)), ((0,), (0,))
SHARE = 49
PAD = 56
SMALL = 104
CHIP_ID, CORE_ID, D_ID, T_ID = range(4)


def swap(value, mask):
    return lax.ppermute(value, AXES, [(i, i ^ mask) for i in range(32)])


def dot(left, right, dims):
    return lax.dot_general(left, right, (dims, ((), ())), preferred_element_type=F32)


TIMES = {
    "pack": 1.2,
    "pick": 1.5,
    "norm_one": 1.0,
    "qkv": 1.6,
    "attention": 7.6,
    "proj": 1.1,
    "norm_two": 0.9,
    "grad_hidden": 1.6,
    "fc": 5.6,
    "grads_fc1": 1.8,
    "grads_fc2": 1.8,
    "fc2": 1.6,
    "norm_two_back": 1.5,
    "grad_att": 1.1,
    "attention_back": 12.0,
    "qkv_back": 1.5,
    "half_grad": 1.1,
    "grads_att": 1.8,
    "norm_one_back": 1.0,
    "give": 1.3,
    "take": 12.0,
    "finish_mlp": 1.7,
    "finish_att": 1.4,
}


def call(body, outs, scalars, *args, scratch=()):
    moved = sum(math.prod(a.shape) * a.dtype.itemsize for a in args)
    moved += sum(math.prod(s) * jnp.dtype(t).itemsize for s, t in outs)
    held = sum(math.prod(s[:-1]) * max(s[-1], 128) * jnp.dtype(t).itemsize for s, t in scratch)
    time = TIMES.get(body.__name__.removesuffix("_kernel"), 0.7)
    return pl.pallas_call(
        body,
        out_shape=[jax.ShapeDtypeStruct(s, t) for s, t in outs],
        in_specs=[pl.BlockSpec(memory_space=pltpu.SMEM)]
        + [pl.BlockSpec(memory_space=pltpu.VMEM)] * len(args),
        out_specs=[pl.BlockSpec(memory_space=pltpu.VMEM)] * len(outs),
        scratch_shapes=[pltpu.VMEM(s, t) for s, t in scratch],
        compiler_params=pltpu.CompilerParams(vmem_limit_bytes=moved + held + (4 << 20)),
        cost_estimate=pl.CostEstimate(
            flops=int(time * 1.15e9), bytes_accessed=moved, transcendentals=0
        ),
    )(scalars, *args)


def chip_lanes(ids, m):
    return pl.ds(pl.multiple_of((ids[CHIP_ID] ^ m) * 256, 256), 256)


def lanes(m):
    return slice(256 * m, 256 * m + 256)


def row_ids(shape):
    return lax.broadcasted_iota(jnp.int32, shape, 0)


def pick(condition, left, right):
    return jnp.where(jnp.full(left.shape, condition, jnp.int32) != 0, left, right)


def is_zero(number):
    return jnp.where(number == 0, 1, 0)


def z_low(ids):
    return ids[T_ID] & 1


def z_high(ids):
    return ids[T_ID] >> 1


def far_chips(ids, core_flip):
    return [(ids[CHIP_ID] ^ m) * 2 + (ids[CORE_ID] ^ core_flip) for m in range(4)]


def pack_kernel(ids, rows, grads, params, keep, send, wide, stage):
    lane32 = lax.broadcasted_iota(jnp.int32, (32, 128), 1)
    spot = (lane32 == row_ids((32, 128)) + 32 * ids[T_ID]).astype(F32).astype(BF16)
    lane8 = lax.broadcasted_iota(jnp.int32, (8, 128), 1)
    spot8 = (lane8 == row_ids((8, 128)) + 8 * ids[D_ID]).astype(F32).astype(BF16)
    placed = dot(params[0:8, 0:32], spot, NN)
    qv_rows = dot(params[8:16, 0:8], spot8, NN)
    row_a = jnp.concatenate(
        [placed[k : k + 1] for k in range(6)]
        + [params[...].astype(F32)[16:17], jnp.zeros((1, 128), F32)],
        axis=1,
    )
    row_b = jnp.concatenate([qv_rows[k : k + 1] for k in range(8)], axis=1)
    flag = jnp.full((PAD, 1024), ids[4], jnp.int32).astype(F32)
    row = row_ids((PAD, 1024))
    tail = jnp.where(row == SHARE, row_a, jnp.where(row == SHARE + 1, row_b, flag))
    wide[0 : rows.shape[0], :] = rows[...].astype(F32)
    for j in range(8):
        block = wide[SHARE * j : SHARE * j + PAD, :]
        stage[j, 0:PAD, :] = jnp.where(row < SHARE, block, tail).astype(BF16)
    wide[0 : rows.shape[0], :] = grads[...].astype(F32)
    for j in range(8):
        stage[j, PAD : 2 * PAD, :] = wide[SHARE * j : SHARE * j + PAD, :].astype(BF16)
    for m, (d0, d1) in enumerate(zip(far_chips(ids, 0), far_chips(ids, 1))):
        keep[m, :, :] = stage[d0, :, :]
        send[m, :, :] = stage[d1, :, :]


def pair_up_kernel(ids, keep, got, o1, o2, o3):
    for m, out in enumerate((o1, o2, o3)):
        out[0, :, :] = keep[m + 1, :, :]
        out[1, :, :] = got[m + 1, :, :]


def arrived(ids, keep, got, d1, d2, d3):
    parts = []
    for m, (a0, a1) in enumerate(zip(far_chips(ids, 0), far_chips(ids, 1))):
        first, second = ((keep, 0), (got, 0)) if m == 0 else (((d1, d2, d3)[m - 1], k) for k in range(2))
        parts += [(a0, *first), (a1, *second)]
    return parts


def pick_kernel(ids, keep, got, d1, d2, d3, here, there, here_grad, there_grad, slots):
    row8 = row_ids((8, 1024))
    row = row_ids((PAD, 1024))
    mine = jnp.zeros((PAD, 1024), F32)
    other, mine_grad, other_grad = mine, mine, mine
    params = jnp.zeros((8, 1024), F32)
    qv = jnp.zeros((1, 1024), F32)
    high = jnp.full((1, 1024), z_high(ids), jnp.int32).astype(F32)
    parts = arrived(ids, keep, got, d1, d2, d3)
    flags = [
        ref[k, PAD - 8 : PAD, :].astype(F32)[SHARE + 10 - PAD : SHARE + 11 - PAD]
        for _, ref, k in parts
    ]
    for i, (a, ref, k) in enumerate(parts):
        seen = jnp.zeros((1, 1024), F32)
        for (c, _, _), flag in zip(parts, flags):
            earlier = jnp.full((1, 1024), jnp.where(c < a, 1, 0), jnp.int32).astype(F32)
            seen = seen + flag * earlier
        block = ref[k, 0:PAD, :].astype(F32)
        grad = ref[k, PAD : 2 * PAD, :].astype(F32)
        is_mine = jnp.where(seen == high, flags[i], 0.0)
        is_other = flags[i] - is_mine
        mine = jnp.where(is_mine > 0.5, block, mine)
        other = jnp.where(is_other > 0.5, block, other)
        mine_grad = jnp.where(is_mine > 0.5, grad, mine_grad)
        other_grad = jnp.where(is_other > 0.5, grad, other_grad)
        params = jnp.where(row8 == a, block[SHARE : SHARE + 1], params)
        qv = qv + block[SHARE + 1 : SHARE + 2]
        slots[a, :, :] = jnp.broadcast_to(is_mine[:, 0:128], (8, 128))
        slots[8 + a, :, :] = jnp.broadcast_to(is_other[:, 0:128], (8, 128))
    for value, out in ((mine, here), (other, there)):
        out[0:PAD, :] = jnp.where(row == PAD - 1, qv, value).astype(BF16)
        out[PAD : PAD + 8, :] = params.astype(BF16)
    here_grad[...] = mine_grad.astype(BF16)
    there_grad[...] = other_grad.astype(BF16)


def lay_rows(ids, here, r1, r2, r3, wide):
    low = is_zero(z_low(ids))
    for m in range(4):
        cols = chip_lanes(ids, m)
        blocks = [ref[0:PAD, cols].astype(F32) for ref in (here, r1, r2, r3)]
        order = (
            pick(low, blocks[0], blocks[1]),
            pick(low, blocks[2], blocks[3]),
            pick(low, blocks[1], blocks[0]),
            pick(low, blocks[3], blocks[2]),
        )
        for i, block in enumerate(order):
            wide[SHARE * i : SHARE * i + SHARE, lanes(m)] = block[0:SHARE]


def norm_parts(values):
    centre = jnp.mean(values, axis=1, keepdims=True)
    offsets = values - centre
    inverse = lax.rsqrt(jnp.mean(offsets * offsets, axis=1, keepdims=True) + norm_eps)
    return offsets * inverse, inverse


def norm_one_kernel(ids, here, r1, r2, r3, rows, normed, vec, qv_bias, b_fc1, wide, small):
    lay_rows(ids, here, r1, r2, r3, wide)
    own = here[PAD - 8 : PAD + 8, :].astype(F32)
    far = r2[PAD - 8 : PAD + 8, :].astype(F32)
    tails = [own[8:], far[8:]] + [r[PAD : PAD + 8, :].astype(F32) for r in (r1, r3)]
    params = tails[0] + tails[1] + tails[2] + tails[3]
    small[...] = jnp.zeros_like(small)
    for d in range(8):
        for k in range(6):
            small[k : k + 1, 128 * d : 128 * d + 128] = params[
                d : d + 1, 128 * k : 128 * k + 128
            ]
    for m in range(4):
        vec[:, lanes(m)] = small[:, chip_lanes(ids, m)]
    home = pick(is_zero(ids[CORE_ID]), own, far)
    for k in range(8):
        qv_bias[k : k + 1, :] = home[7:8, 128 * k : 128 * k + 128]
        b_fc1[0:1, 128 * k : 128 * k + 128] = home[8 + k : 9 + k, 768:896]
    values = wide[...]
    scaled, _ = norm_parts(values)
    rows[...] = values.astype(BF16)
    normed[...] = (scaled * vec[0:1, :] + vec[2:3, :]).astype(BF16)


def lay_grad_kernel(ids, here, r1, r2, r3, out, wide):
    lay_rows(ids, here, r1, r2, r3, wide)
    out[...] = wide[...].astype(BF16)


def join_rows(wide, own, got):
    half = own.shape[0]
    wide[0:half, :] = own[...].astype(F32)
    wide[half : 2 * half, :] = got[...].astype(F32)


PROJ = 3


def part_of(weights, m, j):
    if m < 3:
        return weights[m][:, lanes(j)]
    return weights[3 + j // 2][:, lanes(j % 2)]


VALUES = 400


def fold_rows(value):
    half = value.shape[0] // 2
    return jnp.concatenate([value[:half], value[half:]], axis=1)


def qkv_kernel(ids, own, got, qv_bias, w0, w1, w2, w3, w4, whole, o0, o1, o2, o3, wide, heads):
    weights = (w0, w1, w2, w3, w4)
    join_rows(wide, own, got)
    whole[...] = wide[...].astype(BF16)
    for j in range(3):
        total = dot(whole[:, lanes(0)], w0[:, lanes(j)], NN)
        for m in range(1, 4):
            total = total + dot(whole[:, lanes(m)], part_of(weights, m, j), NN)
        for h in range(4):
            part = total[:, 64 * h : 64 * h + 64]
            if j != 1:
                k = (j // 2) * 4 + h
                part = part + qv_bias[k : k + 1, 0:64]
            if j < 2:
                heads[h, 0 : part.shape[0], 64 * j : 64 * j + 64] = part.astype(BF16)
            else:
                heads[h, VALUES:, :] = fold_rows(part).astype(BF16)
    for m, out in enumerate((o0, o1, o2, o3)):
        out[...] = heads[ids[CHIP_ID] ^ m, :, :]


STEP = 224


def stage_qkv(stage, parts):
    tokens = stage.shape[0] // 4
    half = tokens // 2
    for m, part in enumerate(parts):
        start = tokens * m
        stage[start : start + tokens, 0:128] = part[0:tokens, :].astype(F32)
        stage[start : start + half, 128:192] = part[VALUES:, 0:64].astype(F32)
        stage[start + half : start + tokens, 128:192] = part[VALUES:, 64:128].astype(F32)


def attention_kernel(ids, a0, a1, a2, a3, o0, o1, o2, o3, lse, stage, q, k, v):
    tokens = stage.shape[0] // 4
    stage_qkv(stage, (a0, a1, a2, a3))
    q[...] = (stage[:, 0:64] * 0.125).astype(BF16)
    k[...] = stage[:, 64:128].astype(BF16)
    v[...] = stage[:, 128:192].astype(BF16)

    def body(i, carry):
        rows = pl.ds(pl.multiple_of(i * STEP, 32), STEP)
        scores = dot(q[rows, :], k[...], NT)
        top = jnp.max(scores, axis=1, keepdims=True)
        weights = jnp.exp(scores - top)
        total = jnp.sum(weights, axis=1, keepdims=True)
        mixed = dot(weights.astype(BF16), v[...], NN)
        stage[rows, 0:64] = mixed / total
        spread = jnp.broadcast_to(top + jnp.log(total), (STEP, 128))
        lse[i, :, :] = jnp.transpose(spread)[0:8, :]
        return carry

    lax.fori_loop(0, stage.shape[0] // STEP, body, 0)
    for m, out in enumerate((o0, o1, o2, o3)):
        out[...] = fold_rows(stage[tokens * m : tokens * m + tokens, 0:64]).astype(BF16)


def attention_back_kernel(
    ids, a0, a1, a2, a3, g0, g1, g2, g3, lse, o0, o1, o2, o3, stage, q, k, v, g, grad_k, grad_v
):
    tokens = stage.shape[0] // 4
    stage_qkv(stage, (a0, a1, a2, a3))
    q[...] = (stage[:, 0:64] * 0.125).astype(BF16)
    k[...] = stage[:, 64:128].astype(BF16)
    v[...] = stage[:, 128:192].astype(BF16)
    for m, part in enumerate((g0, g1, g2, g3)):
        middle = tokens * m + tokens // 2
        stage[tokens * m : middle, 0:64] = part[:, 0:64].astype(F32)
        stage[middle : tokens * m + tokens, 0:64] = part[:, 64:128].astype(F32)
    g[...] = stage[:, 0:64].astype(BF16)
    keys_t = jnp.transpose(k[...])
    grad_k[...] = jnp.zeros_like(grad_k)
    grad_v[...] = jnp.zeros_like(grad_v)

    def body(i, carry):
        rows = pl.ds(pl.multiple_of(i * STEP, 32), STEP)
        queries, grad = q[rows, :], g[rows, :]
        probs = jnp.exp(dot(k[...], queries, NT) - lse[i, 0:1, :])
        grad_probs = dot(v[...], grad, NT)
        row_dot = jnp.sum(probs * grad_probs, axis=0, keepdims=True)
        grad_scores = (probs * (grad_probs - row_dot)).astype(BF16)
        grad_v[...] += dot(probs.astype(BF16), grad, NN)
        grad_k[...] += dot(grad_scores, queries, NN)
        stage[rows, 0:64] = jnp.transpose(dot(keys_t, grad_scores, NN)) * 0.125
        return carry

    lax.fori_loop(0, stage.shape[0] // STEP, body, 0)
    for m, out in enumerate((o0, o1, o2, o3)):
        rows = slice(tokens * m, tokens * m + tokens)
        out[0:tokens, 0:64] = stage[rows, 0:64].astype(BF16)
        out[0:tokens, 64:128] = grad_k[rows, :].astype(BF16)
        out[VALUES:, :] = fold_rows(grad_v[rows, :]).astype(BF16)


def split_rows(total, keep, send, cols):
    half = keep.shape[0]
    keep[:, cols] = total[:half]
    send[:, cols] = total[half:].astype(BF16)


def proj_kernel(ids, a0, a1, a2, a3, w0, w1, w2, w3, w4, joined, keep, send, heads, wide):
    for m, part in enumerate((a0, a1, a2, a3)):
        heads[m, :, :] = part[...]
    half = keep.shape[0]
    for h in range(4):
        part = heads[h ^ ids[CHIP_ID], :, :].astype(F32)
        wide[0:half, 64 * h : 64 * h + 64] = part[:, 0:64]
        wide[half:, 64 * h : 64 * h + 64] = part[:, 64:128]
    joined[...] = wide[...].astype(BF16)
    for m in range(4):
        weight = part_of((w0, w1, w2, w3, w4), m, PROJ)
        split_rows(dot(joined[...], weight, NT), keep, send, lanes(m))


def pair_kernel(ids, keep, got, part, send):
    total = keep[...] + got[...].astype(F32)
    part[...] = total
    send[...] = total.astype(BF16)


def half_kernel(ids, keep, got, part, send):
    own = part.shape[0]
    total = keep[...] + got[...].astype(F32)
    low = is_zero(z_low(ids))
    part[...] = pick(low, total[:own], total[own:])
    send[...] = pick(low, total[own:], total[:own]).astype(BF16)


def half_grad_kernel(ids, keep, got, rows, sums_two, sums_fc1, sums_qv, part, send, small):
    own = part.shape[0]
    total = keep[...] + got[...].astype(F32)
    low = is_zero(z_low(ids))
    part[...] = pick(low, total[:own], total[own:])
    scaled, _ = norm_parts(rows[...].astype(F32))
    send[0:own, :] = pick(low, total[own:], total[:own]).astype(BF16)
    sums = jnp.concatenate(
        [
            jnp.sum(total * scaled, axis=0, keepdims=True),
            sums_two[0:1, :],
            jnp.sum(total, axis=0, keepdims=True),
            sums_two[1:4, :],
            sums_qv[...],
            sums_fc1[...],
        ],
        axis=0,
    )
    small[...] = sums
    send[SMALL : SMALL + 8, :] = sums.astype(BF16)


def norm_two_kernel(ids, rows, part, got, vec, residual, normed):
    total = rows[...].astype(F32) + (part[...] + got[...].astype(F32) + vec[4:5, :])
    residual[...] = total
    scaled, _ = norm_parts(total)
    normed[...] = (scaled * vec[1:2, :] + vec[3:4, :]).astype(BF16)


def grad_hidden_kernel(ids, own, got, w0, w1, w2, w3, whole, out, wide):
    join_rows(wide, own, got)
    whole[...] = wide[...].astype(BF16)
    for c in range(4):
        total = dot(whole[:, lanes(0)], w0[:, lanes(c)], NN)
        for m, weight in enumerate((w1, w2, w3)):
            total = total + dot(whole[:, lanes(m + 1)], weight[:, lanes(c)], NN)
        out[:, lanes(c)] = total


def fc_kernel(
    ids, own, got, grad_hidden, b_fc1, w0, w1, w2, w3, whole, hidden, grad_pre, sums, keep, send, wide
):
    weights = (w0, w1, w2, w3)
    join_rows(wide, own, got)
    whole[...] = wide[...].astype(BF16)
    wide[...] = jnp.zeros_like(wide)

    def body(c, carry):
        cols = pl.ds(pl.multiple_of(c * 256, 256), 256)
        pre = b_fc1[:, cols] + dot(whole[:, lanes(0)], w0[:, cols], NN)
        for m in range(1, 4):
            pre = pre + dot(whole[:, lanes(m)], weights[m][:, cols], NN)
        half_erf = 0.5 * (1.0 + lax.erf(pre * root_half))
        hidden[:, cols] = (pre * half_erf).astype(BF16)
        slope = half_erf + pre * jnp.exp(-0.5 * pre * pre) * inv_root_tau
        grad = (grad_hidden[:, cols] * slope).astype(BF16)
        grad_pre[:, cols] = grad
        sums[:, cols] = jnp.sum(grad.astype(F32), axis=0, keepdims=True)
        for m in range(4):
            wide[:, lanes(m)] += dot(grad, weights[m][:, cols], NT)
        return carry

    lax.fori_loop(0, 4, body, 0)
    for m in range(4):
        split_rows(wide[:, lanes(m)], keep, send, lanes(m))


def norm_back(total, scaled, inverse, gain):
    hat = total * gain
    return (
        hat
        - jnp.mean(hat, axis=1, keepdims=True)
        - scaled * jnp.mean(hat * scaled, axis=1, keepdims=True)
    ) * inverse


def norm_two_back_kernel(ids, residual, part, got, grads, vec, grad_residual, grad_branch, sums):
    scaled, inverse = norm_parts(residual[...])
    total = part[...] + got[...].astype(F32)
    upstream = grads[...].astype(F32)
    result = upstream + norm_back(total, scaled, inverse, vec[1:2, :])
    branch = result.astype(BF16)
    grad_residual[...] = result
    grad_branch[...] = branch
    own = total.shape[0] // 2
    row = row_ids(total.shape)
    low = jnp.full(total.shape, z_low(ids), jnp.int32)
    mine = jnp.where(row < own, 1 - low, low) != 0

    def column_sum(value):
        return jnp.sum(jnp.where(mine, value, 0.0), axis=0, keepdims=True)

    sums[0:1, :] = column_sum(total * scaled)
    sums[1:2, :] = column_sum(total)
    sums[2:3, :] = column_sum(branch.astype(F32))
    sums[3:4, :] = column_sum(upstream)
    sums[4:8, :] = jnp.zeros((4, sums.shape[1]), F32)


def grad_att_kernel(ids, own, got, w0, w1, w2, w3, w4, whole, o0, o1, o2, o3, wide, heads):
    join_rows(wide, own, got)
    whole[...] = wide[...].astype(BF16)
    weights = (w0, w1, w2, w3, w4)
    total = dot(whole[:, lanes(0)], w0[:, lanes(PROJ)], NN)
    for m in range(1, 4):
        total = total + dot(whole[:, lanes(m)], part_of(weights, m, PROJ), NN)
    for h in range(4):
        heads[h, :, :] = fold_rows(total[:, 64 * h : 64 * h + 64]).astype(BF16)
    for m, out in enumerate((o0, o1, o2, o3)):
        out[...] = heads[ids[CHIP_ID] ^ m, :, :]


def qkv_back_kernel(ids, g0, g1, g2, g3, w0, w1, w2, w3, w4, joined, keep, send, sums, heads, wide):
    for m, part in enumerate((g0, g1, g2, g3)):
        heads[m, :, :] = part[...]
    half, tokens = keep.shape[0], joined.shape[0]
    for h in range(4):
        part = heads[h ^ ids[CHIP_ID], :, :]
        for j in range(2):
            joined[:, 256 * j + 64 * h : 256 * j + 64 * h + 64] = part[
                0:tokens, 64 * j : 64 * j + 64
            ]
        values = part[VALUES:, :].astype(F32)
        wide[0:half, 64 * h : 64 * h + 64] = values[:, 0:64]
        wide[half:, 64 * h : 64 * h + 64] = values[:, 64:128]
        for k, value in ((h, part[0:tokens, 0:64]), (4 + h, wide[:, 64 * h : 64 * h + 64])):
            total = jnp.sum(value.astype(F32), axis=0, keepdims=True)
            sums[0:1, 128 * k : 128 * k + 128] = jnp.concatenate(
                [total, jnp.zeros((1, 64), F32)], axis=1
            )
    joined[:, 512:768] = wide[...].astype(BF16)
    for m in range(4):
        weights = (w0, w1, w2, w3, w4)
        total = dot(joined[:, lanes(0)], part_of(weights, m, 0), NT)
        for j in (1, 2):
            total = total + dot(joined[:, lanes(j)], part_of(weights, m, j), NT)
        split_rows(total, keep, send, lanes(m))


def to_owners(ids, value, wide, here, there):
    wide[0 : 2 * SHARE, :] = value
    wide[2 * SHARE :, :] = jnp.zeros((wide.shape[0] - 2 * SHARE, wide.shape[1]), F32)
    for m in range(4):
        cols = chip_lanes(ids, m)
        here[0:PAD, cols] = wide[0:PAD, lanes(m)].astype(BF16)
        there[0:PAD, cols] = wide[SHARE : SHARE + PAD, lanes(m)].astype(BF16)


def own_half(ids, ref):
    own = ref.shape[0] // 2
    value = ref[...].astype(F32)
    return pick(is_zero(z_low(ids)), value[:own], value[own:])


def norm_one_back_kernel(
    ids, rows, part, got, grad_residual, vec, small, here, there, wide
):
    scaled, inverse = norm_parts(own_half(ids, rows))
    total = part[...] + got[0 : 2 * SHARE, :].astype(F32)
    result = own_half(ids, grad_residual) + norm_back(total, scaled, inverse, vec[0:1, :])
    to_owners(ids, result, wide, here, there)
    far = jnp.where(row_ids((8, 1024)) < 6, got[SMALL : SMALL + 8, :].astype(F32), 0.0)
    sums = (small[...] + far).astype(BF16)
    here[PAD : PAD + 8, :] = sums
    there[PAD : PAD + 8, :] = sums


def layer_out_kernel(ids, residual, part, got, vec, here, there, wide):
    result = own_half(ids, residual) + (part[...] + got[...].astype(F32) + vec[5:6, :])
    to_owners(ids, result, wide, here, there)


def fc2_kernel(ids, hidden, w0, w1, w2, w3, keep, send):
    for m, weight in enumerate((w0, w1, w2, w3)):
        split_rows(dot(hidden[...], weight[...], NT), keep, send, lanes(m))


def for_slot(slots, d, left, right):
    value = jnp.where(slots[8 + d, 0:1, 0:1] > 0.5, right, 0.0)
    return jnp.where(slots[d, 0:1, 0:1] > 0.5, left, value)


def give_out_kernel(ids, slots, here, away, keep, send):
    left = here[...].astype(F32)
    right = away[...].astype(F32)
    for out, flip in ((keep, 0), (send, 1)):
        for m, d in enumerate(far_chips(ids, flip)):
            out[m, :, :] = for_slot(slots, d, left, right).astype(BF16)


def give_kernel(ids, slots, here, away, keep, send, rel, flat, tail):
    left = here[0:PAD, :].astype(F32)
    right = away[0:PAD, :].astype(F32)
    own = here[PAD : PAD + 8, :].astype(F32)
    far = away[PAD : PAD + 8, :].astype(F32)
    rel[...] = own + far
    home = pick(is_zero(ids[CORE_ID]), own, far)
    for m in range(4):
        flat[:, chip_lanes(ids, m)] = rel[:, lanes(m)]
    rel[0:1, :] = home[7:8]
    tail[...] = jnp.zeros_like(tail)
    for k in range(8):
        row, lane = (SHARE + k, 128) if k < 7 else (SHARE, 256)
        tail[row : row + 1, lane : lane + 128] = home[6:7, 128 * k : 128 * k + 128]
    row = row_ids((PAD, 1024))
    for out, flip in ((keep, 0), (send, 1)):
        for m, d in enumerate(far_chips(ids, flip)):
            cols = pl.ds(pl.multiple_of(d * 128, 128), 128)
            tail[SHARE : SHARE + 6, 0:128] = flat[0:6, cols]
            tail[SHARE + 6 : PAD, 0:128] = rel[0:1, cols]
            value = for_slot(slots, d, left, right)
            out[m, :, :] = jnp.where(row < SHARE, value, tail[...]).astype(BF16)


def settle_rows(parts, stage, out):
    for a, ref, k in parts:
        stage[a, :, :] = ref[k, :, :].astype(F32)
    for j in range(8):
        out[SHARE * j : SHARE * j + SHARE, :] = stage[j, 0:SHARE, :]


def take_out_kernel(ids, keep, got, d1, d2, d3, out, stage, wide):
    settle_rows(arrived(ids, keep, got, d1, d2, d3), stage, wide)
    out[...] = wide[...].astype(BF16)


def take_kernel(ids, keep, got, d1, d2, d3, out, gains, biases, last, qv, b_fc1, stage):
    parts = arrived(ids, keep, got, d1, d2, d3)
    settle_rows(parts, stage, out)
    total = jnp.zeros((8, 384), F32)
    for _, ref, k in parts:
        total = total + ref[k, PAD - 8 : PAD, 0:384].astype(F32)
    rows = pltpu.roll(total[:, 0:128], (128 - 32 * ids[T_ID]) & 127, 1)
    gains[...] = rows[1:3, 0:32]
    biases[...] = rows[3:7, 0:32]
    last[...] = rows[6:7, 0:32]
    b_fc1[...] = total[7:8, 0:128]
    pieces = jnp.concatenate([total[1:8, 128:256], total[1:2, 256:384]], axis=0)
    qv[...] = pltpu.roll(pieces, (128 - 8 * ids[D_ID]) & 127, 1)[:, 0:8]


def shards_kernel(ids, qkv, proj, fc2, first, second):
    for j in range(3):
        first[:, lanes(j)] = qkv[j, :, :]
    first[:, lanes(PROJ)] = jnp.transpose(proj[...])
    second[...] = jnp.transpose(fc2[...])


def offer_kernel(ids, own, far, send):
    @pl.when(ids[CORE_ID] == 0)
    def _():
        send[...] = far[...]

    @pl.when(ids[CORE_ID] != 0)
    def _():
        send[...] = own[...]


def merge_kernel(ids, own, far, got, out):
    half = own.shape[0]

    @pl.when(ids[CORE_ID] == 0)
    def _():
        out[0:half, :] = own[...]
        out[half:, :] = got[...]

    @pl.when(ids[CORE_ID] != 0)
    def _():
        out[0:half, :] = got[...]
        out[half:, :] = far[...]


X_FIRST, Y_FIRST = (1, 2), (2, 1)


def blocks_of(order, left, right, cols, send, here, there, out_cols):
    near, far = order
    for slot, m in ((0, near), (1, 3)):
        send[slot, :, out_cols] = dot(left[:, lanes(m)], right[:, cols], TN).astype(BF16)
    here[:, out_cols] = dot(left[:, lanes(0)], right[:, cols], TN)
    there[:, out_cols] = dot(left[:, lanes(far)], right[:, cols], TN)


def grads_fc1_kernel(ids, left, right, send, here, there):
    for c in range(2):
        cols = slice(512 * c, 512 * c + 512)
        blocks_of(X_FIRST, left, right, cols, send, here, there, cols)


def grads_fc2_kernel(ids, left, right, send, here, there):
    for c in range(2):
        cols = slice(512 * c, 512 * c + 512)
        blocks_of(Y_FIRST, left, right, cols, send, here, there, cols)


def grads_att_kernel(
    ids, rows, joined, branch, mixed, send_x, here_x, there_x, send_y, here_y, there_y
):
    blocks_of(X_FIRST, rows, joined, slice(0, 512), send_x, here_x, there_x, slice(0, 512))
    blocks_of(Y_FIRST, rows, joined, slice(512, 768), send_y, here_y, there_y, slice(0, 256))
    blocks_of(Y_FIRST, branch, mixed, slice(0, 256), send_y, here_y, there_y, slice(256, 512))


def fold_kernel(ids, here, there, got, other, whole):
    other[...] = (there[...] + got[1, :, :].astype(F32)).astype(BF16)
    whole[...] = here[...] + got[0, :, :].astype(F32)


def gather_kernel(ids, whole_x, got_x, whole_y, got_y, keep, send):
    n = whole_x.shape[1]
    for core in range(2):

        @pl.when(ids[CORE_ID] == core)
        def _():
            own = slice(128 * core, 128 * core + 128)
            other = slice(128 - 128 * core, 256 - 128 * core)
            for cols, whole, got in (
                (slice(0, n), whole_x, got_x),
                (slice(n, 2 * n), whole_y, got_y),
            ):
                for out, rows in ((keep, own), (send, other)):
                    total = whole[rows, :] + got[rows, :].astype(F32)
                    out[:, cols] = total.astype(BF16)


def away_kernel(ids, keep, got, out):
    @pl.when(ids[CORE_ID] == 0)
    def _():
        out[...] = got[...]

    @pl.when(ids[CORE_ID] != 0)
    def _():
        out[...] = keep[...]


def whole_sum(ids, keep, got, moved, cols):
    core = is_zero(ids[CORE_ID])
    own = pick(core, keep[:, cols].astype(F32), got[:, cols].astype(F32))
    return own + moved[:, cols].astype(F32)


def finish_mlp_kernel(ids, keep, got, moved, fc1, fc2):
    fc1[...] = whole_sum(ids, keep, got, moved, slice(0, 1024))
    fc2[...] = jnp.transpose(whole_sum(ids, keep, got, moved, slice(1024, 2048)))


def finish_att_kernel(ids, keep, got, moved, qkv, proj):
    for j in range(3):
        qkv[j, :, :] = whole_sum(ids, keep, got, moved, lanes(j))
    proj[...] = jnp.transpose(whole_sum(ids, keep, got, moved, lanes(PROJ)))


def tie(*values):
    return lax.optimization_barrier(values)


def sum_second(ids, first, second):
    n = first[1].shape[1]
    outs = [((256, n), BF16), ((256, n), F32)]
    other_x, whole_x = call(fold_kernel, outs, ids, *first)
    other_y, whole_y = call(fold_kernel, outs, ids, *second)
    return whole_x, other_x, whole_y, other_y


def send_second(whole_x, other_x, whole_y, other_y):
    return whole_x, swap(other_x, Y), whole_y, swap(other_y, X)


def sum_third(ids, parts):
    n = 2 * parts[0].shape[1]
    keep, send = call(gather_kernel, [((128, n), BF16)] * 2, ids, *parts)
    got = swap(send, CORE)
    (away,) = call(away_kernel, [((128, n), BF16)], ids, keep, got)
    return keep, got, away


def on_device_spread(
    clip_rows,
    out_grad,
    clip_valid,
    gain_rows,
    bias_rows,
    qkv_weight,
    qv_bias,
    proj_weight,
    fc1_weight,
    fc1_bias,
    fc2_weight,
):
    d, t = lax.axis_index("dp"), lax.axis_index("tensor")
    core = d & 1
    ids = jnp.stack([d >> 1, core, d, t, clip_valid[0]]).astype(jnp.int32)
    count = clip_rows.shape[0]
    half, own = count // 2, count // 4
    behind = (PAD + 8, 1024)
    plain = (PAD, 1024)
    packed = (VALUES + half, 128)
    wide = ((count, 1024), F32)

    def to_chips(keep, send):
        got = swap(send, CORE)
        shape = (2, *keep.shape[1:])
        return got, *call(pair_up_kernel, [(shape, BF16)] * 3, ids, keep, got)

    def over_chips(pairs):
        return [swap(pairs[m], CHIP_MASKS[m + 1]) for m in range(3)]

    def offer(shard, far):
        (send,) = call(offer_kernel, [(shard.shape, BF16)], ids, shard, far)
        return send

    def merge(shard, far, send):
        (out,) = call(
            merge_kernel, [((256, shard.shape[1]), BF16)], ids, shard, far, swap(send, CORE)
        )
        return out

    def trade(parts):
        return [parts[0]] + [swap(parts[m], CHIP_MASKS[m]) for m in range(1, 4)]

    params = jnp.concatenate(
        [
            jnp.pad(v, ((0, n - v.shape[0]), (0, 128 - v.shape[1])))
            for v, n in (
                (jnp.concatenate([gain_rows, bias_rows]), 8),
                (qv_bias.reshape(8, 8), 8),
                (fc1_bias, 8),
            )
        ]
    )
    shard_a, shard_g = call(
        shards_kernel,
        [((128, 1024), BF16), ((128, 1024), BF16)],
        ids,
        qkv_weight,
        proj_weight,
        fc2_weight,
    )
    far_a = swap(shard_a, Z_HIGH)
    own_rows, _ = tie(clip_rows, shard_a)
    keep, send = call(
        pack_kernel,
        [((4, 2 * PAD, 1024), BF16)] * 2,
        ids,
        own_rows,
        out_grad,
        params,
        scratch=[((400, 1024), F32), ((8, 2 * PAD, 1024), BF16)],
    )
    w0 = merge(shard_a, far_a, offer(shard_a, far_a))
    shard_f, _ = tie(fc1_weight, far_a)
    far_f = swap(shard_f, Z_HIGH)
    got, *pairs = to_chips(keep, send)
    *parts, w0 = tie(keep, got, *over_chips(pairs), w0)
    here, there, here_grad, there_grad, slots = call(
        pick_kernel,
        [(behind, BF16), (behind, BF16), (plain, BF16), (plain, BF16), ((16, 8, 128), F32)],
        ids,
        *parts,
    )
    r1, r2, r3 = swap(here, Z_LOW), swap(there, Z_HIGH), swap(there, Z_LOW | Z_HIGH)
    w1, w2 = swap(w0, X), swap(w0, Y)
    w_att = (w0, w1, w2, swap(w2[:, :512], X), swap(w1[:, 512:], Y))
    r1, r2, r3, far_f, shard_f = tie(r1, r2, r3, far_f, shard_f)
    f0 = merge(shard_f, far_f, offer(shard_f, far_f))
    rows, normed, vec, qkv_bias, b_fc1 = call(
        norm_one_kernel,
        [
            ((half, 1024), BF16),
            ((half, 1024), BF16),
            ((8, 1024), F32),
            ((8, 128), F32),
            ((1, 1024), F32),
        ],
        ids,
        here,
        r1,
        r2,
        r3,
        scratch=[((half, 1024), F32), ((8, 1024), F32)],
    )

    whole_one, *qkv = call(
        qkv_kernel,
        [((count, 1024), BF16)] + [(packed, BF16)] * 4,
        ids,
        normed,
        swap(normed, CORE),
        qkv_bias,
        *w_att,
        scratch=[wide, ((4, *packed), BF16)],
    )
    shard_g, *qkv = tie(shard_g, *qkv)
    far_g = swap(shard_g, Z_HIGH)
    *qkv, f0, here_grad, there_grad = tie(*trade(qkv), f0, here_grad, there_grad)
    f1, f2 = swap(f0, X), swap(f0, Y)
    s1, s2 = swap(here_grad, Z_LOW), swap(there_grad, Z_HIGH)
    tokens = 4 * count
    *mixed, lse = call(
        attention_kernel,
        [((half, 128), BF16)] * 4 + [((tokens // STEP, 8, STEP), F32)],
        ids,
        *qkv,
        scratch=[((tokens, 192), F32)] + [((tokens, 64), BF16)] * 3,
    )
    shard_g, far_g, *mixed = tie(shard_g, far_g, *mixed)
    g0 = merge(shard_g, far_g, offer(shard_g, far_g))
    *mixed, f1, f2, s1, s2 = tie(*trade(mixed), f1, f2, s1, s2)
    g1, g2 = swap(g0, X), swap(g0, Y)
    f3, g3, s3 = swap(f2, X), swap(g1, Y), swap(s2, Z_LOW)
    attended, keep, send = call(
        proj_kernel,
        [((count, 256), BF16), ((half, 1024), F32), ((half, 1024), BF16)],
        ids,
        *mixed,
        *w_att,
        scratch=[((4, half, 128), BF16), ((count, 256), F32)],
    )

    def pair(keep, send):
        return call(
            pair_kernel, [((half, 1024), F32), ((half, 1024), BF16)], ids, keep, swap(send, CORE)
        )

    def halve(keep, send):
        return call(
            half_kernel, [((own, 1024), F32), ((own, 1024), BF16)], ids, keep, swap(send, CORE)
        )

    part, send = pair(keep, send)
    away, s3 = tie(swap(send, Z_LOW), s3)
    w_fc1, w_fc2 = (f0, f1, f2, f3), (g0, g1, g2, g3)
    (grads,) = call(
        lay_grad_kernel,
        [((half, 1024), BF16)],
        ids,
        here_grad,
        s1,
        s2,
        s3,
        scratch=[((half, 1024), F32)],
    )
    residual, normed_two = call(
        norm_two_kernel,
        [((half, 1024), F32), ((half, 1024), BF16)],
        ids,
        rows,
        part,
        away,
        vec,
    )
    whole_mlp, grad_hidden = call(
        grad_hidden_kernel,
        [((count, 1024), BF16), ((count, 1024), F32)],
        ids,
        grads,
        swap(grads, CORE),
        *w_fc2,
        scratch=[wide],
    )

    whole_two, hidden, grad_pre, sums_fc1, keep, send = call(
        fc_kernel,
        [((count, 1024), BF16)] * 3
        + [((1, 1024), F32), ((half, 1024), F32), ((half, 1024), BF16)],
        ids,
        normed_two,
        swap(normed_two, CORE),
        grad_hidden,
        b_fc1,
        *w_fc1,
        scratch=[wide],
    )
    part, send = pair(keep, send)
    late = tie(send, whole_mlp, hidden, whole_two, grad_pre)
    grad_outs = [((2, 256, 1024), BF16), ((256, 1024), F32), ((256, 1024), F32)]
    cost = 2 * count * 1024 * 1024
    send_f, *rest_f = call(grads_fc1_kernel, grad_outs, ids, late[3], late[4])
    send_g, *rest_g = call(grads_fc2_kernel, grad_outs, ids, late[1], late[2])
    sums_f = (*rest_f, swap(send_f, X))
    sums_g = (*rest_g, swap(send_g, Y))
    keep_out, send_out = call(
        fc2_kernel,
        [((half, 1024), F32), ((half, 1024), BF16)],
        ids,
        late[2],
        *w_fc2,
    )
    away, keep_out, send_out = tie(swap(send, Z_LOW), keep_out, send_out)
    part_out, send_out = halve(keep_out, send_out)
    away_out = swap(send_out, Z_LOW)
    grad_residual, grad_branch, sums_two = call(
        norm_two_back_kernel,
        [((half, 1024), F32), ((half, 1024), BF16), ((8, 1024), F32)],
        ids,
        residual,
        part,
        away,
        grads,
        vec,
    )

    whole_branch, *grad_att = call(
        grad_att_kernel,
        [((count, 1024), BF16)] + [((half, 128), BF16)] * 4,
        ids,
        grad_branch,
        swap(grad_branch, CORE),
        *w_att,
        scratch=[wide, ((4, half, 128), BF16)],
    )
    *grad_att, part_out, away_out = tie(*grad_att, part_out, away_out)
    here_out, there_out = call(
        layer_out_kernel,
        [(plain, BF16)] * 2,
        ids,
        residual,
        part_out,
        away_out,
        vec,
        scratch=[((2 * PAD, 1024), F32)],
    )
    sums_mlp = sum_second(ids, sums_f, sums_g)
    *grad_att, whole_x, other_x, whole_y, other_y, here_out, there_out = tie(
        *trade(grad_att), *sums_mlp, here_out, there_out
    )
    sums_mlp = send_second(whole_x, other_x, whole_y, other_y)
    away_out = swap(there_out, Z_HIGH)
    grad_qkv = call(
        attention_back_kernel,
        [(packed, BF16)] * 4,
        ids,
        *qkv,
        *grad_att,
        lse,
        scratch=[((tokens, 192), F32)] + [((tokens, 64), BF16)] * 4 + [((tokens, 64), F32)] * 2,
    )
    *grad_qkv, away_out, whole_x, got_x, whole_y, got_y = tie(*grad_qkv, away_out, *sums_mlp)
    *sums_mlp, moved_mlp = sum_third(ids, (whole_x, got_x, whole_y, got_y))
    keep_out, send_out = call(
        give_out_kernel, [((4, PAD, 1024), BF16)] * 2, ids, slots, here_out, away_out
    )
    got_out, *pairs_out = to_chips(keep_out, send_out)
    *grad_qkv, moved_mlp, got_out, p1, p2, p3 = tie(
        *trade(grad_qkv), moved_mlp, got_out, *pairs_out
    )
    moved_mlp = swap(moved_mlp, Z_HIGH)
    parts_out = over_chips((p1, p2, p3))
    joined, keep, send, sums_qv = call(
        qkv_back_kernel,
        [((count, 768), BF16), ((half, 1024), F32), ((half, 1024), BF16), ((1, 1024), F32)],
        ids,
        *grad_qkv,
        *w_att,
        scratch=[((4, *packed), BF16), ((count, 256), F32)],
    )
    part, send, small = call(
        half_grad_kernel,
        [((own, 1024), F32), ((SMALL + 8, 1024), BF16), ((8, 1024), F32)],
        ids,
        keep,
        swap(send, CORE),
        rows,
        sums_two,
        sums_fc1,
        sums_qv,
    )
    late = tie(send, whole_one, joined, whole_branch, attended)
    grad_outs = [((2, 256, 512), BF16), ((256, 512), F32), ((256, 512), F32)]
    send_x, here_x, there_x, send_y, here_y, there_y = call(
        grads_att_kernel, grad_outs * 2, ids, *late[1:]
    )
    away, send_x, send_y, *parts_out = tie(swap(send, Z_LOW), send_x, send_y, *parts_out)
    parts_out = keep_out, got_out, *parts_out
    got_x, got_y = swap(send_x, X), swap(send_y, Y)
    here, there = call(
        norm_one_back_kernel,
        [(behind, BF16)] * 2,
        ids,
        rows,
        part,
        away,
        grad_residual,
        vec,
        small,
        scratch=[((2 * PAD, 1024), F32)],
    )
    away, got_x, got_y, moved_mlp = tie(swap(there, Z_HIGH), got_x, got_y, moved_mlp)
    sums_att = sum_second(ids, (here_x, there_x, got_x), (here_y, there_y, got_y))
    keep, send = call(
        give_kernel,
        [((4, PAD, 1024), BF16)] * 2,
        ids,
        slots,
        here,
        away,
        scratch=[((8, 1024), F32), ((8, 1024), F32), (plain, F32)],
    )
    got, *pairs = to_chips(keep, send)
    *pairs, whole_x, other_x, whole_y, other_y = tie(*pairs, *sums_att)
    parts = keep, got, *over_chips(pairs)
    *sums_att, moved_att = sum_third(ids, send_second(whole_x, other_x, whole_y, other_y))
    moved_att = swap(moved_att, Z_HIGH)
    input_grad, grad_gains, grad_biases, grad_last, grad_qv, grad_b_fc1 = call(
        take_kernel,
        [
            ((count, 1024), F32),
            ((2, 32), F32),
            ((4, 32), F32),
            ((1, 32), F32),
            ((8, 8), F32),
            ((1, 128), F32),
        ],
        ids,
        *parts,
        scratch=[((8, PAD, 1024), F32)],
    )
    (layer_out,) = call(
        take_out_kernel,
        [((count, 1024), BF16)],
        ids,
        *parts_out,
        scratch=[((8, PAD, 1024), F32), wide],
    )
    grad_fc1, grad_fc2 = call(
        finish_mlp_kernel,
        [((128, 1024), F32), ((1024, 128), F32)],
        ids,
        *sums_mlp,
        moved_mlp,
    )
    moved_att, _ = tie(moved_att, input_grad)
    grad_w, grad_proj = call(
        finish_att_kernel,
        [((3, 128, 256), F32), ((256, 128), F32)],
        ids,
        *sums_att,
        moved_att,
    )
    return (
        layer_out,
        input_grad,
        grad_gains,
        grad_biases,
        grad_w,
        grad_qv.reshape(2, 4, 8),
        grad_proj,
        grad_fc1,
        grad_b_fc1,
        grad_fc2,
        grad_last[0],
    )


def solution(mesh):
    spread = (mesh.shape["dp"], mesh.shape["tensor"]) == (8, 4)
    in_specs = (
        P(("dp", "tensor"), None),
        P(("dp", "tensor"), None),
        P("dp"),
        P(None, ("dp", "tensor")),
        P(None, ("dp", "tensor")),
        P(None, "dp", "tensor"),
        P(None, "tensor", "dp"),
        P("tensor", "dp"),
        P("dp", "tensor"),
        P("tensor", "dp"),
        P("tensor", "dp"),
    )
    out_specs = (
        P(("dp", "tensor"), None),
        P(("dp", "tensor"), None),
        P(None, ("dp", "tensor")),
        P(None, ("dp", "tensor")),
        P(None, "dp", "tensor"),
        P(None, "tensor", "dp"),
        P("tensor", "dp"),
        P("dp", "tensor"),
        P("tensor", "dp"),
        P("tensor", "dp"),
        P(("dp", "tensor")),
    )
    return jax.shard_map(
        on_device_spread if spread else on_device, mesh=mesh, in_specs=in_specs, out_specs=out_specs, check_vma=False
    )
```

```python
import math

import jax
import jax.numpy as jnp
from jax import lax
from jax.experimental import pallas as pl
from jax.experimental.pallas import tpu as pltpu
from jax.sharding import PartitionSpec as P

HD = 64


norm_eps = 1e-06
root_half = 0.7071067811865476
inv_root_tau = 0.3989422804014327


def normalize(values, gain_row, shift_row):
    centre = jnp.mean(values, axis=1, keepdims=True)
    offsets = values - centre
    inverse = lax.rsqrt(jnp.mean(offsets * offsets, axis=1, keepdims=True) + norm_eps)
    scaled = offsets * inverse
    return (scaled * gain_row + shift_row, scaled, inverse)


def normalize_back(upstream, scaled, inverse, gain_row):
    grad_hat = upstream * gain_row
    return (
        grad_hat
        - jnp.mean(grad_hat, axis=1, keepdims=True)
        - scaled * jnp.mean(grad_hat * scaled, axis=1, keepdims=True)
    ) * inverse


def gelu_value(inputs):
    return 0.5 * inputs * (1.0 + lax.erf(inputs * root_half))


def gelu_slope(inputs):
    return (
        0.5 * (1.0 + lax.erf(inputs * root_half))
        + inputs * jnp.exp(-0.5 * inputs * inputs) * inv_root_tau
    )


def fetch(qkv_weight, proj_weight, fc1_weight, fc2_weight, qv_bias, fc1_bias, gain_rows, bias_rows):
    matrices = (
        lax.all_gather(qkv_weight, "dp", axis=1, tiled=True),
        lax.all_gather(proj_weight, "dp", axis=1, tiled=True),
        lax.all_gather(fc1_weight, "dp", axis=0, tiled=True),
        lax.all_gather(fc2_weight, "dp", axis=1, tiled=True),
        lax.all_gather(qv_bias, "dp", axis=2, tiled=True),
        lax.all_gather(fc1_bias, "dp", axis=1, tiled=True),
    )
    vectors = (
        lax.all_gather(gain_rows, ("dp", "tensor"), axis=1, tiled=True),
        lax.all_gather(bias_rows, ("dp", "tensor"), axis=1, tiled=True),
    )
    return (matrices, (vectors[0].astype(jnp.float32), vectors[1].astype(jnp.float32)))


def spread_rows(local_rows):
    return lax.all_gather(local_rows, "tensor", axis=0, tiled=True)


def reduce_rows(term_fn, row_count):
    return lax.psum_scatter(
        term_fn(jnp.int32(0), lax.axis_size("tensor") * row_count),
        "tensor",
        scatter_dimension=0,
        tiled=True,
    )


def spread_grads(local_rows):
    return lax.all_gather(local_rows, "tensor", axis=0, tiled=True)


def reduce_grads(term_fn, row_count):
    return lax.psum_scatter(
        term_fn(jnp.int32(0), lax.axis_size("tensor") * row_count),
        "tensor",
        scatter_dimension=0,
        tiled=True,
    )


def forward(clip_rows, matrices, vectors):
    w_qkv, w_proj, w_fc1, w_fc2, b_qv, b_fc1 = matrices
    gain_rows, bias_rows = vectors
    row_count = clip_rows.shape[0]
    head_cols = w_qkv.shape[2]
    heads_here = head_cols // HD
    score_scale = 1.0 / math.sqrt(HD)
    inputs = clip_rows.astype(jnp.float32)
    normed_one, scaled_one, inverse_one = normalize(inputs, gain_rows[0], bias_rows[0])
    whole_one = spread_rows(normed_one.astype(jnp.bfloat16))
    seq_len = whole_one.shape[0]
    projected = jnp.einsum("sd,jde->jse", whole_one, w_qkv, preferred_element_type=jnp.float32)
    bias_cols = b_qv.reshape(2, head_cols).astype(jnp.float32)
    queries = (projected[0] + bias_cols[0]).astype(jnp.bfloat16).reshape(seq_len, heads_here, HD)
    keys_all = projected[1].astype(jnp.bfloat16).reshape(seq_len, heads_here, HD)
    values_all = (projected[2] + bias_cols[1]).astype(jnp.bfloat16).reshape(seq_len, heads_here, HD)
    scores = (
        jnp.einsum("qhd,khd->hqk", queries, keys_all, preferred_element_type=jnp.float32)
        * score_scale
    )
    top_score = jnp.max(scores, axis=2, keepdims=True)
    weights_exp = jnp.exp(scores - top_score)
    totals = jnp.sum(weights_exp, axis=2, keepdims=True)
    attn_probs = (weights_exp / totals).astype(jnp.bfloat16)
    log_total = top_score + jnp.log(totals)
    attended = (
        jnp.einsum("hqk,khd->qhd", attn_probs, values_all, preferred_element_type=jnp.float32)
        .reshape(seq_len, head_cols)
        .astype(jnp.bfloat16)
    )

    def proj_term(offset, length):
        return jnp.dot(attended, w_proj, preferred_element_type=jnp.float32)

    residual_one = inputs + (reduce_rows(proj_term, row_count) + bias_rows[2])
    normed_two, scaled_two, inverse_two = normalize(residual_one, gain_rows[1], bias_rows[1])
    whole_two = spread_rows(normed_two.astype(jnp.bfloat16))
    pre_act = jnp.dot(whole_two, w_fc1, preferred_element_type=jnp.float32) + b_fc1.reshape(
        -1
    ).astype(jnp.float32)
    hidden = gelu_value(pre_act).astype(jnp.bfloat16)

    def fc2_term(offset, length):
        return jnp.dot(hidden, w_fc2, preferred_element_type=jnp.float32)

    layer_out = residual_one + (reduce_rows(fc2_term, row_count) + bias_rows[3])
    stored = (
        scaled_one,
        inverse_one,
        whole_one,
        queries,
        keys_all,
        values_all,
        log_total,
        attended,
        scaled_two,
        inverse_two,
        whole_two,
        pre_act,
        hidden,
    )
    return (layer_out, stored)


def backward(upstream, matrices, vectors, stored):
    w_qkv, w_proj, w_fc1, w_fc2, b_qv, b_fc1 = matrices
    gain_rows, bias_rows = vectors
    (
        scaled_one,
        inverse_one,
        whole_one,
        queries,
        keys_all,
        values_all,
        log_total,
        attended,
        scaled_two,
        inverse_two,
        whole_two,
        pre_act,
        hidden,
    ) = stored
    row_count = upstream.shape[0]
    seq_len = queries.shape[0]
    heads_here = queries.shape[1]
    head_cols = heads_here * HD
    score_scale = 1.0 / math.sqrt(HD)
    grad_mlp = upstream.astype(jnp.bfloat16)
    grad_fc2_bias = jnp.sum(grad_mlp.astype(jnp.float32), axis=0)
    whole_mlp = spread_grads(grad_mlp)
    grad_fc2 = jnp.einsum("sf,sd->fd", hidden, whole_mlp, preferred_element_type=jnp.float32)
    grad_hidden = jnp.einsum("sd,fd->sf", whole_mlp, w_fc2, preferred_element_type=jnp.float32)
    grad_pre = (grad_hidden * gelu_slope(pre_act)).astype(jnp.bfloat16)
    grad_fc1_bias = jnp.sum(grad_pre.astype(jnp.float32), axis=0)
    grad_fc1 = jnp.einsum("sd,sf->df", whole_two, grad_pre, preferred_element_type=jnp.float32)

    def fc1_back(offset, length):
        return jnp.einsum("sf,df->sd", grad_pre, w_fc1, preferred_element_type=jnp.float32)

    grad_normed_two = reduce_grads(fc1_back, row_count)
    grad_residual = upstream + normalize_back(
        grad_normed_two, scaled_two, inverse_two, gain_rows[1]
    )
    grad_branch = grad_residual.astype(jnp.bfloat16)
    grad_proj_bias = jnp.sum(grad_branch.astype(jnp.float32), axis=0)
    whole_branch = spread_grads(grad_branch)
    grad_proj = jnp.einsum("se,sd->ed", attended, whole_branch, preferred_element_type=jnp.float32)
    grad_att = (
        jnp.einsum("sd,ed->se", whole_branch, w_proj, preferred_element_type=jnp.float32)
        .astype(jnp.bfloat16)
        .reshape(seq_len, heads_here, HD)
    )
    scores = (
        jnp.einsum("qhd,khd->hqk", queries, keys_all, preferred_element_type=jnp.float32)
        * score_scale
    )
    attn_probs = jnp.exp(scores - log_total)
    grad_probs = jnp.einsum(
        "qhd,khd->hqk", grad_att, values_all, preferred_element_type=jnp.float32
    )
    row_dot = jnp.sum(attn_probs * grad_probs, axis=2, keepdims=True)
    grad_scores = (attn_probs * (grad_probs - row_dot)).astype(jnp.bfloat16)
    grad_query = (
        jnp.einsum("hqk,khd->qhd", grad_scores, keys_all, preferred_element_type=jnp.float32)
        * score_scale
    ).astype(jnp.bfloat16)
    grad_key = (
        jnp.einsum("hqk,qhd->khd", grad_scores, queries, preferred_element_type=jnp.float32)
        * score_scale
    ).astype(jnp.bfloat16)
    grad_value = jnp.einsum(
        "hqk,qhd->khd",
        attn_probs.astype(jnp.bfloat16),
        grad_att,
        preferred_element_type=jnp.float32,
    ).astype(jnp.bfloat16)
    grad_qkv = jnp.stack([grad_query, grad_key, grad_value]).reshape(3, seq_len, head_cols)
    grad_qv = jnp.stack(
        [
            jnp.sum(grad_query.astype(jnp.float32), axis=0),
            jnp.sum(grad_value.astype(jnp.float32), axis=0),
        ]
    )
    grad_qkv_weight = jnp.einsum(
        "sd,jse->jde", whole_one, grad_qkv, preferred_element_type=jnp.float32
    )

    def qkv_back(offset, length):
        return jnp.einsum("jse,jde->sd", grad_qkv, w_qkv, preferred_element_type=jnp.float32)

    grad_normed_one = reduce_grads(qkv_back, row_count)
    grad_input = grad_residual + normalize_back(
        grad_normed_one, scaled_one, inverse_one, gain_rows[0]
    )
    grad_gain = jnp.stack(
        [
            jnp.sum(grad_normed_one * scaled_one, axis=0),
            jnp.sum(grad_normed_two * scaled_two, axis=0),
        ]
    )
    grad_bias = jnp.stack(
        [
            jnp.sum(grad_normed_one, axis=0),
            jnp.sum(grad_normed_two, axis=0),
            grad_proj_bias,
            grad_fc2_bias,
        ]
    )
    weight_part = (
        lax.psum_scatter(grad_qkv_weight, "dp", scatter_dimension=1, tiled=True),
        lax.psum_scatter(grad_proj, "dp", scatter_dimension=1, tiled=True),
        lax.psum_scatter(grad_fc1, "dp", scatter_dimension=0, tiled=True),
        lax.psum_scatter(grad_fc2, "dp", scatter_dimension=1, tiled=True),
        lax.psum_scatter(grad_qv, "dp", scatter_dimension=2, tiled=True),
        lax.psum_scatter(grad_fc1_bias.reshape(1, -1), "dp", scatter_dimension=1, tiled=True),
    )
    vector_part = (
        lax.psum_scatter(grad_gain, ("dp", "tensor"), scatter_dimension=1, tiled=True),
        lax.psum_scatter(grad_bias, ("dp", "tensor"), scatter_dimension=1, tiled=True),
    )
    return (grad_input, weight_part, vector_part)


def on_device(
    clip_rows,
    out_grad,
    clip_valid,
    gain_rows,
    bias_rows,
    qkv_weight,
    qv_bias,
    proj_weight,
    fc1_weight,
    fc1_bias,
    fc2_weight,
):
    clip_weight = clip_valid[0].astype(jnp.float32)
    upstream = out_grad.astype(jnp.float32) * clip_weight
    matrices, vectors = fetch(
        qkv_weight, proj_weight, fc1_weight, fc2_weight, qv_bias, fc1_bias, gain_rows, bias_rows
    )
    layer_out, stored = forward(clip_rows, matrices, vectors)
    matrices, vectors = fetch(
        qkv_weight, proj_weight, fc1_weight, fc2_weight, qv_bias, fc1_bias, gain_rows, bias_rows
    )
    unused_out, stored = forward(clip_rows, matrices, vectors)
    grad_input, weight_part, vector_part = backward(upstream, matrices, vectors, stored)
    return (
        (layer_out * clip_weight).astype(jnp.bfloat16),
        grad_input,
        vector_part[0],
        vector_part[1],
        weight_part[0],
        weight_part[4],
        weight_part[1],
        weight_part[2],
        weight_part[5],
        weight_part[3],
        vector_part[1][3],
    )


AXES = ("dp", "tensor")
Z_LOW, Z_HIGH, CORE, X, Y = 1, 2, 4, 8, 16
CHIP_MASKS = (0, X, Y, X | Y)
BF16, F32 = jnp.bfloat16, jnp.float32
NN, NT, TN = ((1,), (0,)), ((1,), (1,)), ((0,), (0,))
SHARE = 49
PAD = 56
SMALL = 104
CHIP_ID, CORE_ID, D_ID, T_ID = range(4)


def swap(value, mask):
    return lax.ppermute(value, AXES, [(i, i ^ mask) for i in range(32)])


def dot(left, right, dims):
    return lax.dot_general(left, right, (dims, ((), ())), preferred_element_type=F32)


TIMES = {
    "pack": 1.2,
    "pick": 1.5,
    "norm_one": 1.0,
    "qkv": 1.6,
    "attention": 7.6,
    "proj": 1.1,
    "norm_two": 0.9,
    "grad_hidden": 1.6,
    "fc": 5.6,
    "grads_fc1": 1.8,
    "grads_fc2": 1.8,
    "fc2": 1.6,
    "norm_two_back": 1.5,
    "grad_att": 1.1,
    "attention_back": 12.0,
    "qkv_back": 1.5,
    "half_grad": 1.1,
    "grads_att": 1.8,
    "norm_one_back": 1.0,
    "give": 1.3,
    "take": 2.0,
    "finish_mlp": 1.7,
    "finish_att": 1.4,
}


SPACE = {"attention_kernel": 16, "attention_back_kernel": 12}


def call(body, outs, scalars, *args, scratch=()):
    moved = sum(math.prod(a.shape) * a.dtype.itemsize for a in args)
    moved += sum(math.prod(s) * jnp.dtype(t).itemsize for s, t in outs)
    held = sum(math.prod(s[:-1]) * max(s[-1], 128) * jnp.dtype(t).itemsize for s, t in scratch)
    time = TIMES.get(body.__name__.removesuffix("_kernel"), 0.7)
    return pl.pallas_call(
        body,
        out_shape=[jax.ShapeDtypeStruct(s, t) for s, t in outs],
        in_specs=[pl.BlockSpec(memory_space=pltpu.SMEM)]
        + [pl.BlockSpec(memory_space=pltpu.VMEM)] * len(args),
        out_specs=[pl.BlockSpec(memory_space=pltpu.VMEM)] * len(outs),
        scratch_shapes=[pltpu.VMEM(s, t) for s, t in scratch],
        compiler_params=pltpu.CompilerParams(vmem_limit_bytes=moved + held + (SPACE.get(body.__name__, 4) << 20)),
        cost_estimate=pl.CostEstimate(
            flops=int(time * 1.15e9), bytes_accessed=moved, transcendentals=0
        ),
    )(scalars, *args)


def chip_lanes(ids, m):
    return pl.ds(pl.multiple_of((ids[CHIP_ID] ^ m) * 256, 256), 256)


def lanes(m):
    return slice(256 * m, 256 * m + 256)


def row_ids(shape):
    return lax.broadcasted_iota(jnp.int32, shape, 0)


def pick(condition, left, right):
    return jnp.where(jnp.full(left.shape, condition, jnp.int32) != 0, left, right)


def is_zero(number):
    return jnp.where(number == 0, 1, 0)


def z_low(ids):
    return ids[T_ID] & 1


def z_high(ids):
    return ids[T_ID] >> 1


def far_chips(ids, core_flip):
    return [(ids[CHIP_ID] ^ m) * 2 + (ids[CORE_ID] ^ core_flip) for m in range(4)]


def pack_kernel(ids, rows, grads, params, keep, send, wide, stage):
    lane32 = lax.broadcasted_iota(jnp.int32, (32, 128), 1)
    spot = (lane32 == row_ids((32, 128)) + 32 * ids[T_ID]).astype(F32).astype(BF16)
    lane8 = lax.broadcasted_iota(jnp.int32, (8, 128), 1)
    spot8 = (lane8 == row_ids((8, 128)) + 8 * ids[D_ID]).astype(F32).astype(BF16)
    placed = dot(params[0:8, 0:32], spot, NN)
    qv_rows = dot(params[8:16, 0:8], spot8, NN)
    row_a = jnp.concatenate(
        [placed[k : k + 1] for k in range(6)]
        + [params[...].astype(F32)[16:17], jnp.zeros((1, 128), F32)],
        axis=1,
    )
    row_b = jnp.concatenate([qv_rows[k : k + 1] for k in range(8)], axis=1)
    flag = jnp.full((PAD, 1024), ids[4], jnp.int32).astype(F32)
    row = row_ids((PAD, 1024))
    tail = jnp.where(row == SHARE, row_a, jnp.where(row == SHARE + 1, row_b, flag))
    wide[0 : rows.shape[0], :] = rows[...].astype(F32)
    for j in range(8):
        block = wide[SHARE * j : SHARE * j + PAD, :]
        stage[j, 0:PAD, :] = jnp.where(row < SHARE, block, tail).astype(BF16)
    wide[0 : rows.shape[0], :] = grads[...].astype(F32)
    for j in range(8):
        stage[j, PAD : 2 * PAD, :] = wide[SHARE * j : SHARE * j + PAD, :].astype(BF16)
    for m, (d0, d1) in enumerate(zip(far_chips(ids, 0), far_chips(ids, 1))):
        keep[m, :, :] = stage[d0, :, :]
        send[m, :, :] = stage[d1, :, :]


def pair_up_kernel(ids, keep, got, o1, o2, o3):
    for m, out in enumerate((o1, o2, o3)):
        out[0, :, :] = keep[m + 1, :, :]
        out[1, :, :] = got[m + 1, :, :]


def arrived(ids, keep, got, d1, d2, d3):
    parts = []
    for m, (a0, a1) in enumerate(zip(far_chips(ids, 0), far_chips(ids, 1))):
        first, second = ((keep, 0), (got, 0)) if m == 0 else (((d1, d2, d3)[m - 1], k) for k in range(2))
        parts += [(a0, *first), (a1, *second)]
    return parts


def pick_kernel(ids, keep, got, d1, d2, d3, here, there, here_grad, there_grad, slots):
    row8 = row_ids((8, 1024))
    row = row_ids((PAD, 1024))
    mine = jnp.zeros((PAD, 1024), F32)
    other, mine_grad, other_grad = mine, mine, mine
    params = jnp.zeros((8, 1024), F32)
    qv = jnp.zeros((1, 1024), F32)
    high = jnp.full((1, 1024), z_high(ids), jnp.int32).astype(F32)
    parts = arrived(ids, keep, got, d1, d2, d3)
    flags = [
        ref[k, PAD - 8 : PAD, :].astype(F32)[SHARE + 10 - PAD : SHARE + 11 - PAD]
        for _, ref, k in parts
    ]
    for i, (a, ref, k) in enumerate(parts):
        seen = jnp.zeros((1, 1024), F32)
        for (c, _, _), flag in zip(parts, flags):
            earlier = jnp.full((1, 1024), jnp.where(c < a, 1, 0), jnp.int32).astype(F32)
            seen = seen + flag * earlier
        block = ref[k, 0:PAD, :].astype(F32)
        grad = ref[k, PAD : 2 * PAD, :].astype(F32)
        is_mine = jnp.where(seen == high, flags[i], 0.0)
        is_other = flags[i] - is_mine
        mine = jnp.where(is_mine > 0.5, block, mine)
        other = jnp.where(is_other > 0.5, block, other)
        mine_grad = jnp.where(is_mine > 0.5, grad, mine_grad)
        other_grad = jnp.where(is_other > 0.5, grad, other_grad)
        params = jnp.where(row8 == a, block[SHARE : SHARE + 1], params)
        qv = qv + block[SHARE + 1 : SHARE + 2]
        slots[a, :, :] = jnp.broadcast_to(is_mine[:, 0:128], (8, 128))
        slots[8 + a, :, :] = jnp.broadcast_to(is_other[:, 0:128], (8, 128))
    for value, out in ((mine, here), (other, there)):
        out[0:PAD, :] = jnp.where(row == PAD - 1, qv, value).astype(BF16)
        out[PAD : PAD + 8, :] = params.astype(BF16)
    here_grad[...] = mine_grad.astype(BF16)
    there_grad[...] = other_grad.astype(BF16)


def lay_rows(ids, here, r1, r2, r3, wide):
    low = is_zero(z_low(ids))
    for m in range(4):
        cols = chip_lanes(ids, m)
        blocks = [ref[0:PAD, cols].astype(F32) for ref in (here, r1, r2, r3)]
        order = (
            pick(low, blocks[0], blocks[1]),
            pick(low, blocks[2], blocks[3]),
            pick(low, blocks[1], blocks[0]),
            pick(low, blocks[3], blocks[2]),
        )
        for i, block in enumerate(order):
            wide[SHARE * i : SHARE * i + SHARE, lanes(m)] = block[0:SHARE]


def norm_parts(values):
    centre = jnp.mean(values, axis=1, keepdims=True)
    offsets = values - centre
    inverse = lax.rsqrt(jnp.mean(offsets * offsets, axis=1, keepdims=True) + norm_eps)
    return offsets * inverse, inverse


def norm_one_kernel(ids, here, r1, r2, r3, rows, normed, vec, qv_bias, b_fc1, wide, small):
    lay_rows(ids, here, r1, r2, r3, wide)
    own = here[PAD - 8 : PAD + 8, :].astype(F32)
    far = r2[PAD - 8 : PAD + 8, :].astype(F32)
    tails = [own[8:], far[8:]] + [r[PAD : PAD + 8, :].astype(F32) for r in (r1, r3)]
    params = tails[0] + tails[1] + tails[2] + tails[3]
    small[...] = jnp.zeros_like(small)
    for d in range(8):
        for k in range(6):
            small[k : k + 1, 128 * d : 128 * d + 128] = params[
                d : d + 1, 128 * k : 128 * k + 128
            ]
    for m in range(4):
        vec[:, lanes(m)] = small[:, chip_lanes(ids, m)]
    home = pick(is_zero(ids[CORE_ID]), own, far)
    for k in range(8):
        qv_bias[k : k + 1, :] = home[7:8, 128 * k : 128 * k + 128]
        b_fc1[0:1, 128 * k : 128 * k + 128] = home[8 + k : 9 + k, 768:896]
    values = wide[...]
    scaled, _ = norm_parts(values)
    rows[...] = values.astype(BF16)
    normed[...] = (scaled * vec[0:1, :] + vec[2:3, :]).astype(BF16)


def lay_grad_kernel(ids, here, r1, r2, r3, out, wide):
    lay_rows(ids, here, r1, r2, r3, wide)
    out[...] = wide[...].astype(BF16)


def join_rows(wide, own, got):
    half = own.shape[0]
    wide[0:half, :] = own[...].astype(F32)
    wide[half : 2 * half, :] = got[...].astype(F32)


PROJ = 3


def part_of(weights, m, j):
    if m < 3:
        return weights[m][:, lanes(j)]
    return weights[3 + j // 2][:, lanes(j % 2)]


VALUES = 400


def fold_rows(value):
    half = value.shape[0] // 2
    return jnp.concatenate([value[:half], value[half:]], axis=1)


def qkv_kernel(ids, own, got, qv_bias, w0, w1, w2, w3, w4, whole, o0, o1, o2, o3, wide, heads):
    weights = (w0, w1, w2, w3, w4)
    join_rows(wide, own, got)
    whole[...] = wide[...].astype(BF16)
    for j in range(3):
        total = dot(whole[:, lanes(0)], w0[:, lanes(j)], NN)
        for m in range(1, 4):
            total = total + dot(whole[:, lanes(m)], part_of(weights, m, j), NN)
        for h in range(4):
            part = total[:, 64 * h : 64 * h + 64]
            if j != 1:
                k = (j // 2) * 4 + h
                part = part + qv_bias[k : k + 1, 0:64]
            if j < 2:
                heads[h, 0 : part.shape[0], 64 * j : 64 * j + 64] = part.astype(BF16)
            else:
                heads[h, VALUES:, :] = fold_rows(part).astype(BF16)
    for m, out in enumerate((o0, o1, o2, o3)):
        out[...] = heads[ids[CHIP_ID] ^ m, :, :]


STEP, BACK_STEP = 392, 112


def stage_qkv(stage, parts):
    tokens = stage.shape[0] // 4
    half = tokens // 2
    for m, part in enumerate(parts):
        start = tokens * m
        stage[start : start + tokens, 0:128] = part[0:tokens, :].astype(F32)
        stage[start : start + half, 128:192] = part[VALUES:, 0:64].astype(F32)
        stage[start + half : start + tokens, 128:192] = part[VALUES:, 64:128].astype(F32)


def attention_kernel(ids, a0, a1, a2, a3, o0, o1, o2, o3, back, stage, q, k, v):
    tokens = stage.shape[0] // 4
    stage_qkv(stage, (a0, a1, a2, a3))
    q[...] = (stage[:, 0:64] * 0.125).astype(BF16)
    k[...] = stage[:, 64:128].astype(BF16)
    v[:, 0:64] = stage[:, 128:192].astype(BF16)
    v[:, 64:128] = jnp.ones((v.shape[0], 64), BF16)
    for i in range(stage.shape[0] // STEP):
        rows = slice(i * STEP, i * STEP + STEP)
        scores = dot(q[rows, :], k[...], NT)
        top = jnp.max(scores, axis=1, keepdims=True)
        mixed = dot(jnp.exp(scores - top).astype(BF16), v[...], NN)
        total = mixed[:, 64:128]
        back[rows, 0:64] = mixed[:, 0:64] / total
        back[rows, 64:128] = top + jnp.log(total)
    for m, out in enumerate((o0, o1, o2, o3)):
        out[...] = fold_rows(back[tokens * m : tokens * m + tokens, 0:64]).astype(BF16)


def with_shift(value, shift):
    high = shift.astype(BF16).astype(F32)
    middle = (shift - high).astype(BF16).astype(F32)
    low = shift - high - middle
    lane = lax.broadcasted_iota(jnp.int32, (value.shape[0], 64), 1)
    extra = jnp.where(lane == 0, -high, jnp.where(lane == 1, -middle, jnp.where(lane == 2, -low, 0.0)))
    return jnp.concatenate([value, extra], axis=1).astype(BF16)


def with_ones(value):
    lane = lax.broadcasted_iota(jnp.int32, (value.shape[0], 64), 1)
    return jnp.concatenate([value, jnp.where(lane < 3, 1.0, 0.0)], axis=1).astype(BF16)


def attention_back_kernel(
    ids, a0, a1, a2, a3, g0, g1, g2, g3, back, o0, o1, o2, o3, stage, q, k, v, g, grad_k, grad_v
):
    tokens = stage.shape[0] // 4
    stage_qkv(stage, (a0, a1, a2, a3))
    q[...] = with_shift(stage[:, 0:64] * 0.125, back[:, 64:65])
    k[...] = with_ones(stage[:, 64:128])
    v[...] = with_ones(stage[:, 128:192])
    for m, part in enumerate((g0, g1, g2, g3)):
        middle = tokens * m + tokens // 2
        stage[tokens * m : middle, 0:64] = part[:, 0:64].astype(F32)
        stage[middle : tokens * m + tokens, 0:64] = part[:, 64:128].astype(F32)
    grads = stage[:, 0:64]
    g[...] = with_shift(grads, jnp.sum(grads * back[:, 0:64], axis=1, keepdims=True))
    keys_t = jnp.transpose(k[:, 0:64])
    for i in range(stage.shape[0] // BACK_STEP):
        rows = slice(i * BACK_STEP, i * BACK_STEP + BACK_STEP)
        probs = jnp.exp(dot(k[...], q[rows, :], NT))
        grad_scores = (probs * dot(v[...], g[rows, :], NT)).astype(BF16)
        part_v = dot(probs.astype(BF16), g[rows, 0:64], NN)
        part_k = dot(grad_scores, q[rows, 0:64], NN)
        grad_v[...] = part_v if i == 0 else grad_v[...] + part_v
        grad_k[...] = part_k if i == 0 else grad_k[...] + part_k
        stage[rows, 0:64] = jnp.transpose(dot(keys_t, grad_scores, NN)) * 0.125
    for m, out in enumerate((o0, o1, o2, o3)):
        rows = slice(tokens * m, tokens * m + tokens)
        out[0:tokens, 0:64] = stage[rows, 0:64].astype(BF16)
        out[0:tokens, 64:128] = grad_k[rows, :].astype(BF16)
        out[VALUES:, :] = fold_rows(grad_v[rows, :]).astype(BF16)


def split_rows(total, keep, send, cols):
    half = keep.shape[0]
    keep[:, cols] = total[:half]
    send[:, cols] = total[half:].astype(BF16)


def proj_kernel(ids, a0, a1, a2, a3, w0, w1, w2, w3, w4, joined, keep, send, heads, wide):
    for m, part in enumerate((a0, a1, a2, a3)):
        heads[m, :, :] = part[...]
    half = keep.shape[0]
    for h in range(4):
        part = heads[h ^ ids[CHIP_ID], :, :].astype(F32)
        wide[0:half, 64 * h : 64 * h + 64] = part[:, 0:64]
        wide[half:, 64 * h : 64 * h + 64] = part[:, 64:128]
    joined[...] = wide[...].astype(BF16)
    for m in range(4):
        weight = part_of((w0, w1, w2, w3, w4), m, PROJ)
        split_rows(dot(joined[...], weight, NT), keep, send, lanes(m))


def pair_kernel(ids, keep, got, part, send):
    total = keep[...] + got[...].astype(F32)
    part[...] = total
    send[...] = total.astype(BF16)


def half_kernel(ids, keep, got, part, send):
    own = part.shape[0]
    total = keep[...] + got[...].astype(F32)
    low = is_zero(z_low(ids))
    part[...] = pick(low, total[:own], total[own:])
    send[...] = pick(low, total[own:], total[:own]).astype(BF16)


def half_grad_kernel(ids, keep, got, rows, sums_two, sums_fc1, sums_qv, part, send, small):
    own = part.shape[0]
    total = keep[...] + got[...].astype(F32)
    low = is_zero(z_low(ids))
    part[...] = pick(low, total[:own], total[own:])
    scaled, _ = norm_parts(rows[...].astype(F32))
    send[0:own, :] = pick(low, total[own:], total[:own]).astype(BF16)
    sums = jnp.concatenate(
        [
            jnp.sum(total * scaled, axis=0, keepdims=True),
            sums_two[0:1, :],
            jnp.sum(total, axis=0, keepdims=True),
            sums_two[1:4, :],
            sums_qv[...],
            sums_fc1[...],
        ],
        axis=0,
    )
    small[...] = sums
    send[SMALL : SMALL + 8, :] = sums.astype(BF16)


def norm_two_kernel(ids, rows, part, got, vec, residual, normed):
    total = rows[...].astype(F32) + (part[...] + got[...].astype(F32) + vec[4:5, :])
    residual[...] = total
    scaled, _ = norm_parts(total)
    normed[...] = (scaled * vec[1:2, :] + vec[3:4, :]).astype(BF16)


def grad_hidden_kernel(ids, own, got, w0, w1, w2, w3, whole, out, wide):
    join_rows(wide, own, got)
    whole[...] = wide[...].astype(BF16)
    for c in range(4):
        total = dot(whole[:, lanes(0)], w0[:, lanes(c)], NN)
        for m, weight in enumerate((w1, w2, w3)):
            total = total + dot(whole[:, lanes(m + 1)], weight[:, lanes(c)], NN)
        out[:, lanes(c)] = total


def fc_kernel(
    ids, own, got, grad_hidden, b_fc1, w0, w1, w2, w3, whole, hidden, grad_pre, sums, keep, send, wide
):
    weights = (w0, w1, w2, w3)
    join_rows(wide, own, got)
    whole[...] = wide[...].astype(BF16)
    wide[...] = jnp.zeros_like(wide)

    def body(c, carry):
        cols = pl.ds(pl.multiple_of(c * 256, 256), 256)
        pre = b_fc1[:, cols] + dot(whole[:, lanes(0)], w0[:, cols], NN)
        for m in range(1, 4):
            pre = pre + dot(whole[:, lanes(m)], weights[m][:, cols], NN)
        half_erf = 0.5 * (1.0 + lax.erf(pre * root_half))
        hidden[:, cols] = (pre * half_erf).astype(BF16)
        slope = half_erf + pre * jnp.exp(-0.5 * pre * pre) * inv_root_tau
        grad = (grad_hidden[:, cols] * slope).astype(BF16)
        grad_pre[:, cols] = grad
        sums[:, cols] = jnp.sum(grad.astype(F32), axis=0, keepdims=True)
        for m in range(4):
            wide[:, lanes(m)] += dot(grad, weights[m][:, cols], NT)
        return carry

    lax.fori_loop(0, 4, body, 0)
    for m in range(4):
        split_rows(wide[:, lanes(m)], keep, send, lanes(m))


def norm_back(total, scaled, inverse, gain):
    hat = total * gain
    return (
        hat
        - jnp.mean(hat, axis=1, keepdims=True)
        - scaled * jnp.mean(hat * scaled, axis=1, keepdims=True)
    ) * inverse


def norm_two_back_kernel(ids, residual, part, got, grads, vec, grad_residual, grad_branch, sums):
    scaled, inverse = norm_parts(residual[...])
    total = part[...] + got[...].astype(F32)
    upstream = grads[...].astype(F32)
    result = upstream + norm_back(total, scaled, inverse, vec[1:2, :])
    branch = result.astype(BF16)
    grad_residual[...] = result
    grad_branch[...] = branch
    own = total.shape[0] // 2
    row = row_ids(total.shape)
    low = jnp.full(total.shape, z_low(ids), jnp.int32)
    mine = jnp.where(row < own, 1 - low, low) != 0

    def column_sum(value):
        return jnp.sum(jnp.where(mine, value, 0.0), axis=0, keepdims=True)

    sums[0:1, :] = column_sum(total * scaled)
    sums[1:2, :] = column_sum(total)
    sums[2:3, :] = column_sum(branch.astype(F32))
    sums[3:4, :] = column_sum(upstream)
    sums[4:8, :] = jnp.zeros((4, sums.shape[1]), F32)


def grad_att_kernel(ids, own, got, w0, w1, w2, w3, w4, whole, o0, o1, o2, o3, wide, heads):
    join_rows(wide, own, got)
    whole[...] = wide[...].astype(BF16)
    weights = (w0, w1, w2, w3, w4)
    total = dot(whole[:, lanes(0)], w0[:, lanes(PROJ)], NN)
    for m in range(1, 4):
        total = total + dot(whole[:, lanes(m)], part_of(weights, m, PROJ), NN)
    for h in range(4):
        heads[h, :, :] = fold_rows(total[:, 64 * h : 64 * h + 64]).astype(BF16)
    for m, out in enumerate((o0, o1, o2, o3)):
        out[...] = heads[ids[CHIP_ID] ^ m, :, :]


def qkv_back_kernel(ids, g0, g1, g2, g3, w0, w1, w2, w3, w4, joined, keep, send, sums, heads, wide):
    for m, part in enumerate((g0, g1, g2, g3)):
        heads[m, :, :] = part[...]
    half, tokens = keep.shape[0], joined.shape[0]
    for h in range(4):
        part = heads[h ^ ids[CHIP_ID], :, :]
        for j in range(2):
            joined[:, 256 * j + 64 * h : 256 * j + 64 * h + 64] = part[
                0:tokens, 64 * j : 64 * j + 64
            ]
        values = part[VALUES:, :].astype(F32)
        wide[0:half, 64 * h : 64 * h + 64] = values[:, 0:64]
        wide[half:, 64 * h : 64 * h + 64] = values[:, 64:128]
        for k, value in ((h, part[0:tokens, 0:64]), (4 + h, wide[:, 64 * h : 64 * h + 64])):
            total = jnp.sum(value.astype(F32), axis=0, keepdims=True)
            sums[0:1, 128 * k : 128 * k + 128] = jnp.concatenate(
                [total, jnp.zeros((1, 64), F32)], axis=1
            )
    joined[:, 512:768] = wide[...].astype(BF16)
    for m in range(4):
        weights = (w0, w1, w2, w3, w4)
        total = dot(joined[:, lanes(0)], part_of(weights, m, 0), NT)
        for j in (1, 2):
            total = total + dot(joined[:, lanes(j)], part_of(weights, m, j), NT)
        split_rows(total, keep, send, lanes(m))


def to_owners(ids, value, wide, here, there):
    wide[0 : 2 * SHARE, :] = value
    wide[2 * SHARE :, :] = jnp.zeros((wide.shape[0] - 2 * SHARE, wide.shape[1]), F32)
    for m in range(4):
        cols = chip_lanes(ids, m)
        here[0:PAD, cols] = wide[0:PAD, lanes(m)].astype(BF16)
        there[0:PAD, cols] = wide[SHARE : SHARE + PAD, lanes(m)].astype(BF16)


def own_half(ids, ref):
    own = ref.shape[0] // 2
    value = ref[...].astype(F32)
    return pick(is_zero(z_low(ids)), value[:own], value[own:])


def norm_one_back_kernel(
    ids, rows, part, got, grad_residual, vec, small, here, there, wide
):
    scaled, inverse = norm_parts(own_half(ids, rows))
    total = part[...] + got[0 : 2 * SHARE, :].astype(F32)
    result = own_half(ids, grad_residual) + norm_back(total, scaled, inverse, vec[0:1, :])
    to_owners(ids, result, wide, here, there)
    far = jnp.where(row_ids((8, 1024)) < 6, got[SMALL : SMALL + 8, :].astype(F32), 0.0)
    sums = (small[...] + far).astype(BF16)
    here[PAD : PAD + 8, :] = sums
    there[PAD : PAD + 8, :] = sums


def layer_out_kernel(ids, residual, part, got, vec, here, there, wide):
    result = own_half(ids, residual) + (part[...] + got[...].astype(F32) + vec[5:6, :])
    to_owners(ids, result, wide, here, there)


def fc2_kernel(ids, hidden, w0, w1, w2, w3, keep, send):
    for m, weight in enumerate((w0, w1, w2, w3)):
        split_rows(dot(hidden[...], weight[...], NT), keep, send, lanes(m))


def for_slot(slots, d, left, right):
    value = jnp.where(slots[8 + d, 0:1, 0:1] > 0.5, right, 0.0)
    return jnp.where(slots[d, 0:1, 0:1] > 0.5, left, value)


def give_out_kernel(ids, slots, here, away, keep, send):
    left = here[...].astype(F32)
    right = away[...].astype(F32)
    for out, flip in ((keep, 0), (send, 1)):
        for m, d in enumerate(far_chips(ids, flip)):
            out[m, :, :] = for_slot(slots, d, left, right).astype(BF16)


def give_kernel(ids, slots, here, away, keep, send, rel, flat, tail):
    left = here[0:PAD, :].astype(F32)
    right = away[0:PAD, :].astype(F32)
    own = here[PAD : PAD + 8, :].astype(F32)
    far = away[PAD : PAD + 8, :].astype(F32)
    rel[...] = own + far
    home = pick(is_zero(ids[CORE_ID]), own, far)
    for m in range(4):
        flat[:, chip_lanes(ids, m)] = rel[:, lanes(m)]
    rel[0:1, :] = home[7:8]
    tail[...] = jnp.zeros_like(tail)
    for k in range(8):
        row, lane = (SHARE + k, 128) if k < 7 else (SHARE, 256)
        tail[row : row + 1, lane : lane + 128] = home[6:7, 128 * k : 128 * k + 128]
    row = row_ids((PAD, 1024))
    for out, flip in ((keep, 0), (send, 1)):
        for m, d in enumerate(far_chips(ids, flip)):
            cols = pl.ds(pl.multiple_of(d * 128, 128), 128)
            tail[SHARE : SHARE + 6, 0:128] = flat[0:6, cols]
            tail[SHARE + 6 : PAD, 0:128] = rel[0:1, cols]
            value = for_slot(slots, d, left, right)
            out[m, :, :] = jnp.where(row < SHARE, value, tail[...]).astype(BF16)


def settle_rows(parts, stage, out):
    for a, ref, k in parts:
        stage[a, :, :] = ref[k, :, :].astype(F32)
    for j in range(8):
        out[SHARE * j : SHARE * j + SHARE, :] = stage[j, 0:SHARE, :]


def take_out_kernel(ids, keep, got, d1, d2, d3, out, stage, wide):
    settle_rows(arrived(ids, keep, got, d1, d2, d3), stage, wide)
    out[...] = wide[...].astype(BF16)


def take_kernel(ids, keep, got, d1, d2, d3, out, gains, biases, last, qv, b_fc1, stage):
    parts = arrived(ids, keep, got, d1, d2, d3)
    settle_rows(parts, stage, out)
    total = jnp.zeros((8, 384), F32)
    for _, ref, k in parts:
        total = total + ref[k, PAD - 8 : PAD, 0:384].astype(F32)
    rows = pltpu.roll(total[:, 0:128], (128 - 32 * ids[T_ID]) & 127, 1)
    gains[...] = rows[1:3, 0:32]
    biases[...] = rows[3:7, 0:32]
    last[...] = rows[6:7, 0:32]
    b_fc1[...] = total[7:8, 0:128]
    pieces = jnp.concatenate([total[1:8, 128:256], total[1:2, 256:384]], axis=0)
    qv[...] = pltpu.roll(pieces, (128 - 8 * ids[D_ID]) & 127, 1)[:, 0:8]


def shards_kernel(ids, qkv, proj, fc2, first, second):
    for j in range(3):
        first[:, lanes(j)] = qkv[j, :, :]
    first[:, lanes(PROJ)] = jnp.transpose(proj[...])
    second[...] = jnp.transpose(fc2[...])


def offer_kernel(ids, own, far, send):
    @pl.when(ids[CORE_ID] == 0)
    def _():
        send[...] = far[...]

    @pl.when(ids[CORE_ID] != 0)
    def _():
        send[...] = own[...]


def merge_kernel(ids, own, far, got, out):
    half = own.shape[0]

    @pl.when(ids[CORE_ID] == 0)
    def _():
        out[0:half, :] = own[...]
        out[half:, :] = got[...]

    @pl.when(ids[CORE_ID] != 0)
    def _():
        out[0:half, :] = got[...]
        out[half:, :] = far[...]


X_FIRST, Y_FIRST = (1, 2), (2, 1)


def blocks_of(order, left, right, cols, send, here, there, out_cols):
    near, far = order
    for slot, m in ((0, near), (1, 3)):
        send[slot, :, out_cols] = dot(left[:, lanes(m)], right[:, cols], TN).astype(BF16)
    here[:, out_cols] = dot(left[:, lanes(0)], right[:, cols], TN)
    there[:, out_cols] = dot(left[:, lanes(far)], right[:, cols], TN)


def grads_fc1_kernel(ids, left, right, send, here, there):
    for c in range(2):
        cols = slice(512 * c, 512 * c + 512)
        blocks_of(X_FIRST, left, right, cols, send, here, there, cols)


def grads_fc2_kernel(ids, left, right, send, here, there):
    for c in range(2):
        cols = slice(512 * c, 512 * c + 512)
        blocks_of(Y_FIRST, left, right, cols, send, here, there, cols)


def grads_att_kernel(
    ids, rows, joined, branch, mixed, send_x, here_x, there_x, send_y, here_y, there_y
):
    blocks_of(X_FIRST, rows, joined, slice(0, 512), send_x, here_x, there_x, slice(0, 512))
    blocks_of(Y_FIRST, rows, joined, slice(512, 768), send_y, here_y, there_y, slice(0, 256))
    blocks_of(Y_FIRST, branch, mixed, slice(0, 256), send_y, here_y, there_y, slice(256, 512))


def fold_kernel(ids, here, there, got, other, whole):
    other[...] = (there[...] + got[1, :, :].astype(F32)).astype(BF16)
    whole[...] = here[...] + got[0, :, :].astype(F32)


def gather_kernel(ids, whole_x, got_x, whole_y, got_y, keep, send):
    n = whole_x.shape[1]
    for core in range(2):

        @pl.when(ids[CORE_ID] == core)
        def _():
            own = slice(128 * core, 128 * core + 128)
            other = slice(128 - 128 * core, 256 - 128 * core)
            for cols, whole, got in (
                (slice(0, n), whole_x, got_x),
                (slice(n, 2 * n), whole_y, got_y),
            ):
                for out, rows in ((keep, own), (send, other)):
                    total = whole[rows, :] + got[rows, :].astype(F32)
                    out[:, cols] = total.astype(BF16)


def away_kernel(ids, keep, got, out):
    @pl.when(ids[CORE_ID] == 0)
    def _():
        out[...] = got[...]

    @pl.when(ids[CORE_ID] != 0)
    def _():
        out[...] = keep[...]


def whole_sum(ids, keep, got, moved, cols):
    core = is_zero(ids[CORE_ID])
    own = pick(core, keep[:, cols].astype(F32), got[:, cols].astype(F32))
    return own + moved[:, cols].astype(F32)


def finish_mlp_kernel(ids, keep, got, moved, fc1, fc2):
    fc1[...] = whole_sum(ids, keep, got, moved, slice(0, 1024))
    fc2[...] = jnp.transpose(whole_sum(ids, keep, got, moved, slice(1024, 2048)))


def finish_att_kernel(ids, keep, got, moved, qkv, proj):
    for j in range(3):
        qkv[j, :, :] = whole_sum(ids, keep, got, moved, lanes(j))
    proj[...] = jnp.transpose(whole_sum(ids, keep, got, moved, lanes(PROJ)))


def tie(*values):
    return lax.optimization_barrier(values)


def sum_second(ids, first, second):
    n = first[1].shape[1]
    outs = [((256, n), BF16), ((256, n), F32)]
    other_x, whole_x = call(fold_kernel, outs, ids, *first)
    other_y, whole_y = call(fold_kernel, outs, ids, *second)
    return whole_x, other_x, whole_y, other_y


def send_second(whole_x, other_x, whole_y, other_y):
    return whole_x, swap(other_x, Y), whole_y, swap(other_y, X)


def sum_third(ids, parts):
    n = 2 * parts[0].shape[1]
    keep, send = call(gather_kernel, [((128, n), BF16)] * 2, ids, *parts)
    got = swap(send, CORE)
    (away,) = call(away_kernel, [((128, n), BF16)], ids, keep, got)
    return keep, got, away


def on_device_spread(
    clip_rows,
    out_grad,
    clip_valid,
    gain_rows,
    bias_rows,
    qkv_weight,
    qv_bias,
    proj_weight,
    fc1_weight,
    fc1_bias,
    fc2_weight,
):
    d, t = lax.axis_index("dp"), lax.axis_index("tensor")
    core = d & 1
    ids = jnp.stack([d >> 1, core, d, t, clip_valid[0]]).astype(jnp.int32)
    count = clip_rows.shape[0]
    half, own = count // 2, count // 4
    behind = (PAD + 8, 1024)
    plain = (PAD, 1024)
    packed = (VALUES + half, 128)
    wide = ((count, 1024), F32)

    def to_chips(keep, send):
        got = swap(send, CORE)
        shape = (2, *keep.shape[1:])
        return got, *call(pair_up_kernel, [(shape, BF16)] * 3, ids, keep, got)

    def over_chips(pairs):
        return [swap(pairs[m], CHIP_MASKS[m + 1]) for m in range(3)]

    def offer(shard, far):
        (send,) = call(offer_kernel, [(shard.shape, BF16)], ids, shard, far)
        return send

    def merge(shard, far, send):
        (out,) = call(
            merge_kernel, [((256, shard.shape[1]), BF16)], ids, shard, far, swap(send, CORE)
        )
        return out

    def trade(parts):
        return [parts[0]] + [swap(parts[m], CHIP_MASKS[m]) for m in range(1, 4)]

    params = jnp.concatenate(
        [
            jnp.pad(v, ((0, n - v.shape[0]), (0, 128 - v.shape[1])))
            for v, n in (
                (jnp.concatenate([gain_rows, bias_rows]), 8),
                (qv_bias.reshape(8, 8), 8),
                (fc1_bias, 8),
            )
        ]
    )
    shard_a, shard_g = call(
        shards_kernel,
        [((128, 1024), BF16), ((128, 1024), BF16)],
        ids,
        qkv_weight,
        proj_weight,
        fc2_weight,
    )
    far_a = swap(shard_a, Z_HIGH)
    own_rows, _ = tie(clip_rows, shard_a)
    keep, send = call(
        pack_kernel,
        [((4, 2 * PAD, 1024), BF16)] * 2,
        ids,
        own_rows,
        out_grad,
        params,
        scratch=[((400, 1024), F32), ((8, 2 * PAD, 1024), BF16)],
    )
    w0 = merge(shard_a, far_a, offer(shard_a, far_a))
    shard_f, _ = tie(fc1_weight, far_a)
    far_f = swap(shard_f, Z_HIGH)
    got, *pairs = to_chips(keep, send)
    *parts, w0 = tie(keep, got, *over_chips(pairs), w0)
    here, there, here_grad, there_grad, slots = call(
        pick_kernel,
        [(behind, BF16), (behind, BF16), (plain, BF16), (plain, BF16), ((16, 8, 128), F32)],
        ids,
        *parts,
    )
    r1, r2, r3 = swap(here, Z_LOW), swap(there, Z_HIGH), swap(there, Z_LOW | Z_HIGH)
    w1, w2 = swap(w0, X), swap(w0, Y)
    w_att = (w0, w1, w2, swap(w2[:, :512], X), swap(w1[:, 512:], Y))
    r1, r2, r3, far_f, shard_f = tie(r1, r2, r3, far_f, shard_f)
    f0 = merge(shard_f, far_f, offer(shard_f, far_f))
    rows, normed, vec, qkv_bias, b_fc1 = call(
        norm_one_kernel,
        [
            ((half, 1024), BF16),
            ((half, 1024), BF16),
            ((8, 1024), F32),
            ((8, 128), F32),
            ((1, 1024), F32),
        ],
        ids,
        here,
        r1,
        r2,
        r3,
        scratch=[((half, 1024), F32), ((8, 1024), F32)],
    )

    whole_one, *qkv = call(
        qkv_kernel,
        [((count, 1024), BF16)] + [(packed, BF16)] * 4,
        ids,
        normed,
        swap(normed, CORE),
        qkv_bias,
        *w_att,
        scratch=[wide, ((4, *packed), BF16)],
    )
    shard_g, *qkv = tie(shard_g, *qkv)
    far_g = swap(shard_g, Z_HIGH)
    *qkv, f0, here_grad, there_grad = tie(*trade(qkv), f0, here_grad, there_grad)
    f1, f2 = swap(f0, X), swap(f0, Y)
    s1, s2 = swap(here_grad, Z_LOW), swap(there_grad, Z_HIGH)
    tokens = 4 * count
    *mixed, back = call(
        attention_kernel,
        [((half, 128), BF16)] * 4 + [((tokens, 128), F32)],
        ids,
        *qkv,
        scratch=[((tokens, 192), F32)] + [((tokens, 64), BF16)] * 2 + [((tokens, 128), BF16)],
    )
    shard_g, far_g, *mixed = tie(shard_g, far_g, *mixed)
    g0 = merge(shard_g, far_g, offer(shard_g, far_g))
    *mixed, f1, f2, s1, s2 = tie(*trade(mixed), f1, f2, s1, s2)
    g1, g2 = swap(g0, X), swap(g0, Y)
    f3, g3, s3 = swap(f2, X), swap(g1, Y), swap(s2, Z_LOW)
    attended, keep, send = call(
        proj_kernel,
        [((count, 256), BF16), ((half, 1024), F32), ((half, 1024), BF16)],
        ids,
        *mixed,
        *w_att,
        scratch=[((4, half, 128), BF16), ((count, 256), F32)],
    )

    def pair(keep, send):
        return call(
            pair_kernel, [((half, 1024), F32), ((half, 1024), BF16)], ids, keep, swap(send, CORE)
        )

    def halve(keep, send):
        return call(
            half_kernel, [((own, 1024), F32), ((own, 1024), BF16)], ids, keep, swap(send, CORE)
        )

    part, send = pair(keep, send)
    away, s3 = tie(swap(send, Z_LOW), s3)
    w_fc1, w_fc2 = (f0, f1, f2, f3), (g0, g1, g2, g3)
    (grads,) = call(
        lay_grad_kernel,
        [((half, 1024), BF16)],
        ids,
        here_grad,
        s1,
        s2,
        s3,
        scratch=[((half, 1024), F32)],
    )
    residual, normed_two = call(
        norm_two_kernel,
        [((half, 1024), F32), ((half, 1024), BF16)],
        ids,
        rows,
        part,
        away,
        vec,
    )
    whole_mlp, grad_hidden = call(
        grad_hidden_kernel,
        [((count, 1024), BF16), ((count, 1024), F32)],
        ids,
        grads,
        swap(grads, CORE),
        *w_fc2,
        scratch=[wide],
    )

    whole_two, hidden, grad_pre, sums_fc1, keep, send = call(
        fc_kernel,
        [((count, 1024), BF16)] * 3
        + [((1, 1024), F32), ((half, 1024), F32), ((half, 1024), BF16)],
        ids,
        normed_two,
        swap(normed_two, CORE),
        grad_hidden,
        b_fc1,
        *w_fc1,
        scratch=[wide],
    )
    part, send = pair(keep, send)
    late = tie(send, whole_mlp, hidden, whole_two, grad_pre)
    grad_outs = [((2, 256, 1024), BF16), ((256, 1024), F32), ((256, 1024), F32)]
    cost = 2 * count * 1024 * 1024
    send_f, *rest_f = call(grads_fc1_kernel, grad_outs, ids, late[3], late[4])
    send_g, *rest_g = call(grads_fc2_kernel, grad_outs, ids, late[1], late[2])
    sums_f = (*rest_f, swap(send_f, X))
    sums_g = (*rest_g, swap(send_g, Y))
    keep_out, send_out = call(
        fc2_kernel,
        [((half, 1024), F32), ((half, 1024), BF16)],
        ids,
        late[2],
        *w_fc2,
    )
    away, keep_out, send_out = tie(swap(send, Z_LOW), keep_out, send_out)
    part_out, send_out = halve(keep_out, send_out)
    away_out = swap(send_out, Z_LOW)
    grad_residual, grad_branch, sums_two = call(
        norm_two_back_kernel,
        [((half, 1024), F32), ((half, 1024), BF16), ((8, 1024), F32)],
        ids,
        residual,
        part,
        away,
        grads,
        vec,
    )

    whole_branch, *grad_att = call(
        grad_att_kernel,
        [((count, 1024), BF16)] + [((half, 128), BF16)] * 4,
        ids,
        grad_branch,
        swap(grad_branch, CORE),
        *w_att,
        scratch=[wide, ((4, half, 128), BF16)],
    )
    *grad_att, part_out, away_out = tie(*grad_att, part_out, away_out)
    here_out, there_out = call(
        layer_out_kernel,
        [(plain, BF16)] * 2,
        ids,
        residual,
        part_out,
        away_out,
        vec,
        scratch=[((2 * PAD, 1024), F32)],
    )
    sums_mlp = sum_second(ids, sums_f, sums_g)
    *grad_att, whole_x, other_x, whole_y, other_y, here_out, there_out = tie(
        *trade(grad_att), *sums_mlp, here_out, there_out
    )
    sums_mlp = send_second(whole_x, other_x, whole_y, other_y)
    away_out = swap(there_out, Z_HIGH)
    grad_qkv = call(
        attention_back_kernel,
        [(packed, BF16)] * 4,
        ids,
        *qkv,
        *grad_att,
        back,
        scratch=[((tokens, 192), F32)] + [((tokens, 128), BF16)] * 4 + [((tokens, 64), F32)] * 2,
    )
    *grad_qkv, away_out, whole_x, got_x, whole_y, got_y = tie(*grad_qkv, away_out, *sums_mlp)
    *sums_mlp, moved_mlp = sum_third(ids, (whole_x, got_x, whole_y, got_y))
    moved_mlp = swap(moved_mlp, Z_HIGH)
    keep_out, send_out = call(
        give_out_kernel, [((4, PAD, 1024), BF16)] * 2, ids, slots, here_out, away_out
    )
    got_out, *pairs_out = to_chips(keep_out, send_out)
    *grad_qkv, got_out, p1, p2, p3 = tie(*trade(grad_qkv), got_out, *pairs_out)
    parts_out = over_chips((p1, p2, p3))
    joined, keep, send, sums_qv = call(
        qkv_back_kernel,
        [((count, 768), BF16), ((half, 1024), F32), ((half, 1024), BF16), ((1, 1024), F32)],
        ids,
        *grad_qkv,
        *w_att,
        scratch=[((4, *packed), BF16), ((count, 256), F32)],
    )
    part, send, small = call(
        half_grad_kernel,
        [((own, 1024), F32), ((SMALL + 8, 1024), BF16), ((8, 1024), F32)],
        ids,
        keep,
        swap(send, CORE),
        rows,
        sums_two,
        sums_fc1,
        sums_qv,
    )
    late = tie(send, whole_one, joined, whole_branch, attended)
    grad_outs = [((2, 256, 512), BF16), ((256, 512), F32), ((256, 512), F32)]
    send_x, here_x, there_x, send_y, here_y, there_y = call(
        grads_att_kernel, grad_outs * 2, ids, *late[1:]
    )
    away, send_x, send_y, *parts_out = tie(swap(send, Z_LOW), send_x, send_y, *parts_out)
    parts_out = keep_out, got_out, *parts_out
    got_x, got_y = swap(send_x, X), swap(send_y, Y)
    here, there = call(
        norm_one_back_kernel,
        [(behind, BF16)] * 2,
        ids,
        rows,
        part,
        away,
        grad_residual,
        vec,
        small,
        scratch=[((2 * PAD, 1024), F32)],
    )
    away, got_x, got_y, moved_mlp = tie(swap(there, Z_HIGH), got_x, got_y, moved_mlp)
    sums_att = sum_second(ids, (here_x, there_x, got_x), (here_y, there_y, got_y))
    keep, send = call(
        give_kernel,
        [((4, PAD, 1024), BF16)] * 2,
        ids,
        slots,
        here,
        away,
        scratch=[((8, 1024), F32), ((8, 1024), F32), (plain, F32)],
    )
    got, *pairs = to_chips(keep, send)
    whole_x, other_x, whole_y, other_y = sums_att
    parts = keep, got, *over_chips(pairs)
    *sums_att, moved_att = sum_third(ids, send_second(whole_x, other_x, whole_y, other_y))
    moved_att = swap(moved_att, Z_HIGH)
    input_grad, grad_gains, grad_biases, grad_last, grad_qv, grad_b_fc1 = call(
        take_kernel,
        [
            ((count, 1024), F32),
            ((2, 32), F32),
            ((4, 32), F32),
            ((1, 32), F32),
            ((8, 8), F32),
            ((1, 128), F32),
        ],
        ids,
        *parts,
        scratch=[((8, PAD, 1024), F32)],
    )
    (layer_out,) = call(
        take_out_kernel,
        [((count, 1024), BF16)],
        ids,
        *parts_out,
        scratch=[((8, PAD, 1024), F32), wide],
    )
    grad_fc1, grad_fc2 = call(
        finish_mlp_kernel,
        [((128, 1024), F32), ((1024, 128), F32)],
        ids,
        *sums_mlp,
        moved_mlp,
    )
    moved_att, _ = tie(moved_att, input_grad)
    grad_w, grad_proj = call(
        finish_att_kernel,
        [((3, 128, 256), F32), ((256, 128), F32)],
        ids,
        *sums_att,
        moved_att,
    )
    return (
        layer_out,
        input_grad,
        grad_gains,
        grad_biases,
        grad_w,
        grad_qv.reshape(2, 4, 8),
        grad_proj,
        grad_fc1,
        grad_b_fc1,
        grad_fc2,
        grad_last[0],
    )


def solution(mesh):
    spread = (mesh.shape["dp"], mesh.shape["tensor"]) == (8, 4)
    in_specs = (
        P(("dp", "tensor"), None),
        P(("dp", "tensor"), None),
        P("dp"),
        P(None, ("dp", "tensor")),
        P(None, ("dp", "tensor")),
        P(None, "dp", "tensor"),
        P(None, "tensor", "dp"),
        P("tensor", "dp"),
        P("dp", "tensor"),
        P("tensor", "dp"),
        P("tensor", "dp"),
    )
    out_specs = (
        P(("dp", "tensor"), None),
        P(("dp", "tensor"), None),
        P(None, ("dp", "tensor")),
        P(None, ("dp", "tensor")),
        P(None, "dp", "tensor"),
        P(None, "tensor", "dp"),
        P("tensor", "dp"),
        P("dp", "tensor"),
        P("tensor", "dp"),
        P("tensor", "dp"),
        P(("dp", "tensor")),
    )
    return jax.shard_map(
        on_device_spread if spread else on_device, mesh=mesh, in_specs=in_specs, out_specs=out_specs, check_vma=False
    )
```

```python
import math

import jax
import jax.numpy as jnp
from jax import lax
from jax.experimental import pallas as pl
from jax.experimental.pallas import tpu as pltpu
from jax.sharding import PartitionSpec as P

HD = 64


norm_eps = 1e-06
root_half = 0.7071067811865476
inv_root_tau = 0.3989422804014327


def normalize(values, gain_row, shift_row):
    centre = jnp.mean(values, axis=1, keepdims=True)
    offsets = values - centre
    inverse = lax.rsqrt(jnp.mean(offsets * offsets, axis=1, keepdims=True) + norm_eps)
    scaled = offsets * inverse
    return (scaled * gain_row + shift_row, scaled, inverse)


def normalize_back(upstream, scaled, inverse, gain_row):
    grad_hat = upstream * gain_row
    return (
        grad_hat
        - jnp.mean(grad_hat, axis=1, keepdims=True)
        - scaled * jnp.mean(grad_hat * scaled, axis=1, keepdims=True)
    ) * inverse


def gelu_value(inputs):
    return 0.5 * inputs * (1.0 + lax.erf(inputs * root_half))


def gelu_slope(inputs):
    return (
        0.5 * (1.0 + lax.erf(inputs * root_half))
        + inputs * jnp.exp(-0.5 * inputs * inputs) * inv_root_tau
    )


def fetch(qkv_weight, proj_weight, fc1_weight, fc2_weight, qv_bias, fc1_bias, gain_rows, bias_rows):
    matrices = (
        lax.all_gather(qkv_weight, "dp", axis=1, tiled=True),
        lax.all_gather(proj_weight, "dp", axis=1, tiled=True),
        lax.all_gather(fc1_weight, "dp", axis=0, tiled=True),
        lax.all_gather(fc2_weight, "dp", axis=1, tiled=True),
        lax.all_gather(qv_bias, "dp", axis=2, tiled=True),
        lax.all_gather(fc1_bias, "dp", axis=1, tiled=True),
    )
    vectors = (
        lax.all_gather(gain_rows, ("dp", "tensor"), axis=1, tiled=True),
        lax.all_gather(bias_rows, ("dp", "tensor"), axis=1, tiled=True),
    )
    return (matrices, (vectors[0].astype(jnp.float32), vectors[1].astype(jnp.float32)))


def spread_rows(local_rows):
    return lax.all_gather(local_rows, "tensor", axis=0, tiled=True)


def reduce_rows(term_fn, row_count):
    return lax.psum_scatter(
        term_fn(jnp.int32(0), lax.axis_size("tensor") * row_count),
        "tensor",
        scatter_dimension=0,
        tiled=True,
    )


def spread_grads(local_rows):
    return lax.all_gather(local_rows, "tensor", axis=0, tiled=True)


def reduce_grads(term_fn, row_count):
    return lax.psum_scatter(
        term_fn(jnp.int32(0), lax.axis_size("tensor") * row_count),
        "tensor",
        scatter_dimension=0,
        tiled=True,
    )


def forward(clip_rows, matrices, vectors):
    w_qkv, w_proj, w_fc1, w_fc2, b_qv, b_fc1 = matrices
    gain_rows, bias_rows = vectors
    row_count = clip_rows.shape[0]
    head_cols = w_qkv.shape[2]
    heads_here = head_cols // HD
    score_scale = 1.0 / math.sqrt(HD)
    inputs = clip_rows.astype(jnp.float32)
    normed_one, scaled_one, inverse_one = normalize(inputs, gain_rows[0], bias_rows[0])
    whole_one = spread_rows(normed_one.astype(jnp.bfloat16))
    seq_len = whole_one.shape[0]
    projected = jnp.einsum("sd,jde->jse", whole_one, w_qkv, preferred_element_type=jnp.float32)
    bias_cols = b_qv.reshape(2, head_cols).astype(jnp.float32)
    queries = (projected[0] + bias_cols[0]).astype(jnp.bfloat16).reshape(seq_len, heads_here, HD)
    keys_all = projected[1].astype(jnp.bfloat16).reshape(seq_len, heads_here, HD)
    values_all = (projected[2] + bias_cols[1]).astype(jnp.bfloat16).reshape(seq_len, heads_here, HD)
    scores = (
        jnp.einsum("qhd,khd->hqk", queries, keys_all, preferred_element_type=jnp.float32)
        * score_scale
    )
    top_score = jnp.max(scores, axis=2, keepdims=True)
    weights_exp = jnp.exp(scores - top_score)
    totals = jnp.sum(weights_exp, axis=2, keepdims=True)
    attn_probs = (weights_exp / totals).astype(jnp.bfloat16)
    log_total = top_score + jnp.log(totals)
    attended = (
        jnp.einsum("hqk,khd->qhd", attn_probs, values_all, preferred_element_type=jnp.float32)
        .reshape(seq_len, head_cols)
        .astype(jnp.bfloat16)
    )

    def proj_term(offset, length):
        return jnp.dot(attended, w_proj, preferred_element_type=jnp.float32)

    residual_one = inputs + (reduce_rows(proj_term, row_count) + bias_rows[2])
    normed_two, scaled_two, inverse_two = normalize(residual_one, gain_rows[1], bias_rows[1])
    whole_two = spread_rows(normed_two.astype(jnp.bfloat16))
    pre_act = jnp.dot(whole_two, w_fc1, preferred_element_type=jnp.float32) + b_fc1.reshape(
        -1
    ).astype(jnp.float32)
    hidden = gelu_value(pre_act).astype(jnp.bfloat16)

    def fc2_term(offset, length):
        return jnp.dot(hidden, w_fc2, preferred_element_type=jnp.float32)

    layer_out = residual_one + (reduce_rows(fc2_term, row_count) + bias_rows[3])
    stored = (
        scaled_one,
        inverse_one,
        whole_one,
        queries,
        keys_all,
        values_all,
        log_total,
        attended,
        scaled_two,
        inverse_two,
        whole_two,
        pre_act,
        hidden,
    )
    return (layer_out, stored)


def backward(upstream, matrices, vectors, stored):
    w_qkv, w_proj, w_fc1, w_fc2, b_qv, b_fc1 = matrices
    gain_rows, bias_rows = vectors
    (
        scaled_one,
        inverse_one,
        whole_one,
        queries,
        keys_all,
        values_all,
        log_total,
        attended,
        scaled_two,
        inverse_two,
        whole_two,
        pre_act,
        hidden,
    ) = stored
    row_count = upstream.shape[0]
    seq_len = queries.shape[0]
    heads_here = queries.shape[1]
    head_cols = heads_here * HD
    score_scale = 1.0 / math.sqrt(HD)
    grad_mlp = upstream.astype(jnp.bfloat16)
    grad_fc2_bias = jnp.sum(grad_mlp.astype(jnp.float32), axis=0)
    whole_mlp = spread_grads(grad_mlp)
    grad_fc2 = jnp.einsum("sf,sd->fd", hidden, whole_mlp, preferred_element_type=jnp.float32)
    grad_hidden = jnp.einsum("sd,fd->sf", whole_mlp, w_fc2, preferred_element_type=jnp.float32)
    grad_pre = (grad_hidden * gelu_slope(pre_act)).astype(jnp.bfloat16)
    grad_fc1_bias = jnp.sum(grad_pre.astype(jnp.float32), axis=0)
    grad_fc1 = jnp.einsum("sd,sf->df", whole_two, grad_pre, preferred_element_type=jnp.float32)

    def fc1_back(offset, length):
        return jnp.einsum("sf,df->sd", grad_pre, w_fc1, preferred_element_type=jnp.float32)

    grad_normed_two = reduce_grads(fc1_back, row_count)
    grad_residual = upstream + normalize_back(
        grad_normed_two, scaled_two, inverse_two, gain_rows[1]
    )
    grad_branch = grad_residual.astype(jnp.bfloat16)
    grad_proj_bias = jnp.sum(grad_branch.astype(jnp.float32), axis=0)
    whole_branch = spread_grads(grad_branch)
    grad_proj = jnp.einsum("se,sd->ed", attended, whole_branch, preferred_element_type=jnp.float32)
    grad_att = (
        jnp.einsum("sd,ed->se", whole_branch, w_proj, preferred_element_type=jnp.float32)
        .astype(jnp.bfloat16)
        .reshape(seq_len, heads_here, HD)
    )
    scores = (
        jnp.einsum("qhd,khd->hqk", queries, keys_all, preferred_element_type=jnp.float32)
        * score_scale
    )
    attn_probs = jnp.exp(scores - log_total)
    grad_probs = jnp.einsum(
        "qhd,khd->hqk", grad_att, values_all, preferred_element_type=jnp.float32
    )
    row_dot = jnp.sum(attn_probs * grad_probs, axis=2, keepdims=True)
    grad_scores = (attn_probs * (grad_probs - row_dot)).astype(jnp.bfloat16)
    grad_query = (
        jnp.einsum("hqk,khd->qhd", grad_scores, keys_all, preferred_element_type=jnp.float32)
        * score_scale
    ).astype(jnp.bfloat16)
    grad_key = (
        jnp.einsum("hqk,qhd->khd", grad_scores, queries, preferred_element_type=jnp.float32)
        * score_scale
    ).astype(jnp.bfloat16)
    grad_value = jnp.einsum(
        "hqk,qhd->khd",
        attn_probs.astype(jnp.bfloat16),
        grad_att,
        preferred_element_type=jnp.float32,
    ).astype(jnp.bfloat16)
    grad_qkv = jnp.stack([grad_query, grad_key, grad_value]).reshape(3, seq_len, head_cols)
    grad_qv = jnp.stack(
        [
            jnp.sum(grad_query.astype(jnp.float32), axis=0),
            jnp.sum(grad_value.astype(jnp.float32), axis=0),
        ]
    )
    grad_qkv_weight = jnp.einsum(
        "sd,jse->jde", whole_one, grad_qkv, preferred_element_type=jnp.float32
    )

    def qkv_back(offset, length):
        return jnp.einsum("jse,jde->sd", grad_qkv, w_qkv, preferred_element_type=jnp.float32)

    grad_normed_one = reduce_grads(qkv_back, row_count)
    grad_input = grad_residual + normalize_back(
        grad_normed_one, scaled_one, inverse_one, gain_rows[0]
    )
    grad_gain = jnp.stack(
        [
            jnp.sum(grad_normed_one * scaled_one, axis=0),
            jnp.sum(grad_normed_two * scaled_two, axis=0),
        ]
    )
    grad_bias = jnp.stack(
        [
            jnp.sum(grad_normed_one, axis=0),
            jnp.sum(grad_normed_two, axis=0),
            grad_proj_bias,
            grad_fc2_bias,
        ]
    )
    weight_part = (
        lax.psum_scatter(grad_qkv_weight, "dp", scatter_dimension=1, tiled=True),
        lax.psum_scatter(grad_proj, "dp", scatter_dimension=1, tiled=True),
        lax.psum_scatter(grad_fc1, "dp", scatter_dimension=0, tiled=True),
        lax.psum_scatter(grad_fc2, "dp", scatter_dimension=1, tiled=True),
        lax.psum_scatter(grad_qv, "dp", scatter_dimension=2, tiled=True),
        lax.psum_scatter(grad_fc1_bias.reshape(1, -1), "dp", scatter_dimension=1, tiled=True),
    )
    vector_part = (
        lax.psum_scatter(grad_gain, ("dp", "tensor"), scatter_dimension=1, tiled=True),
        lax.psum_scatter(grad_bias, ("dp", "tensor"), scatter_dimension=1, tiled=True),
    )
    return (grad_input, weight_part, vector_part)


def on_device(
    clip_rows,
    out_grad,
    clip_valid,
    gain_rows,
    bias_rows,
    qkv_weight,
    qv_bias,
    proj_weight,
    fc1_weight,
    fc1_bias,
    fc2_weight,
):
    clip_weight = clip_valid[0].astype(jnp.float32)
    upstream = out_grad.astype(jnp.float32) * clip_weight
    matrices, vectors = fetch(
        qkv_weight, proj_weight, fc1_weight, fc2_weight, qv_bias, fc1_bias, gain_rows, bias_rows
    )
    layer_out, stored = forward(clip_rows, matrices, vectors)
    matrices, vectors = fetch(
        qkv_weight, proj_weight, fc1_weight, fc2_weight, qv_bias, fc1_bias, gain_rows, bias_rows
    )
    unused_out, stored = forward(clip_rows, matrices, vectors)
    grad_input, weight_part, vector_part = backward(upstream, matrices, vectors, stored)
    return (
        (layer_out * clip_weight).astype(jnp.bfloat16),
        grad_input,
        vector_part[0],
        vector_part[1],
        weight_part[0],
        weight_part[4],
        weight_part[1],
        weight_part[2],
        weight_part[5],
        weight_part[3],
        vector_part[1][3],
    )


AXES = ("dp", "tensor")
Z_LOW, Z_HIGH, CORE, X, Y = 1, 2, 4, 8, 16
CHIP_MASKS = (0, X, Y, X | Y)
BF16, F32 = jnp.bfloat16, jnp.float32
NN, NT, TN = ((1,), (0,)), ((1,), (1,)), ((0,), (0,))
SHARE = 49
PAD = 56
SMALL = 104
CHIP_ID, CORE_ID, D_ID, T_ID = range(4)


def swap(value, mask):
    return lax.ppermute(value, AXES, [(i, i ^ mask) for i in range(32)])


def dot(left, right, dims):
    return lax.dot_general(left, right, (dims, ((), ())), preferred_element_type=F32)


TIMES = {
    "pack": 1.2,
    "pick": 1.5,
    "norm_one": 1.0,
    "qkv": 1.6,
    "attention": 7.6,
    "proj": 1.1,
    "norm_two": 0.9,
    "mlp_start": 1.0,
    "fc": 5.0,
    "grads_fc1": 1.8,
    "grads_fc2": 1.8,
    "fc2": 1.6,
    "norm_two_back": 1.5,
    "grad_att": 1.1,
    "attention_back": 12.0,
    "qkv_back": 1.5,
    "half_grad": 1.1,
    "grads_att": 1.8,
    "norm_one_back": 1.0,
    "give": 1.3,
    "take": 2.0,
    "finish_mlp": 1.7,
    "finish_att": 1.4,
}


SPACE = {"attention_kernel": 16, "attention_back_kernel": 12}


def call(body, outs, scalars, *args, scratch=()):
    moved = sum(math.prod(a.shape) * a.dtype.itemsize for a in args)
    moved += sum(math.prod(s) * jnp.dtype(t).itemsize for s, t in outs)
    held = sum(math.prod(s[:-1]) * max(s[-1], 128) * jnp.dtype(t).itemsize for s, t in scratch)
    time = TIMES.get(body.__name__.removesuffix("_kernel"), 0.7)
    return pl.pallas_call(
        body,
        out_shape=[jax.ShapeDtypeStruct(s, t) for s, t in outs],
        in_specs=[pl.BlockSpec(memory_space=pltpu.SMEM)]
        + [pl.BlockSpec(memory_space=pltpu.VMEM)] * len(args),
        out_specs=[pl.BlockSpec(memory_space=pltpu.VMEM)] * len(outs),
        scratch_shapes=[pltpu.VMEM(s, t) for s, t in scratch],
        compiler_params=pltpu.CompilerParams(vmem_limit_bytes=moved + held + (SPACE.get(body.__name__, 4) << 20)),
        cost_estimate=pl.CostEstimate(
            flops=int(time * 1.15e9), bytes_accessed=moved, transcendentals=0
        ),
    )(scalars, *args)


def chip_lanes(ids, m):
    return pl.ds(pl.multiple_of((ids[CHIP_ID] ^ m) * 256, 256), 256)


def lanes(m):
    return slice(256 * m, 256 * m + 256)


def row_ids(shape):
    return lax.broadcasted_iota(jnp.int32, shape, 0)


def pick(condition, left, right):
    return jnp.where(jnp.full(left.shape, condition, jnp.int32) != 0, left, right)


def is_zero(number):
    return jnp.where(number == 0, 1, 0)


def z_low(ids):
    return ids[T_ID] & 1


def z_high(ids):
    return ids[T_ID] >> 1


def far_chips(ids, core_flip):
    return [(ids[CHIP_ID] ^ m) * 2 + (ids[CORE_ID] ^ core_flip) for m in range(4)]


def pack_kernel(ids, rows, grads, params, keep, send, wide, stage):
    lane32 = lax.broadcasted_iota(jnp.int32, (32, 128), 1)
    spot = (lane32 == row_ids((32, 128)) + 32 * ids[T_ID]).astype(F32).astype(BF16)
    lane8 = lax.broadcasted_iota(jnp.int32, (8, 128), 1)
    spot8 = (lane8 == row_ids((8, 128)) + 8 * ids[D_ID]).astype(F32).astype(BF16)
    placed = dot(params[0:8, 0:32], spot, NN)
    qv_rows = dot(params[8:16, 0:8], spot8, NN)
    row_a = jnp.concatenate(
        [placed[k : k + 1] for k in range(6)]
        + [params[...].astype(F32)[16:17], jnp.zeros((1, 128), F32)],
        axis=1,
    )
    row_b = jnp.concatenate([qv_rows[k : k + 1] for k in range(8)], axis=1)
    flag = jnp.full((PAD, 1024), ids[4], jnp.int32).astype(F32)
    row = row_ids((PAD, 1024))
    tail = jnp.where(row == SHARE, row_a, jnp.where(row == SHARE + 1, row_b, flag))
    wide[0 : rows.shape[0], :] = rows[...].astype(F32)
    for j in range(8):
        block = wide[SHARE * j : SHARE * j + PAD, :]
        stage[j, 0:PAD, :] = jnp.where(row < SHARE, block, tail).astype(BF16)
    wide[0 : rows.shape[0], :] = grads[...].astype(F32)
    for j in range(8):
        stage[j, PAD : 2 * PAD, :] = wide[SHARE * j : SHARE * j + PAD, :].astype(BF16)
    for m, (d0, d1) in enumerate(zip(far_chips(ids, 0), far_chips(ids, 1))):
        keep[m, :, :] = stage[d0, :, :]
        send[m, :, :] = stage[d1, :, :]


def pair_up_kernel(ids, keep, got, o1, o2, o3):
    for m, out in enumerate((o1, o2, o3)):
        out[0, :, :] = keep[m + 1, :, :]
        out[1, :, :] = got[m + 1, :, :]


def arrived(ids, keep, got, d1, d2, d3):
    parts = []
    for m, (a0, a1) in enumerate(zip(far_chips(ids, 0), far_chips(ids, 1))):
        first, second = ((keep, 0), (got, 0)) if m == 0 else (((d1, d2, d3)[m - 1], k) for k in range(2))
        parts += [(a0, *first), (a1, *second)]
    return parts


def pick_kernel(ids, keep, got, d1, d2, d3, here, there, here_grad, there_grad, slots):
    row8 = row_ids((8, 1024))
    row = row_ids((PAD, 1024))
    mine = jnp.zeros((PAD, 1024), F32)
    other, mine_grad, other_grad = mine, mine, mine
    params = jnp.zeros((8, 1024), F32)
    qv = jnp.zeros((1, 1024), F32)
    high = jnp.full((1, 1024), z_high(ids), jnp.int32).astype(F32)
    parts = arrived(ids, keep, got, d1, d2, d3)
    flags = [
        ref[k, PAD - 8 : PAD, :].astype(F32)[SHARE + 10 - PAD : SHARE + 11 - PAD]
        for _, ref, k in parts
    ]
    for i, (a, ref, k) in enumerate(parts):
        seen = jnp.zeros((1, 1024), F32)
        for (c, _, _), flag in zip(parts, flags):
            earlier = jnp.full((1, 1024), jnp.where(c < a, 1, 0), jnp.int32).astype(F32)
            seen = seen + flag * earlier
        block = ref[k, 0:PAD, :].astype(F32)
        grad = ref[k, PAD : 2 * PAD, :].astype(F32)
        is_mine = jnp.where(seen == high, flags[i], 0.0)
        is_other = flags[i] - is_mine
        mine = jnp.where(is_mine > 0.5, block, mine)
        other = jnp.where(is_other > 0.5, block, other)
        mine_grad = jnp.where(is_mine > 0.5, grad, mine_grad)
        other_grad = jnp.where(is_other > 0.5, grad, other_grad)
        params = jnp.where(row8 == a, block[SHARE : SHARE + 1], params)
        qv = qv + block[SHARE + 1 : SHARE + 2]
        slots[a, :, :] = jnp.broadcast_to(is_mine[:, 0:128], (8, 128))
        slots[8 + a, :, :] = jnp.broadcast_to(is_other[:, 0:128], (8, 128))
    for value, out in ((mine, here), (other, there)):
        out[0:PAD, :] = jnp.where(row == PAD - 1, qv, value).astype(BF16)
        out[PAD : PAD + 8, :] = params.astype(BF16)
    here_grad[...] = mine_grad.astype(BF16)
    there_grad[...] = other_grad.astype(BF16)


def lay_rows(ids, here, r1, r2, r3, wide):
    low = is_zero(z_low(ids))
    for m in range(4):
        cols = chip_lanes(ids, m)
        blocks = [ref[0:PAD, cols].astype(F32) for ref in (here, r1, r2, r3)]
        order = (
            pick(low, blocks[0], blocks[1]),
            pick(low, blocks[2], blocks[3]),
            pick(low, blocks[1], blocks[0]),
            pick(low, blocks[3], blocks[2]),
        )
        for i, block in enumerate(order):
            wide[SHARE * i : SHARE * i + SHARE, lanes(m)] = block[0:SHARE]


def norm_parts(values):
    centre = jnp.mean(values, axis=1, keepdims=True)
    offsets = values - centre
    inverse = lax.rsqrt(jnp.mean(offsets * offsets, axis=1, keepdims=True) + norm_eps)
    return offsets * inverse, inverse


def norm_one_kernel(ids, here, r1, r2, r3, rows, normed, vec, qv_bias, b_fc1, wide, small):
    lay_rows(ids, here, r1, r2, r3, wide)
    own = here[PAD - 8 : PAD + 8, :].astype(F32)
    far = r2[PAD - 8 : PAD + 8, :].astype(F32)
    tails = [own[8:], far[8:]] + [r[PAD : PAD + 8, :].astype(F32) for r in (r1, r3)]
    params = tails[0] + tails[1] + tails[2] + tails[3]
    small[...] = jnp.zeros_like(small)
    for d in range(8):
        for k in range(6):
            small[k : k + 1, 128 * d : 128 * d + 128] = params[
                d : d + 1, 128 * k : 128 * k + 128
            ]
    for m in range(4):
        vec[:, lanes(m)] = small[:, chip_lanes(ids, m)]
    home = pick(is_zero(ids[CORE_ID]), own, far)
    for k in range(8):
        qv_bias[k : k + 1, :] = home[7:8, 128 * k : 128 * k + 128]
        b_fc1[0:1, 128 * k : 128 * k + 128] = home[8 + k : 9 + k, 768:896]
    values = wide[...]
    scaled, _ = norm_parts(values)
    rows[...] = values.astype(BF16)
    normed[...] = (scaled * vec[0:1, :] + vec[2:3, :]).astype(BF16)


def lay_grad_kernel(ids, here, r1, r2, r3, out, wide):
    lay_rows(ids, here, r1, r2, r3, wide)
    out[...] = wide[...].astype(BF16)


def join_rows(wide, own, got):
    half = own.shape[0]
    wide[0:half, :] = own[...].astype(F32)
    wide[half : 2 * half, :] = got[...].astype(F32)


PROJ = 3


def part_of(weights, m, j):
    if m < 3:
        return weights[m][:, lanes(j)]
    return weights[3 + j // 2][:, lanes(j % 2)]


VALUES = 400


def fold_rows(value):
    half = value.shape[0] // 2
    return jnp.concatenate([value[:half], value[half:]], axis=1)


def qkv_kernel(ids, own, got, qv_bias, w0, w1, w2, w3, w4, whole, o0, o1, o2, o3, wide, heads):
    weights = (w0, w1, w2, w3, w4)
    join_rows(wide, own, got)
    whole[...] = wide[...].astype(BF16)
    for j in range(3):
        total = dot(whole[:, lanes(0)], w0[:, lanes(j)], NN)
        for m in range(1, 4):
            total = total + dot(whole[:, lanes(m)], part_of(weights, m, j), NN)
        for h in range(4):
            part = total[:, 64 * h : 64 * h + 64]
            if j != 1:
                k = (j // 2) * 4 + h
                part = part + qv_bias[k : k + 1, 0:64]
            if j < 2:
                heads[h, 0 : part.shape[0], 64 * j : 64 * j + 64] = part.astype(BF16)
            else:
                heads[h, VALUES:, :] = fold_rows(part).astype(BF16)
    for m, out in enumerate((o0, o1, o2, o3)):
        out[...] = heads[ids[CHIP_ID] ^ m, :, :]


STEP, BACK_STEP = 392, 112


def stage_qkv(stage, parts):
    tokens = stage.shape[0] // 4
    half = tokens // 2
    for m, part in enumerate(parts):
        start = tokens * m
        stage[start : start + tokens, 0:128] = part[0:tokens, :].astype(F32)
        stage[start : start + half, 128:192] = part[VALUES:, 0:64].astype(F32)
        stage[start + half : start + tokens, 128:192] = part[VALUES:, 64:128].astype(F32)


def attention_kernel(ids, a0, a1, a2, a3, o0, o1, o2, o3, back, stage, q, k, v):
    tokens = stage.shape[0] // 4
    stage_qkv(stage, (a0, a1, a2, a3))
    q[...] = (stage[:, 0:64] * 0.125).astype(BF16)
    k[...] = stage[:, 64:128].astype(BF16)
    v[:, 0:64] = stage[:, 128:192].astype(BF16)
    v[:, 64:128] = jnp.ones((v.shape[0], 64), BF16)
    for i in range(stage.shape[0] // STEP):
        rows = slice(i * STEP, i * STEP + STEP)
        scores = dot(q[rows, :], k[...], NT)
        top = jnp.max(scores, axis=1, keepdims=True)
        mixed = dot(jnp.exp(scores - top).astype(BF16), v[...], NN)
        total = mixed[:, 64:128]
        back[rows, 0:64] = mixed[:, 0:64] / total
        back[rows, 64:128] = top + jnp.log(total)
    for m, out in enumerate((o0, o1, o2, o3)):
        out[...] = fold_rows(back[tokens * m : tokens * m + tokens, 0:64]).astype(BF16)


def with_shift(value, shift):
    high = shift.astype(BF16).astype(F32)
    middle = (shift - high).astype(BF16).astype(F32)
    low = shift - high - middle
    lane = lax.broadcasted_iota(jnp.int32, (value.shape[0], 64), 1)
    extra = jnp.where(lane == 0, -high, jnp.where(lane == 1, -middle, jnp.where(lane == 2, -low, 0.0)))
    return jnp.concatenate([value, extra], axis=1).astype(BF16)


def with_ones(value):
    lane = lax.broadcasted_iota(jnp.int32, (value.shape[0], 64), 1)
    return jnp.concatenate([value, jnp.where(lane < 3, 1.0, 0.0)], axis=1).astype(BF16)


def attention_back_kernel(
    ids, a0, a1, a2, a3, g0, g1, g2, g3, back, o0, o1, o2, o3, stage, q, k, v, g, grad_k, grad_v
):
    tokens = stage.shape[0] // 4
    stage_qkv(stage, (a0, a1, a2, a3))
    q[...] = with_shift(stage[:, 0:64] * 0.125, back[:, 64:65])
    k[...] = with_ones(stage[:, 64:128])
    v[...] = with_ones(stage[:, 128:192])
    for m, part in enumerate((g0, g1, g2, g3)):
        middle = tokens * m + tokens // 2
        stage[tokens * m : middle, 0:64] = part[:, 0:64].astype(F32)
        stage[middle : tokens * m + tokens, 0:64] = part[:, 64:128].astype(F32)
    grads = stage[:, 0:64]
    g[...] = with_shift(grads, jnp.sum(grads * back[:, 0:64], axis=1, keepdims=True))
    keys_t = jnp.transpose(k[:, 0:64])
    for i in range(stage.shape[0] // BACK_STEP):
        rows = slice(i * BACK_STEP, i * BACK_STEP + BACK_STEP)
        probs = jnp.exp(dot(k[...], q[rows, :], NT))
        grad_scores = (probs * dot(v[...], g[rows, :], NT)).astype(BF16)
        part_v = dot(probs.astype(BF16), g[rows, 0:64], NN)
        part_k = dot(grad_scores, q[rows, 0:64], NN)
        grad_v[...] = part_v if i == 0 else grad_v[...] + part_v
        grad_k[...] = part_k if i == 0 else grad_k[...] + part_k
        stage[rows, 0:64] = jnp.transpose(dot(keys_t, grad_scores, NN)) * 0.125
    for m, out in enumerate((o0, o1, o2, o3)):
        rows = slice(tokens * m, tokens * m + tokens)
        out[0:tokens, 0:64] = stage[rows, 0:64].astype(BF16)
        out[0:tokens, 64:128] = grad_k[rows, :].astype(BF16)
        out[VALUES:, :] = fold_rows(grad_v[rows, :]).astype(BF16)


def split_rows(total, keep, send, cols):
    half = keep.shape[0]
    keep[:, cols] = total[:half]
    send[:, cols] = total[half:].astype(BF16)


def proj_kernel(ids, a0, a1, a2, a3, w0, w1, w2, w3, w4, joined, keep, send, heads, wide):
    for m, part in enumerate((a0, a1, a2, a3)):
        heads[m, :, :] = part[...]
    half = keep.shape[0]
    for h in range(4):
        part = heads[h ^ ids[CHIP_ID], :, :].astype(F32)
        wide[0:half, 64 * h : 64 * h + 64] = part[:, 0:64]
        wide[half:, 64 * h : 64 * h + 64] = part[:, 64:128]
    joined[...] = wide[...].astype(BF16)
    for m in range(4):
        weight = part_of((w0, w1, w2, w3, w4), m, PROJ)
        split_rows(dot(joined[...], weight, NT), keep, send, lanes(m))


def pair_kernel(ids, keep, got, part, send):
    total = keep[...] + got[...].astype(F32)
    part[...] = total
    send[...] = total.astype(BF16)


def half_kernel(ids, keep, got, part, send):
    own = part.shape[0]
    total = keep[...] + got[...].astype(F32)
    low = is_zero(z_low(ids))
    part[...] = pick(low, total[:own], total[own:])
    send[...] = pick(low, total[own:], total[:own]).astype(BF16)


def half_grad_kernel(ids, keep, got, rows, sums_two, sums_fc1, sums_qv, part, send, small):
    own = part.shape[0]
    total = keep[...] + got[...].astype(F32)
    low = is_zero(z_low(ids))
    part[...] = pick(low, total[:own], total[own:])
    scaled, _ = norm_parts(rows[...].astype(F32))
    send[0:own, :] = pick(low, total[own:], total[:own]).astype(BF16)
    sums = jnp.concatenate(
        [
            jnp.sum(total * scaled, axis=0, keepdims=True),
            sums_two[0:1, :],
            jnp.sum(total, axis=0, keepdims=True),
            sums_two[1:4, :],
            sums_qv[...],
            sums_fc1[...],
        ],
        axis=0,
    )
    small[...] = sums
    send[SMALL : SMALL + 8, :] = sums.astype(BF16)


def norm_two_kernel(ids, rows, part, got, vec, residual, normed):
    total = rows[...].astype(F32) + (part[...] + got[...].astype(F32) + vec[4:5, :])
    residual[...] = total
    scaled, _ = norm_parts(total)
    normed[...] = (scaled * vec[1:2, :] + vec[3:4, :]).astype(BF16)


def mlp_start_kernel(
    ids, own, got, own_grad, got_grad, b_fc1, f0, f1, f2, g0, g1, g2, whole, whole_grad, pre, back, wide
):
    join_rows(wide, own, got)
    whole[...] = wide[...].astype(BF16)
    join_rows(wide, own_grad, got_grad)
    whole_grad[...] = wide[...].astype(BF16)

    def body(c, carry):
        cols = pl.ds(pl.multiple_of(c * 256, 256), 256)
        total = b_fc1[:, cols] + dot(whole[:, lanes(0)], f0[:, cols], NN)
        grad = dot(whole_grad[:, lanes(0)], g0[:, cols], NN)
        for m, (f, g) in ((1, (f1, g1)), (2, (f2, g2))):
            total = total + dot(whole[:, lanes(m)], f[:, cols], NN)
            grad = grad + dot(whole_grad[:, lanes(m)], g[:, cols], NN)
        pre[:, cols] = total
        back[:, cols] = grad
        return carry

    lax.fori_loop(0, 4, body, 0)


def fc_kernel(
    ids, whole, whole_grad, start, back, w0, w1, w2, w3, g3, hidden, grad_pre, sums, keep, send, wide
):
    weights = (w0, w1, w2, w3)
    wide[...] = jnp.zeros_like(wide)

    def body(c, carry):
        cols = pl.ds(pl.multiple_of(c * 256, 256), 256)
        pre = start[:, cols] + dot(whole[:, lanes(3)], w3[:, cols], NN)
        grad_hidden = back[:, cols] + dot(whole_grad[:, lanes(3)], g3[:, cols], NN)
        half_erf = 0.5 * (1.0 + lax.erf(pre * root_half))
        hidden[:, cols] = (pre * half_erf).astype(BF16)
        slope = half_erf + pre * jnp.exp(-0.5 * pre * pre) * inv_root_tau
        grad = (grad_hidden * slope).astype(BF16)
        grad_pre[:, cols] = grad
        sums[:, cols] = jnp.sum(grad.astype(F32), axis=0, keepdims=True)
        for m in range(4):
            wide[:, lanes(m)] += dot(grad, weights[m][:, cols], NT)
        return carry

    lax.fori_loop(0, 4, body, 0)
    for m in range(4):
        split_rows(wide[:, lanes(m)], keep, send, lanes(m))


def norm_back(total, scaled, inverse, gain):
    hat = total * gain
    return (
        hat
        - jnp.mean(hat, axis=1, keepdims=True)
        - scaled * jnp.mean(hat * scaled, axis=1, keepdims=True)
    ) * inverse


def norm_two_back_kernel(ids, residual, part, got, grads, vec, grad_residual, grad_branch, sums):
    scaled, inverse = norm_parts(residual[...])
    total = part[...] + got[...].astype(F32)
    upstream = grads[...].astype(F32)
    result = upstream + norm_back(total, scaled, inverse, vec[1:2, :])
    branch = result.astype(BF16)
    grad_residual[...] = result
    grad_branch[...] = branch
    own = total.shape[0] // 2
    row = row_ids(total.shape)
    low = jnp.full(total.shape, z_low(ids), jnp.int32)
    mine = jnp.where(row < own, 1 - low, low) != 0

    def column_sum(value):
        return jnp.sum(jnp.where(mine, value, 0.0), axis=0, keepdims=True)

    sums[0:1, :] = column_sum(total * scaled)
    sums[1:2, :] = column_sum(total)
    sums[2:3, :] = column_sum(branch.astype(F32))
    sums[3:4, :] = column_sum(upstream)
    sums[4:8, :] = jnp.zeros((4, sums.shape[1]), F32)


def grad_att_kernel(ids, own, got, w0, w1, w2, w3, w4, whole, o0, o1, o2, o3, wide, heads):
    join_rows(wide, own, got)
    whole[...] = wide[...].astype(BF16)
    weights = (w0, w1, w2, w3, w4)
    total = dot(whole[:, lanes(0)], w0[:, lanes(PROJ)], NN)
    for m in range(1, 4):
        total = total + dot(whole[:, lanes(m)], part_of(weights, m, PROJ), NN)
    for h in range(4):
        heads[h, :, :] = fold_rows(total[:, 64 * h : 64 * h + 64]).astype(BF16)
    for m, out in enumerate((o0, o1, o2, o3)):
        out[...] = heads[ids[CHIP_ID] ^ m, :, :]


def qkv_back_kernel(ids, g0, g1, g2, g3, w0, w1, w2, w3, w4, joined, keep, send, sums, heads, wide):
    for m, part in enumerate((g0, g1, g2, g3)):
        heads[m, :, :] = part[...]
    half, tokens = keep.shape[0], joined.shape[0]
    for h in range(4):
        part = heads[h ^ ids[CHIP_ID], :, :]
        for j in range(2):
            joined[:, 256 * j + 64 * h : 256 * j + 64 * h + 64] = part[
                0:tokens, 64 * j : 64 * j + 64
            ]
        values = part[VALUES:, :].astype(F32)
        wide[0:half, 64 * h : 64 * h + 64] = values[:, 0:64]
        wide[half:, 64 * h : 64 * h + 64] = values[:, 64:128]
        for k, value in ((h, part[0:tokens, 0:64]), (4 + h, wide[:, 64 * h : 64 * h + 64])):
            total = jnp.sum(value.astype(F32), axis=0, keepdims=True)
            sums[0:1, 128 * k : 128 * k + 128] = jnp.concatenate(
                [total, jnp.zeros((1, 64), F32)], axis=1
            )
    joined[:, 512:768] = wide[...].astype(BF16)
    for m in range(4):
        weights = (w0, w1, w2, w3, w4)
        total = dot(joined[:, lanes(0)], part_of(weights, m, 0), NT)
        for j in (1, 2):
            total = total + dot(joined[:, lanes(j)], part_of(weights, m, j), NT)
        split_rows(total, keep, send, lanes(m))


def to_owners(ids, value, wide, here, there):
    wide[0 : 2 * SHARE, :] = value
    wide[2 * SHARE :, :] = jnp.zeros((wide.shape[0] - 2 * SHARE, wide.shape[1]), F32)
    for m in range(4):
        cols = chip_lanes(ids, m)
        here[0:PAD, cols] = wide[0:PAD, lanes(m)].astype(BF16)
        there[0:PAD, cols] = wide[SHARE : SHARE + PAD, lanes(m)].astype(BF16)


def own_half(ids, ref):
    own = ref.shape[0] // 2
    value = ref[...].astype(F32)
    return pick(is_zero(z_low(ids)), value[:own], value[own:])


def norm_one_back_kernel(
    ids, rows, part, got, grad_residual, vec, small, here, there, wide
):
    scaled, inverse = norm_parts(own_half(ids, rows))
    total = part[...] + got[0 : 2 * SHARE, :].astype(F32)
    result = own_half(ids, grad_residual) + norm_back(total, scaled, inverse, vec[0:1, :])
    to_owners(ids, result, wide, here, there)
    far = jnp.where(row_ids((8, 1024)) < 6, got[SMALL : SMALL + 8, :].astype(F32), 0.0)
    sums = (small[...] + far).astype(BF16)
    here[PAD : PAD + 8, :] = sums
    there[PAD : PAD + 8, :] = sums


def layer_out_kernel(ids, residual, part, got, vec, here, there, wide):
    result = own_half(ids, residual) + (part[...] + got[...].astype(F32) + vec[5:6, :])
    to_owners(ids, result, wide, here, there)


def fc2_kernel(ids, hidden, w0, w1, w2, w3, keep, send):
    for m, weight in enumerate((w0, w1, w2, w3)):
        split_rows(dot(hidden[...], weight[...], NT), keep, send, lanes(m))


def for_slot(slots, d, left, right):
    value = jnp.where(slots[8 + d, 0:1, 0:1] > 0.5, right, 0.0)
    return jnp.where(slots[d, 0:1, 0:1] > 0.5, left, value)


def give_out_kernel(ids, slots, here, away, keep, send):
    left = here[...].astype(F32)
    right = away[...].astype(F32)
    for out, flip in ((keep, 0), (send, 1)):
        for m, d in enumerate(far_chips(ids, flip)):
            out[m, :, :] = for_slot(slots, d, left, right).astype(BF16)


def give_kernel(ids, slots, here, away, keep, send, rel, flat, tail):
    left = here[0:PAD, :].astype(F32)
    right = away[0:PAD, :].astype(F32)
    own = here[PAD : PAD + 8, :].astype(F32)
    far = away[PAD : PAD + 8, :].astype(F32)
    rel[...] = own + far
    home = pick(is_zero(ids[CORE_ID]), own, far)
    for m in range(4):
        flat[:, chip_lanes(ids, m)] = rel[:, lanes(m)]
    rel[0:1, :] = home[7:8]
    tail[...] = jnp.zeros_like(tail)
    for k in range(8):
        row, lane = (SHARE + k, 128) if k < 7 else (SHARE, 256)
        tail[row : row + 1, lane : lane + 128] = home[6:7, 128 * k : 128 * k + 128]
    row = row_ids((PAD, 1024))
    for out, flip in ((keep, 0), (send, 1)):
        for m, d in enumerate(far_chips(ids, flip)):
            cols = pl.ds(pl.multiple_of(d * 128, 128), 128)
            tail[SHARE : SHARE + 6, 0:128] = flat[0:6, cols]
            tail[SHARE + 6 : PAD, 0:128] = rel[0:1, cols]
            value = for_slot(slots, d, left, right)
            out[m, :, :] = jnp.where(row < SHARE, value, tail[...]).astype(BF16)


def settle_rows(parts, stage, out):
    for a, ref, k in parts:
        stage[a, :, :] = ref[k, :, :].astype(F32)
    for j in range(8):
        out[SHARE * j : SHARE * j + SHARE, :] = stage[j, 0:SHARE, :]


def take_out_kernel(ids, keep, got, d1, d2, d3, out, stage, wide):
    settle_rows(arrived(ids, keep, got, d1, d2, d3), stage, wide)
    out[...] = wide[...].astype(BF16)


def take_kernel(ids, keep, got, d1, d2, d3, out, gains, biases, last, qv, b_fc1, stage):
    parts = arrived(ids, keep, got, d1, d2, d3)
    settle_rows(parts, stage, out)
    total = jnp.zeros((8, 384), F32)
    for _, ref, k in parts:
        total = total + ref[k, PAD - 8 : PAD, 0:384].astype(F32)
    rows = pltpu.roll(total[:, 0:128], (128 - 32 * ids[T_ID]) & 127, 1)
    gains[...] = rows[1:3, 0:32]
    biases[...] = rows[3:7, 0:32]
    last[...] = rows[6:7, 0:32]
    b_fc1[...] = total[7:8, 0:128]
    pieces = jnp.concatenate([total[1:8, 128:256], total[1:2, 256:384]], axis=0)
    qv[...] = pltpu.roll(pieces, (128 - 8 * ids[D_ID]) & 127, 1)[:, 0:8]


def shards_kernel(ids, qkv, proj, fc2, first, second):
    for j in range(3):
        first[:, lanes(j)] = qkv[j, :, :]
    first[:, lanes(PROJ)] = jnp.transpose(proj[...])
    second[...] = jnp.transpose(fc2[...])


def offer_kernel(ids, own, far, send):
    @pl.when(ids[CORE_ID] == 0)
    def _():
        send[...] = far[...]

    @pl.when(ids[CORE_ID] != 0)
    def _():
        send[...] = own[...]


def merge_kernel(ids, own, far, got, out):
    half = own.shape[0]

    @pl.when(ids[CORE_ID] == 0)
    def _():
        out[0:half, :] = own[...]
        out[half:, :] = got[...]

    @pl.when(ids[CORE_ID] != 0)
    def _():
        out[0:half, :] = got[...]
        out[half:, :] = far[...]


X_FIRST, Y_FIRST = (1, 2), (2, 1)


def blocks_of(order, left, right, cols, send, here, there, out_cols):
    near, far = order
    for slot, m in ((0, near), (1, 3)):
        send[slot, :, out_cols] = dot(left[:, lanes(m)], right[:, cols], TN).astype(BF16)
    here[:, out_cols] = dot(left[:, lanes(0)], right[:, cols], TN)
    there[:, out_cols] = dot(left[:, lanes(far)], right[:, cols], TN)


def grads_fc1_kernel(ids, left, right, send, here, there):
    for c in range(2):
        cols = slice(512 * c, 512 * c + 512)
        blocks_of(X_FIRST, left, right, cols, send, here, there, cols)


def grads_fc2_kernel(ids, left, right, send, here, there):
    for c in range(2):
        cols = slice(512 * c, 512 * c + 512)
        blocks_of(Y_FIRST, left, right, cols, send, here, there, cols)


def grads_att_kernel(
    ids, rows, joined, branch, mixed, send_x, here_x, there_x, send_y, here_y, there_y
):
    blocks_of(X_FIRST, rows, joined, slice(0, 512), send_x, here_x, there_x, slice(0, 512))
    blocks_of(Y_FIRST, rows, joined, slice(512, 768), send_y, here_y, there_y, slice(0, 256))
    blocks_of(Y_FIRST, branch, mixed, slice(0, 256), send_y, here_y, there_y, slice(256, 512))


def fold_kernel(ids, here, there, got, other, whole):
    other[...] = (there[...] + got[1, :, :].astype(F32)).astype(BF16)
    whole[...] = here[...] + got[0, :, :].astype(F32)


def gather_kernel(ids, whole_x, got_x, whole_y, got_y, keep, send):
    n = whole_x.shape[1]
    for core in range(2):

        @pl.when(ids[CORE_ID] == core)
        def _():
            own = slice(128 * core, 128 * core + 128)
            other = slice(128 - 128 * core, 256 - 128 * core)
            for cols, whole, got in (
                (slice(0, n), whole_x, got_x),
                (slice(n, 2 * n), whole_y, got_y),
            ):
                for out, rows in ((keep, own), (send, other)):
                    total = whole[rows, :] + got[rows, :].astype(F32)
                    out[:, cols] = total.astype(BF16)


def away_kernel(ids, keep, got, out):
    @pl.when(ids[CORE_ID] == 0)
    def _():
        out[...] = got[...]

    @pl.when(ids[CORE_ID] != 0)
    def _():
        out[...] = keep[...]


def whole_sum(ids, keep, got, moved, cols):
    core = is_zero(ids[CORE_ID])
    own = pick(core, keep[:, cols].astype(F32), got[:, cols].astype(F32))
    return own + moved[:, cols].astype(F32)


def finish_mlp_kernel(ids, keep, got, moved, fc1, fc2):
    fc1[...] = whole_sum(ids, keep, got, moved, slice(0, 1024))
    fc2[...] = jnp.transpose(whole_sum(ids, keep, got, moved, slice(1024, 2048)))


def finish_att_kernel(ids, keep, got, moved, qkv, proj):
    for j in range(3):
        qkv[j, :, :] = whole_sum(ids, keep, got, moved, lanes(j))
    proj[...] = jnp.transpose(whole_sum(ids, keep, got, moved, lanes(PROJ)))


def tie(*values):
    return lax.optimization_barrier(values)


def sum_second(ids, first, second):
    n = first[1].shape[1]
    outs = [((256, n), BF16), ((256, n), F32)]
    other_x, whole_x = call(fold_kernel, outs, ids, *first)
    other_y, whole_y = call(fold_kernel, outs, ids, *second)
    return whole_x, other_x, whole_y, other_y


def send_second(whole_x, other_x, whole_y, other_y):
    return whole_x, swap(other_x, Y), whole_y, swap(other_y, X)


def sum_third(ids, parts):
    n = 2 * parts[0].shape[1]
    keep, send = call(gather_kernel, [((128, n), BF16)] * 2, ids, *parts)
    got = swap(send, CORE)
    (away,) = call(away_kernel, [((128, n), BF16)], ids, keep, got)
    return keep, got, away


def on_device_spread(
    clip_rows,
    out_grad,
    clip_valid,
    gain_rows,
    bias_rows,
    qkv_weight,
    qv_bias,
    proj_weight,
    fc1_weight,
    fc1_bias,
    fc2_weight,
):
    d, t = lax.axis_index("dp"), lax.axis_index("tensor")
    core = d & 1
    ids = jnp.stack([d >> 1, core, d, t, clip_valid[0]]).astype(jnp.int32)
    count = clip_rows.shape[0]
    half, own = count // 2, count // 4
    behind = (PAD + 8, 1024)
    plain = (PAD, 1024)
    packed = (VALUES + half, 128)
    wide = ((count, 1024), F32)

    def to_chips(keep, send):
        got = swap(send, CORE)
        shape = (2, *keep.shape[1:])
        return got, *call(pair_up_kernel, [(shape, BF16)] * 3, ids, keep, got)

    def over_chips(pairs):
        return [swap(pairs[m], CHIP_MASKS[m + 1]) for m in range(3)]

    def offer(shard, far):
        (send,) = call(offer_kernel, [(shard.shape, BF16)], ids, shard, far)
        return send

    def merge(shard, far, send):
        (out,) = call(
            merge_kernel, [((256, shard.shape[1]), BF16)], ids, shard, far, swap(send, CORE)
        )
        return out

    def trade(parts):
        return [parts[0]] + [swap(parts[m], CHIP_MASKS[m]) for m in range(1, 4)]

    params = jnp.concatenate(
        [
            jnp.pad(v, ((0, n - v.shape[0]), (0, 128 - v.shape[1])))
            for v, n in (
                (jnp.concatenate([gain_rows, bias_rows]), 8),
                (qv_bias.reshape(8, 8), 8),
                (fc1_bias, 8),
            )
        ]
    )
    shard_a, shard_g = call(
        shards_kernel,
        [((128, 1024), BF16), ((128, 1024), BF16)],
        ids,
        qkv_weight,
        proj_weight,
        fc2_weight,
    )
    far_a = swap(shard_a, Z_HIGH)
    own_rows = clip_rows
    keep, send = call(
        pack_kernel,
        [((4, 2 * PAD, 1024), BF16)] * 2,
        ids,
        own_rows,
        out_grad,
        params,
        scratch=[((400, 1024), F32), ((8, 2 * PAD, 1024), BF16)],
    )
    w0 = merge(shard_a, far_a, offer(shard_a, far_a))
    shard_f, _ = tie(fc1_weight, far_a)
    far_f = swap(shard_f, Z_HIGH)
    got, *pairs = to_chips(keep, send)
    *parts, w0 = tie(keep, got, *over_chips(pairs), w0)
    here, there, here_grad, there_grad, slots = call(
        pick_kernel,
        [(behind, BF16), (behind, BF16), (plain, BF16), (plain, BF16), ((16, 8, 128), F32)],
        ids,
        *parts,
    )
    r1, r2, r3 = swap(here, Z_LOW), swap(there, Z_HIGH), swap(there, Z_LOW | Z_HIGH)
    w1, w2 = swap(w0, X), swap(w0, Y)
    w_att = (w0, w1, w2, swap(w2[:, :512], X), swap(w1[:, 512:], Y))
    r1, r2, r3, far_f, shard_f = tie(r1, r2, r3, far_f, shard_f)
    f0 = merge(shard_f, far_f, offer(shard_f, far_f))
    rows, normed, vec, qkv_bias, b_fc1 = call(
        norm_one_kernel,
        [
            ((half, 1024), BF16),
            ((half, 1024), BF16),
            ((8, 1024), F32),
            ((8, 128), F32),
            ((1, 1024), F32),
        ],
        ids,
        here,
        r1,
        r2,
        r3,
        scratch=[((half, 1024), F32), ((8, 1024), F32)],
    )

    whole_one, *qkv = call(
        qkv_kernel,
        [((count, 1024), BF16)] + [(packed, BF16)] * 4,
        ids,
        normed,
        swap(normed, CORE),
        qkv_bias,
        *w_att,
        scratch=[wide, ((4, *packed), BF16)],
    )
    shard_g, *qkv = tie(shard_g, *qkv)
    far_g = swap(shard_g, Z_HIGH)
    *qkv, f0, here_grad, there_grad = tie(*trade(qkv), f0, here_grad, there_grad)
    f1, f2 = swap(f0, X), swap(f0, Y)
    s1, s2 = swap(here_grad, Z_LOW), swap(there_grad, Z_HIGH)
    tokens = 4 * count
    *mixed, back = call(
        attention_kernel,
        [((half, 128), BF16)] * 4 + [((tokens, 128), F32)],
        ids,
        *qkv,
        scratch=[((tokens, 192), F32)] + [((tokens, 64), BF16)] * 2 + [((tokens, 128), BF16)],
    )
    shard_g, far_g, *mixed = tie(shard_g, far_g, *mixed)
    g0 = merge(shard_g, far_g, offer(shard_g, far_g))
    *mixed, f1, f2, s1, s2 = tie(*trade(mixed), f1, f2, s1, s2)
    g1, g2 = swap(g0, X), swap(g0, Y)
    f3, g3, s3 = swap(f2, X), swap(g1, Y), swap(s2, Z_LOW)
    attended, keep, send = call(
        proj_kernel,
        [((count, 256), BF16), ((half, 1024), F32), ((half, 1024), BF16)],
        ids,
        *mixed,
        *w_att,
        scratch=[((4, half, 128), BF16), ((count, 256), F32)],
    )

    def pair(keep, send):
        return call(
            pair_kernel, [((half, 1024), F32), ((half, 1024), BF16)], ids, keep, swap(send, CORE)
        )

    def halve(keep, send):
        return call(
            half_kernel, [((own, 1024), F32), ((own, 1024), BF16)], ids, keep, swap(send, CORE)
        )

    part, send = pair(keep, send)
    away, s3 = tie(swap(send, Z_LOW), s3)
    w_fc1, w_fc2 = (f0, f1, f2, f3), (g0, g1, g2, g3)
    (grads,) = call(
        lay_grad_kernel,
        [((half, 1024), BF16)],
        ids,
        here_grad,
        s1,
        s2,
        s3,
        scratch=[((half, 1024), F32)],
    )
    residual, normed_two = call(
        norm_two_kernel,
        [((half, 1024), F32), ((half, 1024), BF16)],
        ids,
        rows,
        part,
        away,
        vec,
    )
    whole_two, whole_mlp, start, grad_hidden = call(
        mlp_start_kernel,
        [((count, 1024), BF16)] * 2 + [((count, 1024), F32)] * 2,
        ids,
        normed_two,
        swap(normed_two, CORE),
        grads,
        swap(grads, CORE),
        b_fc1,
        *w_fc1[:3],
        *w_fc2[:3],
        scratch=[wide],
    )

    hidden, grad_pre, sums_fc1, keep, send = call(
        fc_kernel,
        [((count, 1024), BF16)] * 2
        + [((1, 1024), F32), ((half, 1024), F32), ((half, 1024), BF16)],
        ids,
        whole_two,
        whole_mlp,
        start,
        grad_hidden,
        *w_fc1,
        w_fc2[3],
        scratch=[wide],
    )
    part, send = pair(keep, send)
    late = tie(send, whole_mlp, hidden, whole_two, grad_pre)
    grad_outs = [((2, 256, 1024), BF16), ((256, 1024), F32), ((256, 1024), F32)]
    cost = 2 * count * 1024 * 1024
    send_f, *rest_f = call(grads_fc1_kernel, grad_outs, ids, late[3], late[4])
    send_g, *rest_g = call(grads_fc2_kernel, grad_outs, ids, late[1], late[2])
    sums_f = (*rest_f, swap(send_f, X))
    sums_g = (*rest_g, swap(send_g, Y))
    keep_out, send_out = call(
        fc2_kernel,
        [((half, 1024), F32), ((half, 1024), BF16)],
        ids,
        late[2],
        *w_fc2,
    )
    away, keep_out, send_out = tie(swap(send, Z_LOW), keep_out, send_out)
    part_out, send_out = halve(keep_out, send_out)
    away_out = swap(send_out, Z_LOW)
    grad_residual, grad_branch, sums_two = call(
        norm_two_back_kernel,
        [((half, 1024), F32), ((half, 1024), BF16), ((8, 1024), F32)],
        ids,
        residual,
        part,
        away,
        grads,
        vec,
    )

    whole_branch, *grad_att = call(
        grad_att_kernel,
        [((count, 1024), BF16)] + [((half, 128), BF16)] * 4,
        ids,
        grad_branch,
        swap(grad_branch, CORE),
        *w_att,
        scratch=[wide, ((4, half, 128), BF16)],
    )
    *grad_att, part_out, away_out = tie(*grad_att, part_out, away_out)
    here_out, there_out = call(
        layer_out_kernel,
        [(plain, BF16)] * 2,
        ids,
        residual,
        part_out,
        away_out,
        vec,
        scratch=[((2 * PAD, 1024), F32)],
    )
    sums_mlp = sum_second(ids, sums_f, sums_g)
    *grad_att, whole_x, other_x, whole_y, other_y, here_out, there_out = tie(
        *trade(grad_att), *sums_mlp, here_out, there_out
    )
    sums_mlp = send_second(whole_x, other_x, whole_y, other_y)
    away_out = swap(there_out, Z_HIGH)
    grad_qkv = call(
        attention_back_kernel,
        [(packed, BF16)] * 4,
        ids,
        *qkv,
        *grad_att,
        back,
        scratch=[((tokens, 192), F32)] + [((tokens, 128), BF16)] * 4 + [((tokens, 64), F32)] * 2,
    )
    *grad_qkv, away_out, whole_x, got_x, whole_y, got_y = tie(*grad_qkv, away_out, *sums_mlp)
    *sums_mlp, moved_mlp = sum_third(ids, (whole_x, got_x, whole_y, got_y))
    moved_mlp = swap(moved_mlp, Z_HIGH)
    keep_out, send_out = call(
        give_out_kernel, [((4, PAD, 1024), BF16)] * 2, ids, slots, here_out, away_out
    )
    got_out, *pairs_out = to_chips(keep_out, send_out)
    *grad_qkv, got_out, p1, p2, p3 = tie(*trade(grad_qkv), got_out, *pairs_out)
    parts_out = over_chips((p1, p2, p3))
    joined, keep, send, sums_qv = call(
        qkv_back_kernel,
        [((count, 768), BF16), ((half, 1024), F32), ((half, 1024), BF16), ((1, 1024), F32)],
        ids,
        *grad_qkv,
        *w_att,
        scratch=[((4, *packed), BF16), ((count, 256), F32)],
    )
    part, send, small = call(
        half_grad_kernel,
        [((own, 1024), F32), ((SMALL + 8, 1024), BF16), ((8, 1024), F32)],
        ids,
        keep,
        swap(send, CORE),
        rows,
        sums_two,
        sums_fc1,
        sums_qv,
    )
    late = tie(send, whole_one, joined, whole_branch, attended)
    grad_outs = [((2, 256, 512), BF16), ((256, 512), F32), ((256, 512), F32)]
    send_x, here_x, there_x, send_y, here_y, there_y = call(
        grads_att_kernel, grad_outs * 2, ids, *late[1:]
    )
    away, send_x, send_y, *parts_out = tie(swap(send, Z_LOW), send_x, send_y, *parts_out)
    parts_out = keep_out, got_out, *parts_out
    got_x, got_y = swap(send_x, X), swap(send_y, Y)
    here, there = call(
        norm_one_back_kernel,
        [(behind, BF16)] * 2,
        ids,
        rows,
        part,
        away,
        grad_residual,
        vec,
        small,
        scratch=[((2 * PAD, 1024), F32)],
    )
    away, got_x, got_y, moved_mlp = tie(swap(there, Z_HIGH), got_x, got_y, moved_mlp)
    sums_att = sum_second(ids, (here_x, there_x, got_x), (here_y, there_y, got_y))
    keep, send = call(
        give_kernel,
        [((4, PAD, 1024), BF16)] * 2,
        ids,
        slots,
        here,
        away,
        scratch=[((8, 1024), F32), ((8, 1024), F32), (plain, F32)],
    )
    got, *pairs = to_chips(keep, send)
    whole_x, other_x, whole_y, other_y = sums_att
    parts = keep, got, *over_chips(pairs)
    *sums_att, moved_att = sum_third(ids, send_second(whole_x, other_x, whole_y, other_y))
    moved_att = swap(moved_att, Z_HIGH)
    input_grad, grad_gains, grad_biases, grad_last, grad_qv, grad_b_fc1 = call(
        take_kernel,
        [
            ((count, 1024), F32),
            ((2, 32), F32),
            ((4, 32), F32),
            ((1, 32), F32),
            ((8, 8), F32),
            ((1, 128), F32),
        ],
        ids,
        *parts,
        scratch=[((8, PAD, 1024), F32)],
    )
    (layer_out,) = call(
        take_out_kernel,
        [((count, 1024), BF16)],
        ids,
        *parts_out,
        scratch=[((8, PAD, 1024), F32), wide],
    )
    grad_fc1, grad_fc2 = call(
        finish_mlp_kernel,
        [((128, 1024), F32), ((1024, 128), F32)],
        ids,
        *sums_mlp,
        moved_mlp,
    )
    moved_att, _ = tie(moved_att, input_grad)
    grad_w, grad_proj = call(
        finish_att_kernel,
        [((3, 128, 256), F32), ((256, 128), F32)],
        ids,
        *sums_att,
        moved_att,
    )
    return (
        layer_out,
        input_grad,
        grad_gains,
        grad_biases,
        grad_w,
        grad_qv.reshape(2, 4, 8),
        grad_proj,
        grad_fc1,
        grad_b_fc1,
        grad_fc2,
        grad_last[0],
    )


def solution(mesh):
    spread = (mesh.shape["dp"], mesh.shape["tensor"]) == (8, 4)
    in_specs = (
        P(("dp", "tensor"), None),
        P(("dp", "tensor"), None),
        P("dp"),
        P(None, ("dp", "tensor")),
        P(None, ("dp", "tensor")),
        P(None, "dp", "tensor"),
        P(None, "tensor", "dp"),
        P("tensor", "dp"),
        P("dp", "tensor"),
        P("tensor", "dp"),
        P("tensor", "dp"),
    )
    out_specs = (
        P(("dp", "tensor"), None),
        P(("dp", "tensor"), None),
        P(None, ("dp", "tensor")),
        P(None, ("dp", "tensor")),
        P(None, "dp", "tensor"),
        P(None, "tensor", "dp"),
        P("tensor", "dp"),
        P("dp", "tensor"),
        P("tensor", "dp"),
        P("tensor", "dp"),
        P(("dp", "tensor")),
    )
    return jax.shard_map(
        on_device_spread if spread else on_device, mesh=mesh, in_specs=in_specs, out_specs=out_specs, check_vma=False
    )
```

```python
import math

import jax
import jax.numpy as jnp
from jax import lax
from jax.experimental import pallas as pl
from jax.experimental.pallas import tpu as pltpu
from jax.sharding import PartitionSpec as P

HD = 64


norm_eps = 1e-06
root_half = 0.7071067811865476
inv_root_tau = 0.3989422804014327


def normalize(values, gain_row, shift_row):
    centre = jnp.mean(values, axis=1, keepdims=True)
    offsets = values - centre
    inverse = lax.rsqrt(jnp.mean(offsets * offsets, axis=1, keepdims=True) + norm_eps)
    scaled = offsets * inverse
    return (scaled * gain_row + shift_row, scaled, inverse)


def normalize_back(upstream, scaled, inverse, gain_row):
    grad_hat = upstream * gain_row
    return (
        grad_hat
        - jnp.mean(grad_hat, axis=1, keepdims=True)
        - scaled * jnp.mean(grad_hat * scaled, axis=1, keepdims=True)
    ) * inverse


def gelu_value(inputs):
    return 0.5 * inputs * (1.0 + lax.erf(inputs * root_half))


def gelu_slope(inputs):
    return (
        0.5 * (1.0 + lax.erf(inputs * root_half))
        + inputs * jnp.exp(-0.5 * inputs * inputs) * inv_root_tau
    )


def fetch(qkv_weight, proj_weight, fc1_weight, fc2_weight, qv_bias, fc1_bias, gain_rows, bias_rows):
    matrices = (
        lax.all_gather(qkv_weight, "dp", axis=1, tiled=True),
        lax.all_gather(proj_weight, "dp", axis=1, tiled=True),
        lax.all_gather(fc1_weight, "dp", axis=0, tiled=True),
        lax.all_gather(fc2_weight, "dp", axis=1, tiled=True),
        lax.all_gather(qv_bias, "dp", axis=2, tiled=True),
        lax.all_gather(fc1_bias, "dp", axis=1, tiled=True),
    )
    vectors = (
        lax.all_gather(gain_rows, ("dp", "tensor"), axis=1, tiled=True),
        lax.all_gather(bias_rows, ("dp", "tensor"), axis=1, tiled=True),
    )
    return (matrices, (vectors[0].astype(jnp.float32), vectors[1].astype(jnp.float32)))


def spread_rows(local_rows):
    return lax.all_gather(local_rows, "tensor", axis=0, tiled=True)


def reduce_rows(term_fn, row_count):
    return lax.psum_scatter(
        term_fn(jnp.int32(0), lax.axis_size("tensor") * row_count),
        "tensor",
        scatter_dimension=0,
        tiled=True,
    )


def spread_grads(local_rows):
    return lax.all_gather(local_rows, "tensor", axis=0, tiled=True)


def reduce_grads(term_fn, row_count):
    return lax.psum_scatter(
        term_fn(jnp.int32(0), lax.axis_size("tensor") * row_count),
        "tensor",
        scatter_dimension=0,
        tiled=True,
    )


def forward(clip_rows, matrices, vectors):
    w_qkv, w_proj, w_fc1, w_fc2, b_qv, b_fc1 = matrices
    gain_rows, bias_rows = vectors
    row_count = clip_rows.shape[0]
    head_cols = w_qkv.shape[2]
    heads_here = head_cols // HD
    score_scale = 1.0 / math.sqrt(HD)
    inputs = clip_rows.astype(jnp.float32)
    normed_one, scaled_one, inverse_one = normalize(inputs, gain_rows[0], bias_rows[0])
    whole_one = spread_rows(normed_one.astype(jnp.bfloat16))
    seq_len = whole_one.shape[0]
    projected = jnp.einsum("sd,jde->jse", whole_one, w_qkv, preferred_element_type=jnp.float32)
    bias_cols = b_qv.reshape(2, head_cols).astype(jnp.float32)
    queries = (projected[0] + bias_cols[0]).astype(jnp.bfloat16).reshape(seq_len, heads_here, HD)
    keys_all = projected[1].astype(jnp.bfloat16).reshape(seq_len, heads_here, HD)
    values_all = (projected[2] + bias_cols[1]).astype(jnp.bfloat16).reshape(seq_len, heads_here, HD)
    scores = (
        jnp.einsum("qhd,khd->hqk", queries, keys_all, preferred_element_type=jnp.float32)
        * score_scale
    )
    top_score = jnp.max(scores, axis=2, keepdims=True)
    weights_exp = jnp.exp(scores - top_score)
    totals = jnp.sum(weights_exp, axis=2, keepdims=True)
    attn_probs = (weights_exp / totals).astype(jnp.bfloat16)
    log_total = top_score + jnp.log(totals)
    attended = (
        jnp.einsum("hqk,khd->qhd", attn_probs, values_all, preferred_element_type=jnp.float32)
        .reshape(seq_len, head_cols)
        .astype(jnp.bfloat16)
    )

    def proj_term(offset, length):
        return jnp.dot(attended, w_proj, preferred_element_type=jnp.float32)

    residual_one = inputs + (reduce_rows(proj_term, row_count) + bias_rows[2])
    normed_two, scaled_two, inverse_two = normalize(residual_one, gain_rows[1], bias_rows[1])
    whole_two = spread_rows(normed_two.astype(jnp.bfloat16))
    pre_act = jnp.dot(whole_two, w_fc1, preferred_element_type=jnp.float32) + b_fc1.reshape(
        -1
    ).astype(jnp.float32)
    hidden = gelu_value(pre_act).astype(jnp.bfloat16)

    def fc2_term(offset, length):
        return jnp.dot(hidden, w_fc2, preferred_element_type=jnp.float32)

    layer_out = residual_one + (reduce_rows(fc2_term, row_count) + bias_rows[3])
    stored = (
        scaled_one,
        inverse_one,
        whole_one,
        queries,
        keys_all,
        values_all,
        log_total,
        attended,
        scaled_two,
        inverse_two,
        whole_two,
        pre_act,
        hidden,
    )
    return (layer_out, stored)


def backward(upstream, matrices, vectors, stored):
    w_qkv, w_proj, w_fc1, w_fc2, b_qv, b_fc1 = matrices
    gain_rows, bias_rows = vectors
    (
        scaled_one,
        inverse_one,
        whole_one,
        queries,
        keys_all,
        values_all,
        log_total,
        attended,
        scaled_two,
        inverse_two,
        whole_two,
        pre_act,
        hidden,
    ) = stored
    row_count = upstream.shape[0]
    seq_len = queries.shape[0]
    heads_here = queries.shape[1]
    head_cols = heads_here * HD
    score_scale = 1.0 / math.sqrt(HD)
    grad_mlp = upstream.astype(jnp.bfloat16)
    grad_fc2_bias = jnp.sum(grad_mlp.astype(jnp.float32), axis=0)
    whole_mlp = spread_grads(grad_mlp)
    grad_fc2 = jnp.einsum("sf,sd->fd", hidden, whole_mlp, preferred_element_type=jnp.float32)
    grad_hidden = jnp.einsum("sd,fd->sf", whole_mlp, w_fc2, preferred_element_type=jnp.float32)
    grad_pre = (grad_hidden * gelu_slope(pre_act)).astype(jnp.bfloat16)
    grad_fc1_bias = jnp.sum(grad_pre.astype(jnp.float32), axis=0)
    grad_fc1 = jnp.einsum("sd,sf->df", whole_two, grad_pre, preferred_element_type=jnp.float32)

    def fc1_back(offset, length):
        return jnp.einsum("sf,df->sd", grad_pre, w_fc1, preferred_element_type=jnp.float32)

    grad_normed_two = reduce_grads(fc1_back, row_count)
    grad_residual = upstream + normalize_back(
        grad_normed_two, scaled_two, inverse_two, gain_rows[1]
    )
    grad_branch = grad_residual.astype(jnp.bfloat16)
    grad_proj_bias = jnp.sum(grad_branch.astype(jnp.float32), axis=0)
    whole_branch = spread_grads(grad_branch)
    grad_proj = jnp.einsum("se,sd->ed", attended, whole_branch, preferred_element_type=jnp.float32)
    grad_att = (
        jnp.einsum("sd,ed->se", whole_branch, w_proj, preferred_element_type=jnp.float32)
        .astype(jnp.bfloat16)
        .reshape(seq_len, heads_here, HD)
    )
    scores = (
        jnp.einsum("qhd,khd->hqk", queries, keys_all, preferred_element_type=jnp.float32)
        * score_scale
    )
    attn_probs = jnp.exp(scores - log_total)
    grad_probs = jnp.einsum(
        "qhd,khd->hqk", grad_att, values_all, preferred_element_type=jnp.float32
    )
    row_dot = jnp.sum(attn_probs * grad_probs, axis=2, keepdims=True)
    grad_scores = (attn_probs * (grad_probs - row_dot)).astype(jnp.bfloat16)
    grad_query = (
        jnp.einsum("hqk,khd->qhd", grad_scores, keys_all, preferred_element_type=jnp.float32)
        * score_scale
    ).astype(jnp.bfloat16)
    grad_key = (
        jnp.einsum("hqk,qhd->khd", grad_scores, queries, preferred_element_type=jnp.float32)
        * score_scale
    ).astype(jnp.bfloat16)
    grad_value = jnp.einsum(
        "hqk,qhd->khd",
        attn_probs.astype(jnp.bfloat16),
        grad_att,
        preferred_element_type=jnp.float32,
    ).astype(jnp.bfloat16)
    grad_qkv = jnp.stack([grad_query, grad_key, grad_value]).reshape(3, seq_len, head_cols)
    grad_qv = jnp.stack(
        [
            jnp.sum(grad_query.astype(jnp.float32), axis=0),
            jnp.sum(grad_value.astype(jnp.float32), axis=0),
        ]
    )
    grad_qkv_weight = jnp.einsum(
        "sd,jse->jde", whole_one, grad_qkv, preferred_element_type=jnp.float32
    )

    def qkv_back(offset, length):
        return jnp.einsum("jse,jde->sd", grad_qkv, w_qkv, preferred_element_type=jnp.float32)

    grad_normed_one = reduce_grads(qkv_back, row_count)
    grad_input = grad_residual + normalize_back(
        grad_normed_one, scaled_one, inverse_one, gain_rows[0]
    )
    grad_gain = jnp.stack(
        [
            jnp.sum(grad_normed_one * scaled_one, axis=0),
            jnp.sum(grad_normed_two * scaled_two, axis=0),
        ]
    )
    grad_bias = jnp.stack(
        [
            jnp.sum(grad_normed_one, axis=0),
            jnp.sum(grad_normed_two, axis=0),
            grad_proj_bias,
            grad_fc2_bias,
        ]
    )
    weight_part = (
        lax.psum_scatter(grad_qkv_weight, "dp", scatter_dimension=1, tiled=True),
        lax.psum_scatter(grad_proj, "dp", scatter_dimension=1, tiled=True),
        lax.psum_scatter(grad_fc1, "dp", scatter_dimension=0, tiled=True),
        lax.psum_scatter(grad_fc2, "dp", scatter_dimension=1, tiled=True),
        lax.psum_scatter(grad_qv, "dp", scatter_dimension=2, tiled=True),
        lax.psum_scatter(grad_fc1_bias.reshape(1, -1), "dp", scatter_dimension=1, tiled=True),
    )
    vector_part = (
        lax.psum_scatter(grad_gain, ("dp", "tensor"), scatter_dimension=1, tiled=True),
        lax.psum_scatter(grad_bias, ("dp", "tensor"), scatter_dimension=1, tiled=True),
    )
    return (grad_input, weight_part, vector_part)


def on_device(
    clip_rows,
    out_grad,
    clip_valid,
    gain_rows,
    bias_rows,
    qkv_weight,
    qv_bias,
    proj_weight,
    fc1_weight,
    fc1_bias,
    fc2_weight,
):
    clip_weight = clip_valid[0].astype(jnp.float32)
    upstream = out_grad.astype(jnp.float32) * clip_weight
    matrices, vectors = fetch(
        qkv_weight, proj_weight, fc1_weight, fc2_weight, qv_bias, fc1_bias, gain_rows, bias_rows
    )
    layer_out, stored = forward(clip_rows, matrices, vectors)
    matrices, vectors = fetch(
        qkv_weight, proj_weight, fc1_weight, fc2_weight, qv_bias, fc1_bias, gain_rows, bias_rows
    )
    unused_out, stored = forward(clip_rows, matrices, vectors)
    grad_input, weight_part, vector_part = backward(upstream, matrices, vectors, stored)
    return (
        (layer_out * clip_weight).astype(jnp.bfloat16),
        grad_input,
        vector_part[0],
        vector_part[1],
        weight_part[0],
        weight_part[4],
        weight_part[1],
        weight_part[2],
        weight_part[5],
        weight_part[3],
        vector_part[1][3],
    )


AXES = ("dp", "tensor")
Z_LOW, Z_HIGH, CORE, X, Y = 1, 2, 4, 8, 16
CHIP_MASKS = (0, X, Y, X | Y)
BF16, F32 = jnp.bfloat16, jnp.float32
NN, NT, TN = ((1,), (0,)), ((1,), (1,)), ((0,), (0,))
SHARE = 49
PAD = 56
SMALL = 104
CHIP_ID, CORE_ID, D_ID, T_ID = range(4)


def swap(value, mask):
    return lax.ppermute(value, AXES, [(i, i ^ mask) for i in range(32)])


def dot(left, right, dims):
    return lax.dot_general(left, right, (dims, ((), ())), preferred_element_type=F32)


TIMES = {
    "pack": 1.2,
    "pick": 1.5,
    "norm_one": 1.0,
    "qkv": 0.8,
    "qkv_start": 1.4,
    "attention": 7.6,
    "proj": 1.1,
    "norm_two": 0.9,
    "mlp_start": 1.0,
    "fc": 5.0,
    "grads_fc1": 1.8,
    "grads_fc2": 1.8,
    "fc2": 1.6,
    "norm_two_back": 1.5,
    "grad_att": 1.1,
    "attention_back": 12.0,
    "qkv_back": 1.5,
    "half_grad": 1.1,
    "grads_att": 1.8,
    "norm_one_back": 1.0,
    "give": 1.3,
    "take": 2.0,
    "finish_mlp": 1.7,
    "finish_att": 1.4,
}


SPACE = {"attention_kernel": 16, "attention_back_kernel": 12}


def call(body, outs, scalars, *args, scratch=()):
    moved = sum(math.prod(a.shape) * a.dtype.itemsize for a in args)
    moved += sum(math.prod(s) * jnp.dtype(t).itemsize for s, t in outs)
    held = sum(math.prod(s[:-1]) * max(s[-1], 128) * jnp.dtype(t).itemsize for s, t in scratch)
    time = TIMES.get(body.__name__.removesuffix("_kernel"), 0.7)
    return pl.pallas_call(
        body,
        out_shape=[jax.ShapeDtypeStruct(s, t) for s, t in outs],
        in_specs=[pl.BlockSpec(memory_space=pltpu.SMEM)]
        + [pl.BlockSpec(memory_space=pltpu.VMEM)] * len(args),
        out_specs=[pl.BlockSpec(memory_space=pltpu.VMEM)] * len(outs),
        scratch_shapes=[pltpu.VMEM(s, t) for s, t in scratch],
        compiler_params=pltpu.CompilerParams(vmem_limit_bytes=moved + held + (SPACE.get(body.__name__, 4) << 20)),
        cost_estimate=pl.CostEstimate(
            flops=int(time * 1.15e9), bytes_accessed=moved, transcendentals=0
        ),
    )(scalars, *args)


def chip_lanes(ids, m):
    return pl.ds(pl.multiple_of((ids[CHIP_ID] ^ m) * 256, 256), 256)


def lanes(m):
    return slice(256 * m, 256 * m + 256)


def row_ids(shape):
    return lax.broadcasted_iota(jnp.int32, shape, 0)


def pick(condition, left, right):
    return jnp.where(jnp.full(left.shape, condition, jnp.int32) != 0, left, right)


def is_zero(number):
    return jnp.where(number == 0, 1, 0)


def z_low(ids):
    return ids[T_ID] & 1


def z_high(ids):
    return ids[T_ID] >> 1


def far_chips(ids, core_flip):
    return [(ids[CHIP_ID] ^ m) * 2 + (ids[CORE_ID] ^ core_flip) for m in range(4)]


def pack_kernel(ids, rows, grads, params, keep, send, wide, stage):
    lane32 = lax.broadcasted_iota(jnp.int32, (32, 128), 1)
    spot = (lane32 == row_ids((32, 128)) + 32 * ids[T_ID]).astype(F32).astype(BF16)
    lane8 = lax.broadcasted_iota(jnp.int32, (8, 128), 1)
    spot8 = (lane8 == row_ids((8, 128)) + 8 * ids[D_ID]).astype(F32).astype(BF16)
    placed = dot(params[0:8, 0:32], spot, NN)
    qv_rows = dot(params[8:16, 0:8], spot8, NN)
    row_a = jnp.concatenate(
        [placed[k : k + 1] for k in range(6)]
        + [params[...].astype(F32)[16:17], jnp.zeros((1, 128), F32)],
        axis=1,
    )
    row_b = jnp.concatenate([qv_rows[k : k + 1] for k in range(8)], axis=1)
    flag = jnp.full((PAD, 1024), ids[4], jnp.int32).astype(F32)
    row = row_ids((PAD, 1024))
    tail = jnp.where(row == SHARE, row_a, jnp.where(row == SHARE + 1, row_b, flag))
    wide[0 : rows.shape[0], :] = rows[...].astype(F32)
    for j in range(8):
        block = wide[SHARE * j : SHARE * j + PAD, :]
        stage[j, 0:PAD, :] = jnp.where(row < SHARE, block, tail).astype(BF16)
    wide[0 : rows.shape[0], :] = grads[...].astype(F32)
    for j in range(8):
        stage[j, PAD : 2 * PAD, :] = wide[SHARE * j : SHARE * j + PAD, :].astype(BF16)
    for m, (d0, d1) in enumerate(zip(far_chips(ids, 0), far_chips(ids, 1))):
        keep[m, :, :] = stage[d0, :, :]
        send[m, :, :] = stage[d1, :, :]


def pair_up_kernel(ids, keep, got, o1, o2, o3):
    for m, out in enumerate((o1, o2, o3)):
        out[0, :, :] = keep[m + 1, :, :]
        out[1, :, :] = got[m + 1, :, :]


def arrived(ids, keep, got, d1, d2, d3):
    parts = []
    for m, (a0, a1) in enumerate(zip(far_chips(ids, 0), far_chips(ids, 1))):
        first, second = ((keep, 0), (got, 0)) if m == 0 else (((d1, d2, d3)[m - 1], k) for k in range(2))
        parts += [(a0, *first), (a1, *second)]
    return parts


def pick_kernel(ids, keep, got, d1, d2, d3, here, there, here_grad, there_grad, slots):
    row8 = row_ids((8, 1024))
    row = row_ids((PAD, 1024))
    mine = jnp.zeros((PAD, 1024), F32)
    other, mine_grad, other_grad = mine, mine, mine
    params = jnp.zeros((8, 1024), F32)
    qv = jnp.zeros((1, 1024), F32)
    high = jnp.full((1, 1024), z_high(ids), jnp.int32).astype(F32)
    parts = arrived(ids, keep, got, d1, d2, d3)
    flags = [
        ref[k, PAD - 8 : PAD, :].astype(F32)[SHARE + 10 - PAD : SHARE + 11 - PAD]
        for _, ref, k in parts
    ]
    for i, (a, ref, k) in enumerate(parts):
        seen = jnp.zeros((1, 1024), F32)
        for (c, _, _), flag in zip(parts, flags):
            earlier = jnp.full((1, 1024), jnp.where(c < a, 1, 0), jnp.int32).astype(F32)
            seen = seen + flag * earlier
        block = ref[k, 0:PAD, :].astype(F32)
        grad = ref[k, PAD : 2 * PAD, :].astype(F32)
        is_mine = jnp.where(seen == high, flags[i], 0.0)
        is_other = flags[i] - is_mine
        mine = jnp.where(is_mine > 0.5, block, mine)
        other = jnp.where(is_other > 0.5, block, other)
        mine_grad = jnp.where(is_mine > 0.5, grad, mine_grad)
        other_grad = jnp.where(is_other > 0.5, grad, other_grad)
        params = jnp.where(row8 == a, block[SHARE : SHARE + 1], params)
        qv = qv + block[SHARE + 1 : SHARE + 2]
        slots[a, :, :] = jnp.broadcast_to(is_mine[:, 0:128], (8, 128))
        slots[8 + a, :, :] = jnp.broadcast_to(is_other[:, 0:128], (8, 128))
    for value, out in ((mine, here), (other, there)):
        out[0:PAD, :] = jnp.where(row == PAD - 1, qv, value).astype(BF16)
        out[PAD : PAD + 8, :] = params.astype(BF16)
    here_grad[...] = mine_grad.astype(BF16)
    there_grad[...] = other_grad.astype(BF16)


def lay_rows(ids, here, r1, r2, r3, wide):
    low = is_zero(z_low(ids))
    for m in range(4):
        cols = chip_lanes(ids, m)
        blocks = [ref[0:PAD, cols].astype(F32) for ref in (here, r1, r2, r3)]
        order = (
            pick(low, blocks[0], blocks[1]),
            pick(low, blocks[2], blocks[3]),
            pick(low, blocks[1], blocks[0]),
            pick(low, blocks[3], blocks[2]),
        )
        for i, block in enumerate(order):
            wide[SHARE * i : SHARE * i + SHARE, lanes(m)] = block[0:SHARE]


def norm_parts(values):
    centre = jnp.mean(values, axis=1, keepdims=True)
    offsets = values - centre
    inverse = lax.rsqrt(jnp.mean(offsets * offsets, axis=1, keepdims=True) + norm_eps)
    return offsets * inverse, inverse


def norm_one_kernel(ids, here, r1, r2, r3, rows, normed, vec, qv_bias, b_fc1, wide, small):
    lay_rows(ids, here, r1, r2, r3, wide)
    own = here[PAD - 8 : PAD + 8, :].astype(F32)
    far = r2[PAD - 8 : PAD + 8, :].astype(F32)
    tails = [own[8:], far[8:]] + [r[PAD : PAD + 8, :].astype(F32) for r in (r1, r3)]
    params = tails[0] + tails[1] + tails[2] + tails[3]
    small[...] = jnp.zeros_like(small)
    for d in range(8):
        for k in range(6):
            small[k : k + 1, 128 * d : 128 * d + 128] = params[
                d : d + 1, 128 * k : 128 * k + 128
            ]
    for m in range(4):
        vec[:, lanes(m)] = small[:, chip_lanes(ids, m)]
    home = pick(is_zero(ids[CORE_ID]), own, far)
    for k in range(8):
        qv_bias[k : k + 1, :] = home[7:8, 128 * k : 128 * k + 128]
        b_fc1[0:1, 128 * k : 128 * k + 128] = home[8 + k : 9 + k, 768:896]
    values = wide[...]
    scaled, _ = norm_parts(values)
    rows[...] = values.astype(BF16)
    normed[...] = (scaled * vec[0:1, :] + vec[2:3, :]).astype(BF16)


def lay_grad_kernel(ids, here, r1, r2, r3, out, wide):
    lay_rows(ids, here, r1, r2, r3, wide)
    out[...] = wide[...].astype(BF16)


def join_rows(wide, own, got):
    half = own.shape[0]
    wide[0:half, :] = own[...].astype(F32)
    wide[half : 2 * half, :] = got[...].astype(F32)


PROJ = 3


def part_of(weights, m, j):
    if m < 3:
        return weights[m][:, lanes(j)]
    return weights[3 + j // 2][:, lanes(j % 2)]


VALUES = 400


def fold_rows(value):
    half = value.shape[0] // 2
    return jnp.concatenate([value[:half], value[half:]], axis=1)


def qkv_start_kernel(ids, own, got, w0, w1, w2, whole, start, wide):
    join_rows(wide, own, got)
    whole[...] = wide[...].astype(BF16)
    for j in range(3):
        total = dot(whole[:, lanes(0)], w0[:, lanes(j)], NN)
        for m, weight in ((1, w1), (2, w2)):
            total = total + dot(whole[:, lanes(m)], weight[:, lanes(j)], NN)
        start[:, lanes(j)] = total


def qkv_kernel(ids, whole, start, qv_bias, w3, w4, o0, o1, o2, o3, heads):
    for j in range(3):
        weight = (w3, w4)[j // 2][:, lanes(j % 2)]
        total = start[:, lanes(j)] + dot(whole[:, lanes(3)], weight, NN)
        for h in range(4):
            part = total[:, 64 * h : 64 * h + 64]
            if j != 1:
                k = (j // 2) * 4 + h
                part = part + qv_bias[k : k + 1, 0:64]
            if j < 2:
                heads[h, 0 : part.shape[0], 64 * j : 64 * j + 64] = part.astype(BF16)
            else:
                heads[h, VALUES:, :] = fold_rows(part).astype(BF16)
    for m, out in enumerate((o0, o1, o2, o3)):
        out[...] = heads[ids[CHIP_ID] ^ m, :, :]


STEP, BACK_STEP = 392, 112


def stage_qkv(stage, parts):
    tokens = stage.shape[0] // 4
    half = tokens // 2
    for m, part in enumerate(parts):
        start = tokens * m
        stage[start : start + tokens, 0:128] = part[0:tokens, :].astype(F32)
        stage[start : start + half, 128:192] = part[VALUES:, 0:64].astype(F32)
        stage[start + half : start + tokens, 128:192] = part[VALUES:, 64:128].astype(F32)


def attention_kernel(ids, a0, a1, a2, a3, o0, o1, o2, o3, back, stage, q, k, v):
    tokens = stage.shape[0] // 4
    stage_qkv(stage, (a0, a1, a2, a3))
    q[...] = (stage[:, 0:64] * 0.125).astype(BF16)
    k[...] = stage[:, 64:128].astype(BF16)
    v[:, 0:64] = stage[:, 128:192].astype(BF16)
    v[:, 64:128] = jnp.ones((v.shape[0], 64), BF16)
    for i in range(stage.shape[0] // STEP):
        rows = slice(i * STEP, i * STEP + STEP)
        scores = dot(q[rows, :], k[...], NT)
        top = jnp.max(scores, axis=1, keepdims=True)
        mixed = dot(jnp.exp(scores - top).astype(BF16), v[...], NN)
        total = mixed[:, 64:128]
        back[rows, 0:64] = mixed[:, 0:64] / total
        back[rows, 64:128] = top + jnp.log(total)
    for m, out in enumerate((o0, o1, o2, o3)):
        out[...] = fold_rows(back[tokens * m : tokens * m + tokens, 0:64]).astype(BF16)


def with_shift(value, shift):
    high = shift.astype(BF16).astype(F32)
    middle = (shift - high).astype(BF16).astype(F32)
    low = shift - high - middle
    lane = lax.broadcasted_iota(jnp.int32, (value.shape[0], 64), 1)
    extra = jnp.where(lane == 0, -high, jnp.where(lane == 1, -middle, jnp.where(lane == 2, -low, 0.0)))
    return jnp.concatenate([value, extra], axis=1).astype(BF16)


def with_ones(value):
    lane = lax.broadcasted_iota(jnp.int32, (value.shape[0], 64), 1)
    return jnp.concatenate([value, jnp.where(lane < 3, 1.0, 0.0)], axis=1).astype(BF16)


def attention_back_kernel(
    ids, a0, a1, a2, a3, g0, g1, g2, g3, back, o0, o1, o2, o3, stage, q, k, v, g, grad_k, grad_v
):
    tokens = stage.shape[0] // 4
    stage_qkv(stage, (a0, a1, a2, a3))
    q[...] = with_shift(stage[:, 0:64] * 0.125, back[:, 64:65])
    k[...] = with_ones(stage[:, 64:128])
    v[...] = with_ones(stage[:, 128:192])
    for m, part in enumerate((g0, g1, g2, g3)):
        middle = tokens * m + tokens // 2
        stage[tokens * m : middle, 0:64] = part[:, 0:64].astype(F32)
        stage[middle : tokens * m + tokens, 0:64] = part[:, 64:128].astype(F32)
    grads = stage[:, 0:64]
    g[...] = with_shift(grads, jnp.sum(grads * back[:, 0:64], axis=1, keepdims=True))
    keys_t = jnp.transpose(k[:, 0:64])
    for i in range(stage.shape[0] // BACK_STEP):
        rows = slice(i * BACK_STEP, i * BACK_STEP + BACK_STEP)
        probs = jnp.exp(dot(k[...], q[rows, :], NT))
        grad_scores = (probs * dot(v[...], g[rows, :], NT)).astype(BF16)
        part_v = dot(probs.astype(BF16), g[rows, 0:64], NN)
        part_k = dot(grad_scores, q[rows, 0:64], NN)
        grad_v[...] = part_v if i == 0 else grad_v[...] + part_v
        grad_k[...] = part_k if i == 0 else grad_k[...] + part_k
        stage[rows, 0:64] = jnp.transpose(dot(keys_t, grad_scores, NN)) * 0.125
    for m, out in enumerate((o0, o1, o2, o3)):
        rows = slice(tokens * m, tokens * m + tokens)
        out[0:tokens, 0:64] = stage[rows, 0:64].astype(BF16)
        out[0:tokens, 64:128] = grad_k[rows, :].astype(BF16)
        out[VALUES:, :] = fold_rows(grad_v[rows, :]).astype(BF16)


def split_rows(total, keep, send, cols):
    half = keep.shape[0]
    keep[:, cols] = total[:half]
    send[:, cols] = total[half:].astype(BF16)


def proj_kernel(ids, a0, a1, a2, a3, w0, w1, w2, w3, w4, joined, keep, send, heads, wide):
    for m, part in enumerate((a0, a1, a2, a3)):
        heads[m, :, :] = part[...]
    half = keep.shape[0]
    for h in range(4):
        part = heads[h ^ ids[CHIP_ID], :, :].astype(F32)
        wide[0:half, 64 * h : 64 * h + 64] = part[:, 0:64]
        wide[half:, 64 * h : 64 * h + 64] = part[:, 64:128]
    joined[...] = wide[...].astype(BF16)
    for m in range(4):
        weight = part_of((w0, w1, w2, w3, w4), m, PROJ)
        split_rows(dot(joined[...], weight, NT), keep, send, lanes(m))


def pair_kernel(ids, keep, got, part, send):
    total = keep[...] + got[...].astype(F32)
    part[...] = total
    send[...] = total.astype(BF16)


def half_kernel(ids, keep, got, part, send):
    own = part.shape[0]
    total = keep[...] + got[...].astype(F32)
    low = is_zero(z_low(ids))
    part[...] = pick(low, total[:own], total[own:])
    send[...] = pick(low, total[own:], total[:own]).astype(BF16)


def half_grad_kernel(ids, keep, got, rows, sums_two, sums_fc1, sums_qv, part, send, small):
    own = part.shape[0]
    total = keep[...] + got[...].astype(F32)
    low = is_zero(z_low(ids))
    part[...] = pick(low, total[:own], total[own:])
    scaled, _ = norm_parts(rows[...].astype(F32))
    send[0:own, :] = pick(low, total[own:], total[:own]).astype(BF16)
    sums = jnp.concatenate(
        [
            jnp.sum(total * scaled, axis=0, keepdims=True),
            sums_two[0:1, :],
            jnp.sum(total, axis=0, keepdims=True),
            sums_two[1:4, :],
            sums_qv[...],
            sums_fc1[...],
        ],
        axis=0,
    )
    small[...] = sums
    send[SMALL : SMALL + 8, :] = sums.astype(BF16)


def norm_two_kernel(ids, rows, part, got, vec, residual, normed):
    total = rows[...].astype(F32) + (part[...] + got[...].astype(F32) + vec[4:5, :])
    residual[...] = total
    scaled, _ = norm_parts(total)
    normed[...] = (scaled * vec[1:2, :] + vec[3:4, :]).astype(BF16)


def mlp_start_kernel(
    ids, own, got, own_grad, got_grad, b_fc1, f0, f1, f2, g0, g1, g2, whole, whole_grad, pre, back, wide
):
    join_rows(wide, own, got)
    whole[...] = wide[...].astype(BF16)
    join_rows(wide, own_grad, got_grad)
    whole_grad[...] = wide[...].astype(BF16)

    def body(c, carry):
        cols = pl.ds(pl.multiple_of(c * 256, 256), 256)
        total = b_fc1[:, cols] + dot(whole[:, lanes(0)], f0[:, cols], NN)
        grad = dot(whole_grad[:, lanes(0)], g0[:, cols], NN)
        for m, (f, g) in ((1, (f1, g1)), (2, (f2, g2))):
            total = total + dot(whole[:, lanes(m)], f[:, cols], NN)
            grad = grad + dot(whole_grad[:, lanes(m)], g[:, cols], NN)
        pre[:, cols] = total
        back[:, cols] = grad
        return carry

    lax.fori_loop(0, 4, body, 0)


def fc_kernel(
    ids, whole, whole_grad, start, back, w0, w1, w2, w3, g3, hidden, grad_pre, sums, keep, send, wide
):
    weights = (w0, w1, w2, w3)
    wide[...] = jnp.zeros_like(wide)

    def body(c, carry):
        cols = pl.ds(pl.multiple_of(c * 256, 256), 256)
        pre = start[:, cols] + dot(whole[:, lanes(3)], w3[:, cols], NN)
        grad_hidden = back[:, cols] + dot(whole_grad[:, lanes(3)], g3[:, cols], NN)
        half_erf = 0.5 * (1.0 + lax.erf(pre * root_half))
        hidden[:, cols] = (pre * half_erf).astype(BF16)
        slope = half_erf + pre * jnp.exp(-0.5 * pre * pre) * inv_root_tau
        grad = (grad_hidden * slope).astype(BF16)
        grad_pre[:, cols] = grad
        sums[:, cols] = jnp.sum(grad.astype(F32), axis=0, keepdims=True)
        for m in range(4):
            wide[:, lanes(m)] += dot(grad, weights[m][:, cols], NT)
        return carry

    lax.fori_loop(0, 4, body, 0)
    for m in range(4):
        split_rows(wide[:, lanes(m)], keep, send, lanes(m))


def norm_back(total, scaled, inverse, gain):
    hat = total * gain
    return (
        hat
        - jnp.mean(hat, axis=1, keepdims=True)
        - scaled * jnp.mean(hat * scaled, axis=1, keepdims=True)
    ) * inverse


def norm_two_back_kernel(ids, residual, part, got, grads, vec, grad_residual, grad_branch, sums):
    scaled, inverse = norm_parts(residual[...])
    total = part[...] + got[...].astype(F32)
    upstream = grads[...].astype(F32)
    result = upstream + norm_back(total, scaled, inverse, vec[1:2, :])
    branch = result.astype(BF16)
    grad_residual[...] = result
    grad_branch[...] = branch
    own = total.shape[0] // 2
    row = row_ids(total.shape)
    low = jnp.full(total.shape, z_low(ids), jnp.int32)
    mine = jnp.where(row < own, 1 - low, low) != 0

    def column_sum(value):
        return jnp.sum(jnp.where(mine, value, 0.0), axis=0, keepdims=True)

    sums[0:1, :] = column_sum(total * scaled)
    sums[1:2, :] = column_sum(total)
    sums[2:3, :] = column_sum(branch.astype(F32))
    sums[3:4, :] = column_sum(upstream)
    sums[4:8, :] = jnp.zeros((4, sums.shape[1]), F32)


def grad_att_kernel(ids, own, got, w0, w1, w2, w3, w4, whole, o0, o1, o2, o3, wide, heads):
    join_rows(wide, own, got)
    whole[...] = wide[...].astype(BF16)
    weights = (w0, w1, w2, w3, w4)
    total = dot(whole[:, lanes(0)], w0[:, lanes(PROJ)], NN)
    for m in range(1, 4):
        total = total + dot(whole[:, lanes(m)], part_of(weights, m, PROJ), NN)
    for h in range(4):
        heads[h, :, :] = fold_rows(total[:, 64 * h : 64 * h + 64]).astype(BF16)
    for m, out in enumerate((o0, o1, o2, o3)):
        out[...] = heads[ids[CHIP_ID] ^ m, :, :]


def qkv_back_kernel(ids, g0, g1, g2, g3, w0, w1, w2, w3, w4, joined, keep, send, sums, heads, wide):
    for m, part in enumerate((g0, g1, g2, g3)):
        heads[m, :, :] = part[...]
    half, tokens = keep.shape[0], joined.shape[0]
    for h in range(4):
        part = heads[h ^ ids[CHIP_ID], :, :]
        for j in range(2):
            joined[:, 256 * j + 64 * h : 256 * j + 64 * h + 64] = part[
                0:tokens, 64 * j : 64 * j + 64
            ]
        values = part[VALUES:, :].astype(F32)
        wide[0:half, 64 * h : 64 * h + 64] = values[:, 0:64]
        wide[half:, 64 * h : 64 * h + 64] = values[:, 64:128]
        for k, value in ((h, part[0:tokens, 0:64]), (4 + h, wide[:, 64 * h : 64 * h + 64])):
            total = jnp.sum(value.astype(F32), axis=0, keepdims=True)
            sums[0:1, 128 * k : 128 * k + 128] = jnp.concatenate(
                [total, jnp.zeros((1, 64), F32)], axis=1
            )
    joined[:, 512:768] = wide[...].astype(BF16)
    for m in range(4):
        weights = (w0, w1, w2, w3, w4)
        total = dot(joined[:, lanes(0)], part_of(weights, m, 0), NT)
        for j in (1, 2):
            total = total + dot(joined[:, lanes(j)], part_of(weights, m, j), NT)
        split_rows(total, keep, send, lanes(m))


def to_owners(ids, value, wide, here, there):
    wide[0 : 2 * SHARE, :] = value
    wide[2 * SHARE :, :] = jnp.zeros((wide.shape[0] - 2 * SHARE, wide.shape[1]), F32)
    for m in range(4):
        cols = chip_lanes(ids, m)
        here[0:PAD, cols] = wide[0:PAD, lanes(m)].astype(BF16)
        there[0:PAD, cols] = wide[SHARE : SHARE + PAD, lanes(m)].astype(BF16)


def own_half(ids, ref):
    own = ref.shape[0] // 2
    value = ref[...].astype(F32)
    return pick(is_zero(z_low(ids)), value[:own], value[own:])


def norm_one_back_kernel(
    ids, rows, part, got, grad_residual, vec, small, here, there, wide
):
    scaled, inverse = norm_parts(own_half(ids, rows))
    total = part[...] + got[0 : 2 * SHARE, :].astype(F32)
    result = own_half(ids, grad_residual) + norm_back(total, scaled, inverse, vec[0:1, :])
    to_owners(ids, result, wide, here, there)
    far = jnp.where(row_ids((8, 1024)) < 6, got[SMALL : SMALL + 8, :].astype(F32), 0.0)
    sums = (small[...] + far).astype(BF16)
    here[PAD : PAD + 8, :] = sums
    there[PAD : PAD + 8, :] = sums


def layer_out_kernel(ids, residual, part, got, vec, here, there, wide):
    result = own_half(ids, residual) + (part[...] + got[...].astype(F32) + vec[5:6, :])
    to_owners(ids, result, wide, here, there)


def fc2_kernel(ids, hidden, w0, w1, w2, w3, keep, send):
    for m, weight in enumerate((w0, w1, w2, w3)):
        split_rows(dot(hidden[...], weight[...], NT), keep, send, lanes(m))


def for_slot(slots, d, left, right):
    value = jnp.where(slots[8 + d, 0:1, 0:1] > 0.5, right, 0.0)
    return jnp.where(slots[d, 0:1, 0:1] > 0.5, left, value)


def give_out_kernel(ids, slots, here, away, keep, send):
    left = here[...].astype(F32)
    right = away[...].astype(F32)
    for out, flip in ((keep, 0), (send, 1)):
        for m, d in enumerate(far_chips(ids, flip)):
            out[m, :, :] = for_slot(slots, d, left, right).astype(BF16)


def give_kernel(ids, slots, here, away, keep, send, rel, flat, tail):
    left = here[0:PAD, :].astype(F32)
    right = away[0:PAD, :].astype(F32)
    own = here[PAD : PAD + 8, :].astype(F32)
    far = away[PAD : PAD + 8, :].astype(F32)
    rel[...] = own + far
    home = pick(is_zero(ids[CORE_ID]), own, far)
    for m in range(4):
        flat[:, chip_lanes(ids, m)] = rel[:, lanes(m)]
    rel[0:1, :] = home[7:8]
    tail[...] = jnp.zeros_like(tail)
    for k in range(8):
        row, lane = (SHARE + k, 128) if k < 7 else (SHARE, 256)
        tail[row : row + 1, lane : lane + 128] = home[6:7, 128 * k : 128 * k + 128]
    row = row_ids((PAD, 1024))
    for out, flip in ((keep, 0), (send, 1)):
        for m, d in enumerate(far_chips(ids, flip)):
            cols = pl.ds(pl.multiple_of(d * 128, 128), 128)
            tail[SHARE : SHARE + 6, 0:128] = flat[0:6, cols]
            tail[SHARE + 6 : PAD, 0:128] = rel[0:1, cols]
            value = for_slot(slots, d, left, right)
            out[m, :, :] = jnp.where(row < SHARE, value, tail[...]).astype(BF16)


def settle_rows(parts, stage, out):
    for a, ref, k in parts:
        stage[a, :, :] = ref[k, :, :].astype(F32)
    for j in range(8):
        out[SHARE * j : SHARE * j + SHARE, :] = stage[j, 0:SHARE, :]


def take_out_kernel(ids, keep, got, d1, d2, d3, out, stage, wide):
    settle_rows(arrived(ids, keep, got, d1, d2, d3), stage, wide)
    out[...] = wide[...].astype(BF16)


def take_kernel(ids, keep, got, d1, d2, d3, out, gains, biases, last, qv, b_fc1, stage):
    parts = arrived(ids, keep, got, d1, d2, d3)
    settle_rows(parts, stage, out)
    total = jnp.zeros((8, 384), F32)
    for _, ref, k in parts:
        total = total + ref[k, PAD - 8 : PAD, 0:384].astype(F32)
    rows = pltpu.roll(total[:, 0:128], (128 - 32 * ids[T_ID]) & 127, 1)
    gains[...] = rows[1:3, 0:32]
    biases[...] = rows[3:7, 0:32]
    last[...] = rows[6:7, 0:32]
    b_fc1[...] = total[7:8, 0:128]
    pieces = jnp.concatenate([total[1:8, 128:256], total[1:2, 256:384]], axis=0)
    qv[...] = pltpu.roll(pieces, (128 - 8 * ids[D_ID]) & 127, 1)[:, 0:8]


def shards_kernel(ids, qkv, proj, fc2, first, second):
    for j in range(3):
        first[:, lanes(j)] = qkv[j, :, :]
    first[:, lanes(PROJ)] = jnp.transpose(proj[...])
    second[...] = jnp.transpose(fc2[...])


def offer_kernel(ids, own, far, send):
    @pl.when(ids[CORE_ID] == 0)
    def _():
        send[...] = far[...]

    @pl.when(ids[CORE_ID] != 0)
    def _():
        send[...] = own[...]


def merge_kernel(ids, own, far, got, out):
    half = own.shape[0]

    @pl.when(ids[CORE_ID] == 0)
    def _():
        out[0:half, :] = own[...]
        out[half:, :] = got[...]

    @pl.when(ids[CORE_ID] != 0)
    def _():
        out[0:half, :] = got[...]
        out[half:, :] = far[...]


X_FIRST, Y_FIRST = (1, 2), (2, 1)


def blocks_of(order, left, right, cols, send, here, there, out_cols):
    near, far = order
    for slot, m in ((0, near), (1, 3)):
        send[slot, :, out_cols] = dot(left[:, lanes(m)], right[:, cols], TN).astype(BF16)
    here[:, out_cols] = dot(left[:, lanes(0)], right[:, cols], TN)
    there[:, out_cols] = dot(left[:, lanes(far)], right[:, cols], TN)


def grads_fc1_kernel(ids, left, right, send, here, there):
    for c in range(2):
        cols = slice(512 * c, 512 * c + 512)
        blocks_of(X_FIRST, left, right, cols, send, here, there, cols)


def grads_fc2_kernel(ids, left, right, send, here, there):
    for c in range(2):
        cols = slice(512 * c, 512 * c + 512)
        blocks_of(Y_FIRST, left, right, cols, send, here, there, cols)


def grads_att_kernel(
    ids, rows, joined, branch, mixed, send_x, here_x, there_x, send_y, here_y, there_y
):
    blocks_of(X_FIRST, rows, joined, slice(0, 512), send_x, here_x, there_x, slice(0, 512))
    blocks_of(Y_FIRST, rows, joined, slice(512, 768), send_y, here_y, there_y, slice(0, 256))
    blocks_of(Y_FIRST, branch, mixed, slice(0, 256), send_y, here_y, there_y, slice(256, 512))


def fold_kernel(ids, here, there, got, other, whole):
    other[...] = (there[...] + got[1, :, :].astype(F32)).astype(BF16)
    whole[...] = here[...] + got[0, :, :].astype(F32)


def gather_kernel(ids, whole_x, got_x, whole_y, got_y, keep, send):
    n = whole_x.shape[1]
    for core in range(2):

        @pl.when(ids[CORE_ID] == core)
        def _():
            own = slice(128 * core, 128 * core + 128)
            other = slice(128 - 128 * core, 256 - 128 * core)
            for cols, whole, got in (
                (slice(0, n), whole_x, got_x),
                (slice(n, 2 * n), whole_y, got_y),
            ):
                for out, rows in ((keep, own), (send, other)):
                    total = whole[rows, :] + got[rows, :].astype(F32)
                    out[:, cols] = total.astype(BF16)


def away_kernel(ids, keep, got, out):
    @pl.when(ids[CORE_ID] == 0)
    def _():
        out[...] = got[...]

    @pl.when(ids[CORE_ID] != 0)
    def _():
        out[...] = keep[...]


def whole_sum(ids, keep, got, moved, cols):
    core = is_zero(ids[CORE_ID])
    own = pick(core, keep[:, cols].astype(F32), got[:, cols].astype(F32))
    return own + moved[:, cols].astype(F32)


def finish_mlp_kernel(ids, keep, got, moved, fc1, fc2):
    fc1[...] = whole_sum(ids, keep, got, moved, slice(0, 1024))
    fc2[...] = jnp.transpose(whole_sum(ids, keep, got, moved, slice(1024, 2048)))


def finish_att_kernel(ids, keep, got, moved, qkv, proj):
    for j in range(3):
        qkv[j, :, :] = whole_sum(ids, keep, got, moved, lanes(j))
    proj[...] = jnp.transpose(whole_sum(ids, keep, got, moved, lanes(PROJ)))


def tie(*values):
    return lax.optimization_barrier(values)


def sum_second(ids, first, second):
    n = first[1].shape[1]
    outs = [((256, n), BF16), ((256, n), F32)]
    other_x, whole_x = call(fold_kernel, outs, ids, *first)
    other_y, whole_y = call(fold_kernel, outs, ids, *second)
    return whole_x, other_x, whole_y, other_y


def send_second(whole_x, other_x, whole_y, other_y):
    return whole_x, swap(other_x, Y), whole_y, swap(other_y, X)


def sum_third(ids, parts):
    n = 2 * parts[0].shape[1]
    keep, send = call(gather_kernel, [((128, n), BF16)] * 2, ids, *parts)
    got = swap(send, CORE)
    (away,) = call(away_kernel, [((128, n), BF16)], ids, keep, got)
    return keep, got, away


def on_device_spread(
    clip_rows,
    out_grad,
    clip_valid,
    gain_rows,
    bias_rows,
    qkv_weight,
    qv_bias,
    proj_weight,
    fc1_weight,
    fc1_bias,
    fc2_weight,
):
    d, t = lax.axis_index("dp"), lax.axis_index("tensor")
    core = d & 1
    ids = jnp.stack([d >> 1, core, d, t, clip_valid[0]]).astype(jnp.int32)
    count = clip_rows.shape[0]
    half, own = count // 2, count // 4
    behind = (PAD + 8, 1024)
    plain = (PAD, 1024)
    packed = (VALUES + half, 128)
    wide = ((count, 1024), F32)

    def to_chips(keep, send):
        got = swap(send, CORE)
        shape = (2, *keep.shape[1:])
        return got, *call(pair_up_kernel, [(shape, BF16)] * 3, ids, keep, got)

    def over_chips(pairs):
        return [swap(pairs[m], CHIP_MASKS[m + 1]) for m in range(3)]

    def offer(shard, far):
        (send,) = call(offer_kernel, [(shard.shape, BF16)], ids, shard, far)
        return send

    def merge(shard, far, send):
        (out,) = call(
            merge_kernel, [((256, shard.shape[1]), BF16)], ids, shard, far, swap(send, CORE)
        )
        return out

    def trade(parts):
        return [parts[0]] + [swap(parts[m], CHIP_MASKS[m]) for m in range(1, 4)]

    params = jnp.concatenate(
        [
            jnp.pad(v, ((0, n - v.shape[0]), (0, 128 - v.shape[1])))
            for v, n in (
                (jnp.concatenate([gain_rows, bias_rows]), 8),
                (qv_bias.reshape(8, 8), 8),
                (fc1_bias, 8),
            )
        ]
    )
    shard_a, shard_g = call(
        shards_kernel,
        [((128, 1024), BF16), ((128, 1024), BF16)],
        ids,
        qkv_weight,
        proj_weight,
        fc2_weight,
    )
    far_a = swap(shard_a, Z_HIGH)
    own_rows = clip_rows
    keep, send = call(
        pack_kernel,
        [((4, 2 * PAD, 1024), BF16)] * 2,
        ids,
        own_rows,
        out_grad,
        params,
        scratch=[((400, 1024), F32), ((8, 2 * PAD, 1024), BF16)],
    )
    w0 = merge(shard_a, far_a, offer(shard_a, far_a))
    shard_f, _ = tie(fc1_weight, far_a)
    far_f = swap(shard_f, Z_HIGH)
    got, *pairs = to_chips(keep, send)
    *parts, w0 = tie(keep, got, *over_chips(pairs), w0)
    here, there, here_grad, there_grad, slots = call(
        pick_kernel,
        [(behind, BF16), (behind, BF16), (plain, BF16), (plain, BF16), ((16, 8, 128), F32)],
        ids,
        *parts,
    )
    r1, r2, r3 = swap(here, Z_LOW), swap(there, Z_HIGH), swap(there, Z_LOW | Z_HIGH)
    w1, w2 = swap(w0, X), swap(w0, Y)
    w_att = (w0, w1, w2, swap(w2[:, :512], X), swap(w1[:, 512:], Y))
    r1, r2, r3, far_f, shard_f = tie(r1, r2, r3, far_f, shard_f)
    f0 = merge(shard_f, far_f, offer(shard_f, far_f))
    rows, normed, vec, qkv_bias, b_fc1 = call(
        norm_one_kernel,
        [
            ((half, 1024), BF16),
            ((half, 1024), BF16),
            ((8, 1024), F32),
            ((8, 128), F32),
            ((1, 1024), F32),
        ],
        ids,
        here,
        r1,
        r2,
        r3,
        scratch=[((half, 1024), F32), ((8, 1024), F32)],
    )

    whole_one, start = call(
        qkv_start_kernel,
        [((count, 1024), BF16), ((count, 768), F32)],
        ids,
        normed,
        swap(normed, CORE),
        *w_att[:3],
        scratch=[wide],
    )
    qkv = call(
        qkv_kernel,
        [(packed, BF16)] * 4,
        ids,
        whole_one,
        start,
        qkv_bias,
        *w_att[3:],
        scratch=[((4, *packed), BF16)],
    )

    shard_g, *qkv = tie(shard_g, *qkv)
    far_g = swap(shard_g, Z_HIGH)
    *qkv, f0, here_grad, there_grad = tie(*trade(qkv), f0, here_grad, there_grad)
    f1, f2 = swap(f0, X), swap(f0, Y)
    s1, s2 = swap(here_grad, Z_LOW), swap(there_grad, Z_HIGH)
    tokens = 4 * count
    *mixed, back = call(
        attention_kernel,
        [((half, 128), BF16)] * 4 + [((tokens, 128), F32)],
        ids,
        *qkv,
        scratch=[((tokens, 192), F32)] + [((tokens, 64), BF16)] * 2 + [((tokens, 128), BF16)],
    )
    shard_g, far_g, *mixed = tie(shard_g, far_g, *mixed)
    g0 = merge(shard_g, far_g, offer(shard_g, far_g))
    *mixed, f1, f2, s1, s2 = tie(*trade(mixed), f1, f2, s1, s2)
    g1, g2 = swap(g0, X), swap(g0, Y)
    f3, g3, s3 = swap(f2, X), swap(g1, Y), swap(s2, Z_LOW)
    attended, keep, send = call(
        proj_kernel,
        [((count, 256), BF16), ((half, 1024), F32), ((half, 1024), BF16)],
        ids,
        *mixed,
        *w_att,
        scratch=[((4, half, 128), BF16), ((count, 256), F32)],
    )

    def pair(keep, send):
        return call(
            pair_kernel, [((half, 1024), F32), ((half, 1024), BF16)], ids, keep, swap(send, CORE)
        )

    def halve(keep, send):
        return call(
            half_kernel, [((own, 1024), F32), ((own, 1024), BF16)], ids, keep, swap(send, CORE)
        )

    part, send = pair(keep, send)
    away, s3 = tie(swap(send, Z_LOW), s3)
    w_fc1, w_fc2 = (f0, f1, f2, f3), (g0, g1, g2, g3)
    (grads,) = call(
        lay_grad_kernel,
        [((half, 1024), BF16)],
        ids,
        here_grad,
        s1,
        s2,
        s3,
        scratch=[((half, 1024), F32)],
    )
    residual, normed_two = call(
        norm_two_kernel,
        [((half, 1024), F32), ((half, 1024), BF16)],
        ids,
        rows,
        part,
        away,
        vec,
    )
    whole_two, whole_mlp, start, grad_hidden = call(
        mlp_start_kernel,
        [((count, 1024), BF16)] * 2 + [((count, 1024), F32)] * 2,
        ids,
        normed_two,
        swap(normed_two, CORE),
        grads,
        swap(grads, CORE),
        b_fc1,
        *w_fc1[:3],
        *w_fc2[:3],
        scratch=[wide],
    )

    hidden, grad_pre, sums_fc1, keep, send = call(
        fc_kernel,
        [((count, 1024), BF16)] * 2
        + [((1, 1024), F32), ((half, 1024), F32), ((half, 1024), BF16)],
        ids,
        whole_two,
        whole_mlp,
        start,
        grad_hidden,
        *w_fc1,
        w_fc2[3],
        scratch=[wide],
    )
    part, send = pair(keep, send)
    late = tie(send, whole_mlp, hidden, whole_two, grad_pre)
    grad_outs = [((2, 256, 1024), BF16), ((256, 1024), F32), ((256, 1024), F32)]
    cost = 2 * count * 1024 * 1024
    send_f, *rest_f = call(grads_fc1_kernel, grad_outs, ids, late[3], late[4])
    send_g, *rest_g = call(grads_fc2_kernel, grad_outs, ids, late[1], late[2])
    sums_f = (*rest_f, swap(send_f, X))
    sums_g = (*rest_g, swap(send_g, Y))
    keep_out, send_out = call(
        fc2_kernel,
        [((half, 1024), F32), ((half, 1024), BF16)],
        ids,
        late[2],
        *w_fc2,
    )
    away, keep_out, send_out = tie(swap(send, Z_LOW), keep_out, send_out)
    part_out, send_out = halve(keep_out, send_out)
    away_out = swap(send_out, Z_LOW)
    grad_residual, grad_branch, sums_two = call(
        norm_two_back_kernel,
        [((half, 1024), F32), ((half, 1024), BF16), ((8, 1024), F32)],
        ids,
        residual,
        part,
        away,
        grads,
        vec,
    )

    whole_branch, *grad_att = call(
        grad_att_kernel,
        [((count, 1024), BF16)] + [((half, 128), BF16)] * 4,
        ids,
        grad_branch,
        swap(grad_branch, CORE),
        *w_att,
        scratch=[wide, ((4, half, 128), BF16)],
    )
    *grad_att, part_out, away_out = tie(*grad_att, part_out, away_out)
    here_out, there_out = call(
        layer_out_kernel,
        [(plain, BF16)] * 2,
        ids,
        residual,
        part_out,
        away_out,
        vec,
        scratch=[((2 * PAD, 1024), F32)],
    )
    sums_mlp = sum_second(ids, sums_f, sums_g)
    *grad_att, whole_x, other_x, whole_y, other_y, here_out, there_out = tie(
        *trade(grad_att), *sums_mlp, here_out, there_out
    )
    sums_mlp = send_second(whole_x, other_x, whole_y, other_y)
    away_out = swap(there_out, Z_HIGH)
    grad_qkv = call(
        attention_back_kernel,
        [(packed, BF16)] * 4,
        ids,
        *qkv,
        *grad_att,
        back,
        scratch=[((tokens, 192), F32)] + [((tokens, 128), BF16)] * 4 + [((tokens, 64), F32)] * 2,
    )
    *grad_qkv, away_out, whole_x, got_x, whole_y, got_y = tie(*grad_qkv, away_out, *sums_mlp)
    *sums_mlp, moved_mlp = sum_third(ids, (whole_x, got_x, whole_y, got_y))
    moved_mlp = swap(moved_mlp, Z_HIGH)
    keep_out, send_out = call(
        give_out_kernel, [((4, PAD, 1024), BF16)] * 2, ids, slots, here_out, away_out
    )
    got_out, *pairs_out = to_chips(keep_out, send_out)
    *grad_qkv, got_out, p1, p2, p3 = tie(*trade(grad_qkv), got_out, *pairs_out)
    parts_out = over_chips((p1, p2, p3))
    joined, keep, send, sums_qv = call(
        qkv_back_kernel,
        [((count, 768), BF16), ((half, 1024), F32), ((half, 1024), BF16), ((1, 1024), F32)],
        ids,
        *grad_qkv,
        *w_att,
        scratch=[((4, *packed), BF16), ((count, 256), F32)],
    )
    part, send, small = call(
        half_grad_kernel,
        [((own, 1024), F32), ((SMALL + 8, 1024), BF16), ((8, 1024), F32)],
        ids,
        keep,
        swap(send, CORE),
        rows,
        sums_two,
        sums_fc1,
        sums_qv,
    )
    late = tie(send, whole_one, joined, whole_branch, attended)
    grad_outs = [((2, 256, 512), BF16), ((256, 512), F32), ((256, 512), F32)]
    send_x, here_x, there_x, send_y, here_y, there_y = call(
        grads_att_kernel, grad_outs * 2, ids, *late[1:]
    )
    away, send_x, send_y, *parts_out = tie(swap(send, Z_LOW), send_x, send_y, *parts_out)
    parts_out = keep_out, got_out, *parts_out
    got_x, got_y = swap(send_x, X), swap(send_y, Y)
    here, there = call(
        norm_one_back_kernel,
        [(behind, BF16)] * 2,
        ids,
        rows,
        part,
        away,
        grad_residual,
        vec,
        small,
        scratch=[((2 * PAD, 1024), F32)],
    )
    away, got_x, got_y, moved_mlp = tie(swap(there, Z_HIGH), got_x, got_y, moved_mlp)
    sums_att = sum_second(ids, (here_x, there_x, got_x), (here_y, there_y, got_y))
    keep, send = call(
        give_kernel,
        [((4, PAD, 1024), BF16)] * 2,
        ids,
        slots,
        here,
        away,
        scratch=[((8, 1024), F32), ((8, 1024), F32), (plain, F32)],
    )
    got, *pairs = to_chips(keep, send)
    whole_x, other_x, whole_y, other_y = sums_att
    parts = keep, got, *over_chips(pairs)
    *sums_att, moved_att = sum_third(ids, send_second(whole_x, other_x, whole_y, other_y))
    moved_att = swap(moved_att, Z_HIGH)
    input_grad, grad_gains, grad_biases, grad_last, grad_qv, grad_b_fc1 = call(
        take_kernel,
        [
            ((count, 1024), F32),
            ((2, 32), F32),
            ((4, 32), F32),
            ((1, 32), F32),
            ((8, 8), F32),
            ((1, 128), F32),
        ],
        ids,
        *parts,
        scratch=[((8, PAD, 1024), F32)],
    )
    (layer_out,) = call(
        take_out_kernel,
        [((count, 1024), BF16)],
        ids,
        *parts_out,
        scratch=[((8, PAD, 1024), F32), wide],
    )
    grad_fc1, grad_fc2 = call(
        finish_mlp_kernel,
        [((128, 1024), F32), ((1024, 128), F32)],
        ids,
        *sums_mlp,
        moved_mlp,
    )
    moved_att, _ = tie(moved_att, input_grad)
    grad_w, grad_proj = call(
        finish_att_kernel,
        [((3, 128, 256), F32), ((256, 128), F32)],
        ids,
        *sums_att,
        moved_att,
    )
    return (
        layer_out,
        input_grad,
        grad_gains,
        grad_biases,
        grad_w,
        grad_qv.reshape(2, 4, 8),
        grad_proj,
        grad_fc1,
        grad_b_fc1,
        grad_fc2,
        grad_last[0],
    )


def solution(mesh):
    spread = (mesh.shape["dp"], mesh.shape["tensor"]) == (8, 4)
    in_specs = (
        P(("dp", "tensor"), None),
        P(("dp", "tensor"), None),
        P("dp"),
        P(None, ("dp", "tensor")),
        P(None, ("dp", "tensor")),
        P(None, "dp", "tensor"),
        P(None, "tensor", "dp"),
        P("tensor", "dp"),
        P("dp", "tensor"),
        P("tensor", "dp"),
        P("tensor", "dp"),
    )
    out_specs = (
        P(("dp", "tensor"), None),
        P(("dp", "tensor"), None),
        P(None, ("dp", "tensor")),
        P(None, ("dp", "tensor")),
        P(None, "dp", "tensor"),
        P(None, "tensor", "dp"),
        P("tensor", "dp"),
        P("dp", "tensor"),
        P("tensor", "dp"),
        P("tensor", "dp"),
        P(("dp", "tensor")),
    )
    return jax.shard_map(
        on_device_spread if spread else on_device, mesh=mesh, in_specs=in_specs, out_specs=out_specs, check_vma=False
    )
```
